256 devices in a mesh: slide: 4 (over y), rrow: 8 (over x, core), rcol: 8 (over z).
Axes of the slice: x: 4, y: 4, z: 8, core: 2. Of those that a mesh axis runs over, the one named last changes fastest.
Arguments:
- queries: bfloat16 [256, 256, 1024], P(('slide', 'rrow'), 'rcol'), parts along dimension 0, may hold values from -6 to 6
- key_grid: bfloat16 [256, 256, 1024], P(('slide', 'rrow'), 'rcol'), parts along dimension 0, may hold values from -6 to 6
- value_grid: bfloat16 [256, 256, 1024], P(('slide', 'rrow'), 'rcol'), parts along dimension 0, may hold values from -6 to 6
- out_grad: bfloat16 [256, 256, 1024], P(('slide', 'rrow'), 'rcol'), parts along dimension 0, may hold values from -16 to 16
- tissue_mask: int32 [256, 16], P(('slide', 'rrow')), parts along dimension 0, may hold values 0 or 1
- band_offset: int32 [256], P(('slide', 'rrow')), parts along dimension 0, may hold values from -16 to 16, as said below
Outputs:
- query_grad: bfloat16 [256, 256, 1024], P(('slide', 'rrow'), 'rcol'), parts along dimension 0
- key_grad: bfloat16 [256, 256, 1024], P(('slide', 'rrow'), 'rcol'), parts along dimension 0
- value_grad: bfloat16 [256, 256, 1024], P(('slide', 'rrow'), 'rcol'), parts along dimension 0
The draws below stay inside these ranges and needn't reach their ends.
There are 4 independent parts, one for each index of `slide`. The reference program is written for one: setup_inputs(seed, part) draws one part's arguments, and reference() takes and returns one part's arrays. A program takes and returns all parts, laid end to end along the dimension named above; each array names one. Nothing has to cross between parts.
Inputs may be any that keep to these rules, and one draw needn't show every extreme that they name: `band_offset`: some grid row takes each end of the range.
All inputs are finite; a program needn't handle non-finite values. No bound on the sum of `tissue_mask` on one device may be relied on, other than what follows from the above.
Results may differ from the reference program's by a relative error of at most 0.0065.
Values may be sent and summed in bfloat16 or wider, within the bound.
A program may use at most 128 MiB of HBM per device.

```python
import math
import jax
import jax.numpy as jnp
from jax import lax

D = 1024
HD = 64
CC = 32
BLK = 16
HALF = 32
OFFMAX = 16
NR = 64
NC = 256
NCB = 16


def draw_queries(key, part):
    own_key = jax.random.fold_in(key, 1)
    values = jnp.clip(jax.random.normal(own_key, (NR, NC, D), jnp.float32), -4.5, 4.5)
    return values.astype(jnp.bfloat16)


def draw_key_grid(key, part):
    own_key = jax.random.fold_in(key, 2)
    values = jnp.clip(jax.random.normal(own_key, (NR, NC, D), jnp.float32), -4.5, 4.5)
    return values.astype(jnp.bfloat16)


def draw_band_offset(key, part):
    own_key = jax.random.fold_in(key, 3)
    key_vals, key_order = jax.random.split(own_key)
    values = jax.random.randint(key_vals, (NR,), -OFFMAX, OFFMAX + 1)
    row_order = jax.random.permutation(key_order, NR)
    values = values.at[row_order[0]].set(-OFFMAX).at[row_order[1]].set(OFFMAX)
    return values.astype(jnp.int32)


def with_ends(drawn, stream_key, least, largest):
    longest = drawn.shape.index(max(drawn.shape))
    spots = []
    for shift in (0, 1):
        where = [jax.random.randint(jax.random.fold_in(stream_key, axis), (), 0, length) for axis, length in enumerate(drawn.shape)]
        where[longest] = (where[longest] + shift) % drawn.shape[longest]
        spots.append(tuple(where))
    return drawn.at[spots[0]].set(least).at[spots[1]].set(largest)


def steps_of(key, extent, cuts, smallest, high):
    loudness = 1.0
    for dim, shards_of in cuts:
        heights = jax.random.uniform(jax.random.fold_in(jax.random.fold_in(key, 6), dim), (shards_of,), jnp.float32, smallest / len(cuts), high / len(cuts))
        loudness = loudness * jnp.repeat(jnp.exp(heights), extent[dim] // shards_of).reshape((-1,) + (1,) * (len(extent) - 1 - dim))
    return loudness


def scatter_about(stream_key, extent, deviation, bound, cuts=(), kind=jnp.bfloat16):
    values = jax.random.normal(stream_key, extent, jnp.float32) * deviation
    if len(cuts) > 0:
        values = steps_of(stream_key, extent, cuts, -0.22, 0.18) * values
    return jnp.clip(values, min=-bound, max=bound).astype(kind)


def setup_inputs(seed: int = 0, part: int = 0) -> dict:
    streams_of = jax.random.split(jax.random.key(seed), 7)
    own_keys = jax.random.split(jax.random.fold_in(streams_of[6], part), 7)
    return {
        "queries": draw_queries(jax.random.fold_in(jax.random.fold_in(streams_of[6], part), 71), part),
        "key_grid": draw_key_grid(jax.random.fold_in(jax.random.fold_in(streams_of[6], part), 71), part),
        "value_grid": scatter_about(own_keys[2], (NR, NC, D), 1.0, 6.0, ((0, 8), (1, 8))),
        "out_grad": scatter_about(own_keys[3], (NR, NC, D), 4.0, 16.0, ((0, 8), (1, 8))),
        "tissue_mask": with_ends((jax.random.randint(own_keys[4], (NR, NCB), 0, 5) < 3).astype(jnp.int32), jax.random.fold_in(own_keys[4], 1), 0, 1),
        "band_offset": draw_band_offset(jax.random.fold_in(jax.random.fold_in(streams_of[6], part), 71), part),
    }


def attention_grads(query_part, key_part, value_part, grad_part, allowed):
    score_scale = 1.0 / math.sqrt(HD)
    query_f = query_part.astype(jnp.float32)
    key_f = key_part.astype(jnp.float32)
    value_f = value_part.astype(jnp.float32)
    grad_f = grad_part.astype(jnp.float32)
    scores = jnp.einsum('...id,...jd->...ij', query_f, key_f) * score_scale
    if allowed is not None:
        scores = jnp.where(allowed, scores, -jnp.inf)
    row_max = lax.optimization_barrier(jnp.max(scores, axis=-1, keepdims=True))
    exp_scores = jnp.exp(scores - row_max)
    weights = exp_scores / lax.optimization_barrier(jnp.sum(exp_scores, axis=-1, keepdims=True))
    weights_low = weights.astype(jnp.bfloat16).astype(jnp.float32)
    outputs = jnp.einsum('...ij,...jd->...id', weights_low, value_f)
    delta = lax.optimization_barrier(jnp.sum(grad_f * outputs, axis=-1, keepdims=True))
    grad_weights = jnp.einsum('...id,...jd->...ij', grad_f, value_f)
    grad_scores = (weights * (grad_weights - delta)).astype(jnp.bfloat16).astype(jnp.float32)
    query_grad = jnp.einsum('...ij,...jd->...id', grad_scores, key_f) * score_scale
    key_grad = jnp.einsum('...ij,...id->...jd', grad_scores, query_f) * score_scale
    value_grad = jnp.einsum('...ij,...id->...jd', weights_low, grad_f)
    return (query_grad, key_grad, value_grad)

def band_allowed(mask_rows, offsets, first_col, grid_cols, block_cols):
    band_reach = HALF + OFFMAX
    query_cols = first_col + jnp.arange(block_cols, dtype=jnp.int32)
    key_cols = first_col - band_reach + jnp.arange(block_cols + 2 * band_reach, dtype=jnp.int32)
    inside = (key_cols >= 0) & (key_cols < grid_cols)
    key_block = jnp.clip(key_cols, 0, grid_cols - 1) // BLK
    block_ids = jnp.arange(mask_rows.shape[1], dtype=jnp.int32)
    key_open = lax.optimization_barrier(jnp.sum(mask_rows[:, None, :] * (key_block[None, :, None] == block_ids[None, None, :]).astype(jnp.int32), axis=-1))
    relative = key_cols[None, None, :] - query_cols[None, :, None] - offsets[:, None, None]
    same_block = key_cols[None, :] // BLK == query_cols[:, None] // BLK
    return (relative >= -HALF) & (relative < HALF) & inside[None, None, :] & ((key_open[:, None, :] > 0) | same_block[None])

def reference(queries, key_grid, value_grid, out_grad, tissue_mask, band_offset):
    band_reach = HALF + OFFMAX
    span_cols = CC + 2 * band_reach
    head_count = D // HD
    key_pad = jnp.pad(key_grid, ((0, 0), (band_reach, band_reach), (0, 0)))
    value_pad = jnp.pad(value_grid, ((0, 0), (band_reach, band_reach), (0, 0)))

    def heads_first(tensor):
        return tensor.reshape(tensor.shape[0], tensor.shape[1], head_count, HD).transpose(0, 2, 1, 3)

    def heads_last(tensor):
        return tensor.transpose(0, 2, 1, 3).reshape(tensor.shape[0], tensor.shape[2], D)

    def column_first(tensor):
        return tensor.reshape(NR, CC, head_count, HD).transpose(1, 2, 0, 3)

    def column_last(tensor):
        return tensor.transpose(2, 0, 1, 3).reshape(NR, CC, D)

    def rounded(tensor):
        return lax.optimization_barrier(tensor.astype(jnp.bfloat16)).astype(jnp.float32)

    def block_step(carry, block_index):
        key_acc, value_acc = carry
        first_col = (block_index * CC).astype(jnp.int32)

        def take_cols(tensor, count_cols):
            return lax.dynamic_slice_in_dim(tensor, first_col, count_cols, 1)
        query_block = take_cols(queries, CC)
        grad_block = take_cols(out_grad, CC)
        key_span = take_cols(key_pad, span_cols)
        value_span = take_cols(value_pad, span_cols)
        allowed = band_allowed(tissue_mask, band_offset, first_col, NC, CC)[:, None]
        row_q, row_k, row_v = attention_grads(heads_first(query_block), heads_first(key_span), heads_first(value_span), heads_first(grad_block), allowed)
        row_q = heads_last(row_q)
        row_k = heads_last(row_k)
        row_v = heads_last(row_v)

        def keep_inner(tensor):
            outer = rounded(tensor)
            return jnp.concatenate([outer[:, :band_reach], tensor[:, band_reach:band_reach + CC], outer[:, band_reach + CC:]], axis=1)
        key_acc = lax.dynamic_update_slice_in_dim(key_acc, take_cols(key_acc, span_cols) + keep_inner(row_k), first_col, 1)
        value_acc = lax.dynamic_update_slice_in_dim(value_acc, take_cols(value_acc, span_cols) + keep_inner(row_v), first_col, 1)
        col_q, col_k, col_v = attention_grads(column_first(query_block), column_first(take_cols(key_grid, CC)), column_first(take_cols(value_grid, CC)), column_first(grad_block), None)
        outputs = (row_q + rounded(column_last(col_q)), rounded(column_last(col_k)), rounded(column_last(col_v)))
        return ((key_acc, value_acc), outputs)
    zeros_acc = jnp.zeros((NR, NC + 2 * band_reach, D), jnp.float32)
    carried, stacked = lax.scan(block_step, (zeros_acc, zeros_acc), jnp.arange(NC // CC, dtype=jnp.int32))
    key_acc, value_acc = carried

    def join_blocks(blocks):
        return blocks.transpose(1, 0, 2, 3).reshape(NR, NC, D)
    query_grad = join_blocks(stacked[0]).astype(jnp.bfloat16)
    key_grad = (key_acc[:, band_reach:band_reach + NC] + join_blocks(stacked[1])).astype(jnp.bfloat16)
    value_grad = (value_acc[:, band_reach:band_reach + NC] + join_blocks(stacked[2])).astype(jnp.bfloat16)
    return (query_grad, key_grad, value_grad)
```

```python
import math

import jax
import jax.numpy as jnp
from jax import lax
from jax.sharding import PartitionSpec as P

HD = 64
BLK = 16
HALF = 32
OFFMAX = 16


def shortened(value):

    def short(part):
        return part.astype(jnp.bfloat16) if part.dtype == jnp.float32 else part

    return jax.tree.map(short, value)


def shifted(block, axis, distance):
    devices = range(lax.axis_size(axis))
    route = [(i - distance, i) for i in devices if i - distance in devices]
    return lax.ppermute(block, axis, route)


def attention_grads(query_part, key_part, value_part, grad_part, allowed):
    score_scale = 1.0 / math.sqrt(HD)
    scores = (
        jnp.einsum("...id,...jd->...ij", query_part, key_part, preferred_element_type=jnp.float32)
        * score_scale
    )
    if allowed is not None:
        scores = jnp.where(allowed, scores, -jnp.inf)
    row_max = jnp.max(scores, axis=-1, keepdims=True)
    exp_scores = jnp.exp(scores - row_max)
    weights = exp_scores / jnp.sum(exp_scores, axis=-1, keepdims=True)
    weights_low = weights.astype(jnp.bfloat16)
    outputs = jnp.einsum(
        "...ij,...jd->...id", weights_low, value_part, preferred_element_type=jnp.float32
    )
    delta = jnp.sum(grad_part.astype(jnp.float32) * outputs, axis=-1, keepdims=True)
    grad_weights = jnp.einsum(
        "...id,...jd->...ij", grad_part, value_part, preferred_element_type=jnp.float32
    )
    grad_scores = (weights * (grad_weights - delta)).astype(jnp.bfloat16)
    query_grad = (
        jnp.einsum("...ij,...jd->...id", grad_scores, key_part, preferred_element_type=jnp.float32)
        * score_scale
    )
    key_grad = (
        jnp.einsum(
            "...ij,...id->...jd", grad_scores, query_part, preferred_element_type=jnp.float32
        )
        * score_scale
    )
    value_grad = jnp.einsum(
        "...ij,...id->...jd", weights_low, grad_part, preferred_element_type=jnp.float32
    )
    return (query_grad, key_grad, value_grad)


def band_allowed(mask_rows, offsets, first_col, grid_cols, block_cols):
    band_reach = HALF + OFFMAX
    query_cols = first_col + jnp.arange(block_cols, dtype=jnp.int32)
    key_cols = first_col - band_reach + jnp.arange(block_cols + 2 * band_reach, dtype=jnp.int32)
    inside = (key_cols >= 0) & (key_cols < grid_cols)
    key_block = jnp.clip(key_cols, 0, grid_cols - 1) // BLK
    block_ids = jnp.arange(mask_rows.shape[1], dtype=jnp.int32)
    key_open = jnp.sum(
        mask_rows[:, None, :]
        * (key_block[None, :, None] == block_ids[None, None, :]).astype(jnp.int32),
        axis=-1,
    )
    relative = key_cols[None, None, :] - query_cols[None, :, None] - offsets[:, None, None]
    same_block = key_cols[None, :] // BLK == query_cols[:, None] // BLK
    return (
        (relative >= -HALF)
        & (relative < HALF)
        & inside[None, None, :]
        & ((key_open[:, None, :] > 0) | same_block[None])
    )


def row_branch(queries, key_grid, value_grid, out_grad, tissue_mask, band_offset):
    row_count, col_count, feature_width = queries.shape
    head_count = feature_width // HD
    band_reach = HALF + OFFMAX
    far_shards = -(-band_reach // col_count)
    cut_widths = [
        min(col_count, band_reach - (distance - 1) * col_count)
        for distance in range(1, far_shards + 1)
    ]
    pair = jnp.stack([key_grid, value_grid])
    left_parts = []
    right_parts = []
    for distance, cut_width in zip(range(1, far_shards + 1), cut_widths):
        left_parts.append(shifted(pair[:, :, col_count - cut_width :], "rcol", distance))
        right_parts.append(shifted(pair[:, :, :cut_width], "rcol", -distance))
    span = jnp.concatenate(left_parts[::-1] + [pair] + right_parts, axis=2)
    grid_cols = col_count * lax.axis_size("rcol")
    first_col = lax.axis_index("rcol") * col_count
    allowed = band_allowed(tissue_mask, band_offset, first_col, grid_cols, col_count)[:, None]

    def heads_first(tensor):
        return tensor.reshape(row_count, tensor.shape[1], head_count, HD).transpose(0, 2, 1, 3)

    def heads_last(tensor):
        return tensor.transpose(0, 2, 1, 3).reshape(row_count, tensor.shape[2], feature_width)

    grads_in = attention_grads(
        heads_first(queries),
        heads_first(span[0]),
        heads_first(span[1]),
        heads_first(out_grad),
        allowed,
    )
    query_part = heads_last(grads_in[0])
    whole = jnp.stack([heads_last(grads_in[1]), heads_last(grads_in[2])])
    own = whole[:, :, band_reach : band_reach + col_count]
    left_end = band_reach
    right_start = band_reach + col_count
    for distance, cut_width in zip(range(1, far_shards + 1), cut_widths):
        left_piece = whole[:, :, left_end - cut_width : left_end].astype(jnp.bfloat16)
        arrived = shifted(left_piece, "rcol", -distance)
        own = own.at[:, :, col_count - cut_width :].add(arrived.astype(jnp.float32))
        right_piece = whole[:, :, right_start : right_start + cut_width].astype(jnp.bfloat16)
        arrived = shifted(right_piece, "rcol", distance)
        own = own.at[:, :, :cut_width].add(arrived.astype(jnp.float32))
        left_end = left_end - cut_width
        right_start = right_start + cut_width
    return (query_part, own[0], own[1])


def column_wide(queries, key_grid, value_grid, out_grad):
    row_count, col_count, feature_width = queries.shape
    group_count = lax.axis_size("rrow")
    head_count = feature_width // HD
    stacked = jnp.stack([queries, key_grid, value_grid, out_grad])
    whole = lax.all_to_all(stacked, "rrow", split_axis=2, concat_axis=1, tiled=True)
    strip = whole.shape[2]

    def arrange(tensor):
        return tensor.reshape(group_count * row_count, strip, head_count, HD).transpose(1, 2, 0, 3)

    gradients = attention_grads(
        arrange(whole[0]), arrange(whole[1]), arrange(whole[2]), arrange(whole[3]), None
    )

    def restore(tensor):
        return tensor.astype(jnp.bfloat16).transpose(2, 0, 1, 3).reshape(
            group_count * row_count, strip, feature_width
        )

    back = jnp.stack([restore(g) for g in gradients])
    back = lax.all_to_all(back, "rrow", split_axis=1, concat_axis=2, tiled=True)
    return (back[0], back[1], back[2])


def body(queries, key_grid, value_grid, out_grad, tissue_mask, band_offset):
    row_grads = row_branch(queries, key_grid, value_grid, out_grad, tissue_mask, band_offset)
    col_grads = column_wide(queries, key_grid, value_grid, out_grad)
    query_grad = (row_grads[0] + col_grads[0].astype(jnp.float32)).astype(jnp.bfloat16)
    key_grad = (row_grads[1] + col_grads[1].astype(jnp.float32)).astype(jnp.bfloat16)
    value_grad = (row_grads[2] + col_grads[2].astype(jnp.float32)).astype(jnp.bfloat16)
    return (query_grad, key_grad, value_grad)


def solution(mesh):
    in_specs = (
        P(("slide", "rrow"), "rcol", None),
        P(("slide", "rrow"), "rcol", None),
        P(("slide", "rrow"), "rcol", None),
        P(("slide", "rrow"), "rcol", None),
        P(("slide", "rrow"), None),
        P(("slide", "rrow")),
    )
    out_specs = (
        P(("slide", "rrow"), "rcol", None),
        P(("slide", "rrow"), "rcol", None),
        P(("slide", "rrow"), "rcol", None),
    )
    return jax.shard_map(body, mesh=mesh, in_specs=in_specs, out_specs=out_specs, check_vma=False)
```

```python
import functools
import math

import jax
import jax.numpy as jnp
from jax import lax
from jax.experimental import pallas as pl
from jax.experimental.pallas import tpu as pltpu
from jax.sharding import PartitionSpec as P

HD = 64
BLK = 16
HALF = 32
OFFMAX = 16
SCALE = 1.0 / math.sqrt(HD)
LANES = 128


def shifted(block, axis, distance):
    devices = range(lax.axis_size(axis))
    route = [(i - distance, i) for i in devices if i - distance in devices]
    return lax.ppermute(block, axis, route)


def dot_nt(a, b):
    return lax.dot_general(a, b, (((1,), (1,)), ((), ())), preferred_element_type=jnp.float32)


def dot_tn(a, b):
    return lax.dot_general(a, b, (((0,), (0,)), ((), ())), preferred_element_type=jnp.float32)


def pair_grads(q2, k2, v2, g2, bias):
    lane = lax.broadcasted_iota(jnp.int32, (1, LANES), 1)
    low = lane < HD
    zero = jnp.zeros_like(q2)
    parts = []
    for keep in (low, jnp.logical_not(low)):
        qh = jnp.where(keep, q2, zero)
        gh = jnp.where(keep, g2, zero)
        s = dot_nt(qh, k2) * SCALE
        if bias is not None:
            s = s + bias
        mx = jnp.max(s, axis=1, keepdims=True)
        e = jnp.exp(s - mx)
        p = e / jnp.sum(e, axis=1, keepdims=True)
        pb = p.astype(jnp.bfloat16)
        o = jnp.dot(pb, v2, preferred_element_type=jnp.float32)
        delta = jnp.sum(gh.astype(jnp.float32) * o, axis=1, keepdims=True)
        gw = dot_nt(gh, v2)
        ds = (p * (gw - delta)).astype(jnp.bfloat16)
        dq = jnp.dot(ds, k2, preferred_element_type=jnp.float32) * SCALE
        dk = dot_tn(ds, q2) * SCALE
        dv = dot_tn(pb, g2)
        parts.append((dq, dk, dv))
    return tuple(jnp.where(low, a, b) for a, b in zip(parts[0], parts[1]))


def row_kernel(q_ref, g_ref, k_ref, v_ref, l2_ref, l1_ref, r1_ref, r2_ref, bias_ref,
               dq_ref, own_ref, ol2_ref, ol1_ref, or1_ref, or2_ref):
    w2 = l2_ref.shape[2]
    w1 = l1_ref.shape[2]
    cc = q_ref.shape[1]
    bias = bias_ref[0]
    for pair in range(q_ref.shape[2] // LANES):
        lanes = pl.ds(pair * LANES, LANES)

        def span(which, own_ref):
            return jnp.concatenate(
                [l2_ref[which, 0, :, lanes], l1_ref[which, 0, :, lanes], own_ref[0, :, lanes],
                 r1_ref[which, 0, :, lanes], r2_ref[which, 0, :, lanes]],
                axis=0,
            )

        k2 = span(0, k_ref)
        v2 = span(1, v_ref)
        dq, dk, dv = pair_grads(q_ref[0, :, lanes], k2, v2, g_ref[0, :, lanes], bias)
        dq_ref[0, :, lanes] = dq
        for which, full in ((0, dk), (1, dv)):
            ol2_ref[which, 0, :, lanes] = full[:w2].astype(jnp.bfloat16)
            ol1_ref[which, 0, :, lanes] = full[w2:w2 + w1].astype(jnp.bfloat16)
            own_ref[which, 0, :, lanes] = full[w2 + w1:w2 + w1 + cc]
            or1_ref[which, 0, :, lanes] = full[w2 + w1 + cc:w2 + 2 * w1 + cc].astype(jnp.bfloat16)
            or2_ref[which, 0, :, lanes] = full[w2 + 2 * w1 + cc:].astype(jnp.bfloat16)


def row_attention(queries, out_grad, key_grid, value_grid, l2, l1, r1, r2, bias):
    rows, cc, width = queries.shape
    w2 = l2.shape[2]
    w1 = l1.shape[2]

    def one(shape):
        return pl.BlockSpec((1,) + shape[1:], lambda r: (r,) + (0,) * (len(shape) - 1))

    def two(shape):
        return pl.BlockSpec((shape[0], 1) + shape[2:], lambda r: (0, r) + (0,) * (len(shape) - 2))

    out_shape = (
        jax.ShapeDtypeStruct((rows, cc, width), jnp.float32),
        jax.ShapeDtypeStruct((2, rows, cc, width), jnp.float32),
        jax.ShapeDtypeStruct((2, rows, w2, width), jnp.bfloat16),
        jax.ShapeDtypeStruct((2, rows, w1, width), jnp.bfloat16),
        jax.ShapeDtypeStruct((2, rows, w1, width), jnp.bfloat16),
        jax.ShapeDtypeStruct((2, rows, w2, width), jnp.bfloat16),
    )
    return pl.pallas_call(
        row_kernel,
        grid=(rows,),
        in_specs=[one(queries.shape), one(out_grad.shape), one(key_grid.shape),
                  one(value_grid.shape), two(l2.shape), two(l1.shape), two(r1.shape),
                  two(r2.shape), one(bias.shape)],
        out_specs=[one(out_shape[0].shape)] + [two(s.shape) for s in out_shape[1:]],
        out_shape=out_shape,
    )(queries, out_grad, key_grid, value_grid, l2, l1, r1, r2, bias)


def column_kernel(x_ref, o_ref):
    for pair in range(x_ref.shape[3] // LANES):
        lanes = pl.ds(pair * LANES, LANES)
        dq, dk, dv = pair_grads(
            x_ref[0, 0, :, lanes], x_ref[1, 0, :, lanes], x_ref[2, 0, :, lanes],
            x_ref[3, 0, :, lanes], None,
        )
        o_ref[0, 0, :, lanes] = dq.astype(jnp.bfloat16)
        o_ref[1, 0, :, lanes] = dk.astype(jnp.bfloat16)
        o_ref[2, 0, :, lanes] = dv.astype(jnp.bfloat16)


def column_attention(whole):
    arrays, strip, rows, width = whole.shape
    return pl.pallas_call(
        column_kernel,
        grid=(strip,),
        in_specs=[pl.BlockSpec((arrays, 1, rows, width), lambda c: (0, c, 0, 0))],
        out_specs=pl.BlockSpec((3, 1, rows, width), lambda c: (0, c, 0, 0)),
        out_shape=jax.ShapeDtypeStruct((3, strip, rows, width), jnp.bfloat16),
    )(whole)


def band_bias(mask_rows, offsets, first_col, grid_cols, block_cols):
    band_reach = HALF + OFFMAX
    query_cols = first_col + jnp.arange(block_cols, dtype=jnp.int32)
    key_cols = first_col - band_reach + jnp.arange(block_cols + 2 * band_reach, dtype=jnp.int32)
    inside = (key_cols >= 0) & (key_cols < grid_cols)
    key_block = jnp.clip(key_cols, 0, grid_cols - 1) // BLK
    block_ids = jnp.arange(mask_rows.shape[1], dtype=jnp.int32)
    key_open = jnp.sum(
        mask_rows[:, None, :]
        * (key_block[None, :, None] == block_ids[None, None, :]).astype(jnp.int32),
        axis=-1,
    )
    relative = key_cols[None, None, :] - query_cols[None, :, None] - offsets[:, None, None]
    same_block = key_cols[None, :] // BLK == query_cols[:, None] // BLK
    allowed = (
        (relative >= -HALF)
        & (relative < HALF)
        & inside[None, None, :]
        & ((key_open[:, None, :] > 0) | same_block[None])
    )
    return jnp.where(allowed, 0.0, -jnp.inf).astype(jnp.float32)


def body(queries, key_grid, value_grid, out_grad, tissue_mask, band_offset):
    row_count, col_count, feature_width = queries.shape
    group_count = lax.axis_size("rrow")
    band_reach = HALF + OFFMAX
    near = col_count
    far = band_reach - col_count

    stacked = jnp.stack([queries, key_grid, value_grid, out_grad]).transpose(0, 2, 1, 3)
    whole = lax.all_to_all(stacked, "rrow", split_axis=1, concat_axis=2, tiled=True)

    pair = jnp.stack([key_grid, value_grid])
    l1 = shifted(pair[:, :, col_count - near:], "rcol", 1)
    l2 = shifted(pair[:, :, col_count - far:], "rcol", 2)
    r1 = shifted(pair[:, :, :near], "rcol", -1)
    r2 = shifted(pair[:, :, :far], "rcol", -2)
    grid_cols = col_count * lax.axis_size("rcol")
    first_col = lax.axis_index("rcol") * col_count
    bias = band_bias(tissue_mask, band_offset, first_col, grid_cols, col_count)

    col_out = column_attention(whole)
    back = lax.all_to_all(col_out, "rrow", split_axis=2, concat_axis=1, tiled=True)

    dq_row, own, gl2, gl1, gr1, gr2 = row_attention(
        queries, out_grad, key_grid, value_grid, l2, l1, r1, r2, bias
    )
    from_r2 = shifted(gl2, "rcol", -2)
    from_r1 = shifted(gl1, "rcol", -1)
    from_l1 = shifted(gr1, "rcol", 1)
    from_l2 = shifted(gr2, "rcol", 2)
    f32 = jnp.float32
    kv = own
    kv = kv.at[:, :, col_count - far:].add(from_r2.astype(f32))
    kv = kv + from_r1.astype(f32)
    kv = kv + from_l1.astype(f32)
    kv = kv.at[:, :, :far].add(from_l2.astype(f32))
    back = back.transpose(0, 2, 1, 3).astype(f32)
    query_grad = (dq_row + back[0]).astype(jnp.bfloat16)
    key_grad = (kv[0] + back[1]).astype(jnp.bfloat16)
    value_grad = (kv[1] + back[2]).astype(jnp.bfloat16)
    return (query_grad, key_grad, value_grad)


def solution(mesh):
    in_specs = (
        P(("slide", "rrow"), "rcol", None),
        P(("slide", "rrow"), "rcol", None),
        P(("slide", "rrow"), "rcol", None),
        P(("slide", "rrow"), "rcol", None),
        P(("slide", "rrow"), None),
        P(("slide", "rrow")),
    )
    out_specs = (
        P(("slide", "rrow"), "rcol", None),
        P(("slide", "rrow"), "rcol", None),
        P(("slide", "rrow"), "rcol", None),
    )
    return jax.shard_map(body, mesh=mesh, in_specs=in_specs, out_specs=out_specs, check_vma=False)
```

```python
import functools
import math

import jax
import jax.numpy as jnp
from jax import lax
from jax.experimental import pallas as pl
from jax.experimental.pallas import tpu as pltpu
from jax.sharding import PartitionSpec as P

HD = 64
BLK = 16
HALF = 32
OFFMAX = 16
SCALE = 1.0 / math.sqrt(HD)
LANES = 128


def shifted(block, axis, distance):
    devices = range(lax.axis_size(axis))
    route = [(i - distance, i) for i in devices if i - distance in devices]
    return lax.ppermute(block, axis, route)


def dot_nt(a, b):
    return lax.dot_general(a, b, (((1,), (1,)), ((), ())), preferred_element_type=jnp.float32)


def dot_tn(a, b):
    return lax.dot_general(a, b, (((0,), (0,)), ((), ())), preferred_element_type=jnp.float32)


def head_stack(x, heads):
    rows, width = x.shape
    lane_head = lax.broadcasted_iota(jnp.int32, (heads, 1, width), 2) // HD
    which = lax.broadcasted_iota(jnp.int32, (heads, 1, width), 0)
    kept = jnp.where(lane_head == which, x[None], jnp.zeros_like(x)[None])
    return kept.reshape(heads * rows, width)


def block_grads(q, g, k, v, bias):
    nq, width = q.shape
    heads = width // HD
    qm = head_stack(q, heads)
    gm = head_stack(g, heads)
    full_bias = jnp.broadcast_to(bias[None], (heads,) + bias.shape).reshape(heads * nq, -1)
    s = dot_nt(qm, k) * SCALE + full_bias
    mx = jnp.max(s, axis=1, keepdims=True)
    e = jnp.exp(s - mx)
    p = e / jnp.sum(e, axis=1, keepdims=True)
    pb = p.astype(jnp.bfloat16)
    gw = dot_nt(gm, v)
    delta = jnp.sum(pb.astype(jnp.float32) * gw, axis=1, keepdims=True)
    ds = (p * (gw - delta)).astype(jnp.bfloat16)
    dk = dot_tn(ds, qm) * SCALE
    dv = dot_tn(pb, gm)
    lane = lax.broadcasted_iota(jnp.int32, (1, LANES), 1)
    low = lane < HD
    tiles = []
    for pair in range(width // LANES):
        both = jnp.dot(
            ds[2 * pair * nq:(2 * pair + 2) * nq],
            k[:, pair * LANES:(pair + 1) * LANES],
            preferred_element_type=jnp.float32,
        )
        tiles.append(jnp.where(low, both[:nq], both[nq:]) * SCALE)
    dq = jnp.concatenate(tiles, axis=1)
    return dq, dk, dv


def row_kernel(q_ref, g_ref, k_ref, v_ref, l2_ref, l1_ref, r1_ref, r2_ref, bias_ref,
               dq_ref, own_ref, ol2_ref, ol1_ref, or1_ref, or2_ref):
    w2 = l2_ref.shape[2]
    w1 = l1_ref.shape[2]
    cc = q_ref.shape[1]

    def span(which, own_ref):
        return jnp.concatenate(
            [l2_ref[which, 0], l1_ref[which, 0], own_ref[0], r1_ref[which, 0], r2_ref[which, 0]],
            axis=0,
        )

    dq, dk, dv = block_grads(q_ref[0], g_ref[0], span(0, k_ref), span(1, v_ref), bias_ref[0])
    dq_ref[0] = dq
    for which, full in ((0, dk), (1, dv)):
        ol2_ref[which, 0] = full[:w2].astype(jnp.bfloat16)
        ol1_ref[which, 0] = full[w2:w2 + w1].astype(jnp.bfloat16)
        own_ref[which, 0] = full[w2 + w1:w2 + w1 + cc]
        or1_ref[which, 0] = full[w2 + w1 + cc:w2 + 2 * w1 + cc].astype(jnp.bfloat16)
        or2_ref[which, 0] = full[w2 + 2 * w1 + cc:].astype(jnp.bfloat16)


def row_attention(queries, out_grad, key_grid, value_grid, l2, l1, r1, r2, bias):
    rows, cc, width = queries.shape
    w2 = l2.shape[2]
    w1 = l1.shape[2]

    def one(shape):
        return pl.BlockSpec((1,) + shape[1:], lambda r: (r,) + (0,) * (len(shape) - 1))

    def two(shape):
        return pl.BlockSpec((shape[0], 1) + shape[2:], lambda r: (0, r) + (0,) * (len(shape) - 2))

    out_shape = (
        jax.ShapeDtypeStruct((rows, cc, width), jnp.float32),
        jax.ShapeDtypeStruct((2, rows, cc, width), jnp.float32),
        jax.ShapeDtypeStruct((2, rows, w2, width), jnp.bfloat16),
        jax.ShapeDtypeStruct((2, rows, w1, width), jnp.bfloat16),
        jax.ShapeDtypeStruct((2, rows, w1, width), jnp.bfloat16),
        jax.ShapeDtypeStruct((2, rows, w2, width), jnp.bfloat16),
    )
    return pl.pallas_call(
        row_kernel,
        grid=(rows,),
        in_specs=[one(queries.shape), one(out_grad.shape), one(key_grid.shape),
                  one(value_grid.shape), two(l2.shape), two(l1.shape), two(r1.shape),
                  two(r2.shape), one(bias.shape)],
        out_specs=[one(out_shape[0].shape)] + [two(s.shape) for s in out_shape[1:]],
        out_shape=out_shape,
    )(queries, out_grad, key_grid, value_grid, l2, l1, r1, r2, bias)


def column_kernel(x_ref, o_ref):
    per = x_ref.shape[1]
    rows = x_ref.shape[2]

    def joined(which):
        return jnp.concatenate([x_ref[which, c] for c in range(per)], axis=0)

    i = lax.broadcasted_iota(jnp.int32, (per * rows, per * rows), 0) // rows
    j = lax.broadcasted_iota(jnp.int32, (per * rows, per * rows), 1) // rows
    bias = jnp.where(i == j, 0.0, -jnp.inf).astype(jnp.float32)
    grads = block_grads(joined(0), joined(3), joined(1), joined(2), bias)
    for which, full in enumerate(grads):
        for c in range(per):
            o_ref[which, c] = full[c * rows:(c + 1) * rows].astype(jnp.bfloat16)


def column_attention(whole):
    arrays, strip, rows, width = whole.shape
    per = max(1, LANES // rows)
    return pl.pallas_call(
        column_kernel,
        grid=(strip // per,),
        in_specs=[pl.BlockSpec((arrays, per, rows, width), lambda c: (0, c, 0, 0))],
        out_specs=pl.BlockSpec((3, per, rows, width), lambda c: (0, c, 0, 0)),
        out_shape=jax.ShapeDtypeStruct((3, strip, rows, width), jnp.bfloat16),
    )(whole)


def band_bias(mask_rows, offsets, first_col, grid_cols, block_cols):
    band_reach = HALF + OFFMAX
    query_cols = first_col + jnp.arange(block_cols, dtype=jnp.int32)
    key_cols = first_col - band_reach + jnp.arange(block_cols + 2 * band_reach, dtype=jnp.int32)
    inside = (key_cols >= 0) & (key_cols < grid_cols)
    key_block = jnp.clip(key_cols, 0, grid_cols - 1) // BLK
    block_ids = jnp.arange(mask_rows.shape[1], dtype=jnp.int32)
    key_open = jnp.sum(
        mask_rows[:, None, :]
        * (key_block[None, :, None] == block_ids[None, None, :]).astype(jnp.int32),
        axis=-1,
    )
    relative = key_cols[None, None, :] - query_cols[None, :, None] - offsets[:, None, None]
    same_block = key_cols[None, :] // BLK == query_cols[:, None] // BLK
    allowed = (
        (relative >= -HALF)
        & (relative < HALF)
        & inside[None, None, :]
        & ((key_open[:, None, :] > 0) | same_block[None])
    )
    return jnp.where(allowed, 0.0, -jnp.inf).astype(jnp.float32)


def body(queries, key_grid, value_grid, out_grad, tissue_mask, band_offset):
    row_count, col_count, feature_width = queries.shape
    group_count = lax.axis_size("rrow")
    band_reach = HALF + OFFMAX
    near = col_count
    far = band_reach - col_count

    stacked = jnp.stack([queries, key_grid, value_grid, out_grad]).transpose(0, 2, 1, 3)
    whole = lax.all_to_all(stacked, "rrow", split_axis=1, concat_axis=2, tiled=True)

    pair = jnp.stack([key_grid, value_grid])
    l1 = shifted(pair[:, :, col_count - near:], "rcol", 1)
    l2 = shifted(pair[:, :, col_count - far:], "rcol", 2)
    r1 = shifted(pair[:, :, :near], "rcol", -1)
    r2 = shifted(pair[:, :, :far], "rcol", -2)
    grid_cols = col_count * lax.axis_size("rcol")
    first_col = lax.axis_index("rcol") * col_count
    bias = band_bias(tissue_mask, band_offset, first_col, grid_cols, col_count)

    col_out = column_attention(whole)
    back = lax.all_to_all(col_out, "rrow", split_axis=2, concat_axis=1, tiled=True)

    dq_row, own, gl2, gl1, gr1, gr2 = row_attention(
        queries, out_grad, key_grid, value_grid, l2, l1, r1, r2, bias
    )
    from_r2 = shifted(gl2, "rcol", -2)
    from_r1 = shifted(gl1, "rcol", -1)
    from_l1 = shifted(gr1, "rcol", 1)
    from_l2 = shifted(gr2, "rcol", 2)
    f32 = jnp.float32
    kv = own
    kv = kv.at[:, :, col_count - far:].add(from_r2.astype(f32))
    kv = kv + from_r1.astype(f32)
    kv = kv + from_l1.astype(f32)
    kv = kv.at[:, :, :far].add(from_l2.astype(f32))
    back = back.transpose(0, 2, 1, 3).astype(f32)
    query_grad = (dq_row + back[0]).astype(jnp.bfloat16)
    key_grad = (kv[0] + back[1]).astype(jnp.bfloat16)
    value_grad = (kv[1] + back[2]).astype(jnp.bfloat16)
    return (query_grad, key_grad, value_grad)


def solution(mesh):
    in_specs = (
        P(("slide", "rrow"), "rcol", None),
        P(("slide", "rrow"), "rcol", None),
        P(("slide", "rrow"), "rcol", None),
        P(("slide", "rrow"), "rcol", None),
        P(("slide", "rrow"), None),
        P(("slide", "rrow")),
    )
    out_specs = (
        P(("slide", "rrow"), "rcol", None),
        P(("slide", "rrow"), "rcol", None),
        P(("slide", "rrow"), "rcol", None),
    )
    return jax.shard_map(body, mesh=mesh, in_specs=in_specs, out_specs=out_specs, check_vma=False)
```

```python
import functools
import math

import jax
import jax.numpy as jnp
from jax import lax
from jax.experimental import pallas as pl
from jax.experimental.pallas import tpu as pltpu
from jax.sharding import PartitionSpec as P

HD = 64
BLK = 16
HALF = 32
OFFMAX = 16
SCALE = 1.0 / math.sqrt(HD)
LANES = 128


def shifted(block, axis, distance):
    devices = range(lax.axis_size(axis))
    route = [(i - distance, i) for i in devices if i - distance in devices]
    return lax.ppermute(block, axis, route)


def dot_nt(a, b):
    return lax.dot_general(a, b, (((1,), (1,)), ((), ())), preferred_element_type=jnp.float32)


def dot_tn(a, b):
    return lax.dot_general(a, b, (((0,), (0,)), ((), ())), preferred_element_type=jnp.float32)


def head_stack(x, heads):
    rows, width = x.shape
    lane_head = lax.broadcasted_iota(jnp.int32, (heads, 1, width), 2) // HD
    which = lax.broadcasted_iota(jnp.int32, (heads, 1, width), 0)
    kept = jnp.where(lane_head == which, x[None], jnp.zeros_like(x)[None])
    return kept.reshape(heads * rows, width)


def block_grads(q, g, k, v, bias):
    nq, width = q.shape
    heads = width // HD
    qm = head_stack(q, heads)
    gm = head_stack(g, heads)
    full_bias = jnp.broadcast_to(bias[None], (heads,) + bias.shape).reshape(heads * nq, -1)
    s = dot_nt(qm, k) * SCALE + full_bias
    mx = jnp.max(s, axis=1, keepdims=True)
    e = jnp.exp(s - mx)
    p = e / jnp.sum(e, axis=1, keepdims=True)
    pb = p.astype(jnp.bfloat16)
    gw = dot_nt(gm, v)
    delta = jnp.sum(pb.astype(jnp.float32) * gw, axis=1, keepdims=True)
    ds = (p * (gw - delta)).astype(jnp.bfloat16)
    dk = dot_tn(ds, qm) * SCALE
    dv = dot_tn(pb, gm)
    lane = lax.broadcasted_iota(jnp.int32, (1, LANES), 1)
    low = lane < HD
    tiles = []
    for pair in range(width // LANES):
        both = jnp.dot(
            ds[2 * pair * nq:(2 * pair + 2) * nq],
            k[:, pair * LANES:(pair + 1) * LANES],
            preferred_element_type=jnp.float32,
        )
        tiles.append(jnp.where(low, both[:nq], both[nq:]) * SCALE)
    dq = jnp.concatenate(tiles, axis=1)
    return dq, dk, dv


def fused_row_kernel(q_ref, g_ref, k_ref, v_ref, l2_ref, l1_ref, r1_ref, r2_ref, bias_ref, cb_ref,
                     qg_ref, kg_ref, vg_ref,
                     own_s, s_l2, s_l1, s_r1, s_r2, x_r2, x_r1, x_l1, x_l2, send_sem, recv_sem):
    rows, cc, width = q_ref.shape
    w2 = l2_ref.shape[2]
    w1 = l1_ref.shape[2]
    n = lax.axis_size("rcol")
    me = lax.axis_index("rcol")
    here = (lax.axis_index("slide"), lax.axis_index("rrow"))

    def dev(distance):
        return here + (lax.rem(me + distance + n, n),)

    barrier = pltpu.get_barrier_semaphore()
    for distance in (-2, -1, 1, 2):
        pl.semaphore_signal(barrier, 1, device_id=dev(distance), device_id_type=pl.DeviceIdType.MESH)
    pl.semaphore_wait(barrier, 4)

    routes = ((s_l2, x_r2, -2), (s_l1, x_r1, -1), (s_r1, x_l1, 1), (s_r2, x_l2, 2))

    def row_step(r, carry):
        def span(which, own_ref):
            return jnp.concatenate(
                [l2_ref[which, r], l1_ref[which, r], own_ref[r], r1_ref[which, r],
                 r2_ref[which, r]],
                axis=0,
            )

        dq, dk, dv = block_grads(q_ref[r], g_ref[r], span(0, k_ref), span(1, v_ref), bias_ref[r])
        qg_ref[r] = (dq + cb_ref[0, r].astype(jnp.float32)).astype(jnp.bfloat16)
        for which, full in ((0, dk), (1, dv)):
            s_l2[which, r] = full[:w2].astype(jnp.bfloat16)
            s_l1[which, r] = full[w2:w2 + w1].astype(jnp.bfloat16)
            own_s[which, r] = full[w2 + w1:w2 + w1 + cc]
            s_r1[which, r] = full[w2 + w1 + cc:w2 + 2 * w1 + cc].astype(jnp.bfloat16)
            s_r2[which, r] = full[w2 + 2 * w1 + cc:].astype(jnp.bfloat16)
        for slot, (src, dst, distance) in enumerate(routes):
            pltpu.make_async_remote_copy(
                src_ref=src.at[:, pl.ds(r, 1)],
                dst_ref=dst.at[:, pl.ds(r, 1)],
                send_sem=send_sem.at[slot],
                recv_sem=recv_sem.at[slot],
                device_id=dev(distance),
                device_id_type=pl.DeviceIdType.MESH,
            ).start()
        return carry

    lax.fori_loop(0, rows, row_step, 0)
    for slot, (src, dst, distance) in enumerate(routes):
        pltpu.make_async_remote_copy(
            src_ref=src, dst_ref=dst, send_sem=send_sem.at[slot], recv_sem=recv_sem.at[slot],
            device_id=dev(distance), device_id_type=pl.DeviceIdType.MESH,
        ).wait()
    f32 = jnp.float32
    for which, out_ref in ((0, kg_ref), (1, vg_ref)):
        total = own_s[which] + x_r1[which].astype(f32) + x_l1[which].astype(f32)
        total = total + cb_ref[which + 1].astype(f32)
        low = total[:, :w2] + x_l2[which].astype(f32)
        high = total[:, cc - w2:] + x_r2[which].astype(f32)
        out_ref[:, :w2] = low.astype(jnp.bfloat16)
        out_ref[:, cc - w2:] = high.astype(jnp.bfloat16)
        if cc > 2 * w2:
            out_ref[:, w2:cc - w2] = total[:, w2:cc - w2].astype(jnp.bfloat16)


def fused_row(queries, out_grad, key_grid, value_grid, l2, l1, r1, r2, bias, col_back):
    rows, cc, width = queries.shape
    w2 = l2.shape[2]
    w1 = l1.shape[2]
    vmem = pl.BlockSpec(memory_space=pltpu.VMEM)
    grads = jax.ShapeDtypeStruct((rows, cc, width), jnp.bfloat16)
    bf = jnp.bfloat16
    return pl.pallas_call(
        fused_row_kernel,
        in_specs=[vmem] * 10,
        out_specs=[vmem] * 3,
        out_shape=(grads, grads, grads),
        scratch_shapes=[
            pltpu.VMEM((2, rows, cc, width), jnp.float32),
            pltpu.VMEM((2, rows, w2, width), bf),
            pltpu.VMEM((2, rows, w1, width), bf),
            pltpu.VMEM((2, rows, w1, width), bf),
            pltpu.VMEM((2, rows, w2, width), bf),
            pltpu.VMEM((2, rows, w2, width), bf),
            pltpu.VMEM((2, rows, w1, width), bf),
            pltpu.VMEM((2, rows, w1, width), bf),
            pltpu.VMEM((2, rows, w2, width), bf),
            pltpu.SemaphoreType.DMA((4,)),
            pltpu.SemaphoreType.DMA((4,)),
        ],
        compiler_params=pltpu.CompilerParams(
            collective_id=0, has_side_effects=True, vmem_limit_bytes=60 * 1024 * 1024
        ),
    )(queries, out_grad, key_grid, value_grid, l2, l1, r1, r2, bias, col_back)


def column_kernel(width, x_ref, o_ref):
    rows, span_width = x_ref.shape[1], x_ref.shape[2]
    per = span_width // width

    def joined(which):
        return jnp.concatenate(
            [x_ref[which, :, c * width:(c + 1) * width] for c in range(per)], axis=0
        )

    i = lax.broadcasted_iota(jnp.int32, (per * rows, per * rows), 0) // rows
    j = lax.broadcasted_iota(jnp.int32, (per * rows, per * rows), 1) // rows
    bias = jnp.where(i == j, 0.0, -jnp.inf).astype(jnp.float32)
    grads = block_grads(joined(0), joined(3), joined(1), joined(2), bias)
    for which, full in enumerate(grads):
        for c in range(per):
            o_ref[which, :, c * width:(c + 1) * width] = (
                full[c * rows:(c + 1) * rows].astype(jnp.bfloat16)
            )


def column_attention(whole, width):
    arrays, rows, lanes = whole.shape
    per = max(1, LANES // rows)
    block = per * width
    return pl.pallas_call(
        functools.partial(column_kernel, width),
        grid=(lanes // block,),
        in_specs=[pl.BlockSpec((arrays, rows, block), lambda c: (0, 0, c))],
        out_specs=pl.BlockSpec((3, rows, block), lambda c: (0, 0, c)),
        out_shape=jax.ShapeDtypeStruct((3, rows, lanes), jnp.bfloat16),
    )(whole)


def band_bias(mask_rows, offsets, first_col, grid_cols, block_cols):
    band_reach = HALF + OFFMAX
    query_cols = first_col + jnp.arange(block_cols, dtype=jnp.int32)
    key_cols = first_col - band_reach + jnp.arange(block_cols + 2 * band_reach, dtype=jnp.int32)
    inside = (key_cols >= 0) & (key_cols < grid_cols)
    key_block = jnp.clip(key_cols, 0, grid_cols - 1) // BLK
    block_ids = jnp.arange(mask_rows.shape[1], dtype=jnp.int32)
    key_open = jnp.sum(
        mask_rows[:, None, :]
        * (key_block[None, :, None] == block_ids[None, None, :]).astype(jnp.int32),
        axis=-1,
    )
    relative = key_cols[None, None, :] - query_cols[None, :, None] - offsets[:, None, None]
    same_block = key_cols[None, :] // BLK == query_cols[:, None] // BLK
    allowed = (
        (relative >= -HALF)
        & (relative < HALF)
        & inside[None, None, :]
        & ((key_open[:, None, :] > 0) | same_block[None])
    )
    return jnp.where(allowed, 0.0, -jnp.inf).astype(jnp.float32)


def body(queries, key_grid, value_grid, out_grad, tissue_mask, band_offset):
    row_count, col_count, feature_width = queries.shape
    group_count = lax.axis_size("rrow")
    band_reach = HALF + OFFMAX
    near = col_count
    far = band_reach - col_count

    stacked = jnp.stack([queries, key_grid, value_grid, out_grad]).reshape(
        4, row_count, col_count * feature_width
    )
    whole = lax.all_to_all(stacked, "rrow", split_axis=2, concat_axis=1, tiled=True)

    pair = jnp.stack([key_grid, value_grid])
    l1 = shifted(pair[:, :, col_count - near:], "rcol", 1)
    l2 = shifted(pair[:, :, col_count - far:], "rcol", 2)
    r1 = shifted(pair[:, :, :near], "rcol", -1)
    r2 = shifted(pair[:, :, :far], "rcol", -2)
    grid_cols = col_count * lax.axis_size("rcol")
    first_col = lax.axis_index("rcol") * col_count
    bias = band_bias(tissue_mask, band_offset, first_col, grid_cols, col_count)

    col_out = column_attention(whole, feature_width)
    back = lax.all_to_all(col_out, "rrow", split_axis=1, concat_axis=2, tiled=True)
    back = back.reshape(3, row_count, col_count, feature_width)
    return fused_row(queries, out_grad, key_grid, value_grid, l2, l1, r1, r2, bias, back)


def solution(mesh):
    in_specs = (
        P(("slide", "rrow"), "rcol", None),
        P(("slide", "rrow"), "rcol", None),
        P(("slide", "rrow"), "rcol", None),
        P(("slide", "rrow"), "rcol", None),
        P(("slide", "rrow"), None),
        P(("slide", "rrow")),
    )
    out_specs = (
        P(("slide", "rrow"), "rcol", None),
        P(("slide", "rrow"), "rcol", None),
        P(("slide", "rrow"), "rcol", None),
    )
    return jax.shard_map(body, mesh=mesh, in_specs=in_specs, out_specs=out_specs, check_vma=False)
```

```python
import functools
import math

import jax
import jax.numpy as jnp
from jax import lax
from jax.experimental import pallas as pl
from jax.experimental.pallas import tpu as pltpu
from jax.sharding import PartitionSpec as P

HD = 64
BLK = 16
HALF = 32
OFFMAX = 16
SCALE = 1.0 / math.sqrt(HD)
LANES = 128


def shifted(block, axis, distance):
    devices = range(lax.axis_size(axis))
    route = [(i - distance, i) for i in devices if i - distance in devices]
    return lax.ppermute(block, axis, route)


def dot_nt(a, b):
    return lax.dot_general(a, b, (((1,), (1,)), ((), ())), preferred_element_type=jnp.float32)


def dot_tn(a, b):
    return lax.dot_general(a, b, (((0,), (0,)), ((), ())), preferred_element_type=jnp.float32)


def head_stack(x, heads):
    rows, width = x.shape
    lane_head = lax.broadcasted_iota(jnp.int32, (heads, 1, width), 2) // HD
    which = lax.broadcasted_iota(jnp.int32, (heads, 1, width), 0)
    kept = jnp.where(lane_head == which, x[None], jnp.zeros_like(x)[None])
    return kept.reshape(heads * rows, width)


def block_grads(q, g, k, v, bias):
    nq, width = q.shape
    heads = width // HD
    qm = head_stack(q, heads)
    gm = head_stack(g, heads)
    full_bias = jnp.broadcast_to(bias[None], (heads,) + bias.shape).reshape(heads * nq, -1)
    s = dot_nt(qm, k) * SCALE + full_bias
    mx = jnp.max(s, axis=1, keepdims=True)
    e = jnp.exp(s - mx)
    p = e / jnp.sum(e, axis=1, keepdims=True)
    pb = p.astype(jnp.bfloat16)
    gw = dot_nt(gm, v)
    delta = jnp.sum(pb.astype(jnp.float32) * gw, axis=1, keepdims=True)
    ds = (p * (gw - delta)).astype(jnp.bfloat16)
    dk = dot_tn(ds, qm) * SCALE
    dv = dot_tn(pb, gm)
    lane = lax.broadcasted_iota(jnp.int32, (1, LANES), 1)
    low = lane < HD
    tiles = []
    for pair in range(width // LANES):
        both = jnp.dot(
            ds[2 * pair * nq:(2 * pair + 2) * nq],
            k[:, pair * LANES:(pair + 1) * LANES],
            preferred_element_type=jnp.float32,
        )
        tiles.append(jnp.where(low, both[:nq], both[nq:]) * SCALE)
    dq = jnp.concatenate(tiles, axis=1)
    return dq, dk, dv


def fused_row_kernel(q_ref, g_ref, k_ref, v_ref, l2_ref, l1_ref, r1_ref, r2_ref, bias_ref, cb_ref,
                     qg_ref, kg_ref, vg_ref,
                     own_s, s_l2, s_l1, s_r1, s_r2, x_r2, x_r1, x_l1, x_l2, send_sem, recv_sem):
    rows, cc, width = q_ref.shape
    w2 = l2_ref.shape[2]
    w1 = l1_ref.shape[2]
    n = lax.axis_size("rcol")
    me = lax.axis_index("rcol")
    here = (lax.axis_index("slide"), lax.axis_index("rrow"))

    def dev(distance):
        return here + (lax.rem(me + distance + n, n),)

    barrier = pltpu.get_barrier_semaphore()
    for distance in (-2, -1, 1, 2):
        pl.semaphore_signal(barrier, 1, device_id=dev(distance), device_id_type=pl.DeviceIdType.MESH)
    pl.semaphore_wait(barrier, 4)

    routes = ((s_l2, x_r2, -2), (s_l1, x_r1, -1), (s_r1, x_l1, 1), (s_r2, x_l2, 2))

    def row_step(r, carry):
        def span(which, own_ref):
            return jnp.concatenate(
                [l2_ref[which, r], l1_ref[which, r], own_ref[r], r1_ref[which, r],
                 r2_ref[which, r]],
                axis=0,
            )

        dq, dk, dv = block_grads(q_ref[r], g_ref[r], span(0, k_ref), span(1, v_ref), bias_ref[r])
        qg_ref[r] = (dq + cb_ref[0, r].astype(jnp.float32)).astype(jnp.bfloat16)
        for which, full in ((0, dk), (1, dv)):
            s_l2[which, r] = full[:w2].astype(jnp.bfloat16)
            s_l1[which, r] = full[w2:w2 + w1].astype(jnp.bfloat16)
            own_s[which, r] = full[w2 + w1:w2 + w1 + cc]
            s_r1[which, r] = full[w2 + w1 + cc:w2 + 2 * w1 + cc].astype(jnp.bfloat16)
            s_r2[which, r] = full[w2 + 2 * w1 + cc:].astype(jnp.bfloat16)
        for slot, (src, dst, distance) in enumerate(routes):
            pltpu.make_async_remote_copy(
                src_ref=src.at[:, pl.ds(r, 1)],
                dst_ref=dst.at[:, pl.ds(r, 1)],
                send_sem=send_sem.at[slot],
                recv_sem=recv_sem.at[slot],
                device_id=dev(distance),
                device_id_type=pl.DeviceIdType.MESH,
            ).start()
        return carry

    lax.fori_loop(0, rows, row_step, 0)
    for slot, (src, dst, distance) in enumerate(routes):
        pltpu.make_async_remote_copy(
            src_ref=src, dst_ref=dst, send_sem=send_sem.at[slot], recv_sem=recv_sem.at[slot],
            device_id=dev(distance), device_id_type=pl.DeviceIdType.MESH,
        ).wait()
    f32 = jnp.float32
    for which, out_ref in ((0, kg_ref), (1, vg_ref)):
        total = own_s[which] + x_r1[which].astype(f32) + x_l1[which].astype(f32)
        total = total + cb_ref[which + 1].astype(f32)
        low = total[:, :w2] + x_l2[which].astype(f32)
        high = total[:, cc - w2:] + x_r2[which].astype(f32)
        out_ref[:, :w2] = low.astype(jnp.bfloat16)
        out_ref[:, cc - w2:] = high.astype(jnp.bfloat16)
        if cc > 2 * w2:
            out_ref[:, w2:cc - w2] = total[:, w2:cc - w2].astype(jnp.bfloat16)


def fused_row(queries, out_grad, key_grid, value_grid, l2, l1, r1, r2, bias, col_back):
    rows, cc, width = queries.shape
    w2 = l2.shape[2]
    w1 = l1.shape[2]
    vmem = pl.BlockSpec(memory_space=pltpu.VMEM)
    grads = jax.ShapeDtypeStruct((rows, cc, width), jnp.bfloat16)
    bf = jnp.bfloat16
    return pl.pallas_call(
        fused_row_kernel,
        in_specs=[vmem] * 10,
        out_specs=[vmem] * 3,
        out_shape=(grads, grads, grads),
        scratch_shapes=[
            pltpu.VMEM((2, rows, cc, width), jnp.float32),
            pltpu.VMEM((2, rows, w2, width), bf),
            pltpu.VMEM((2, rows, w1, width), bf),
            pltpu.VMEM((2, rows, w1, width), bf),
            pltpu.VMEM((2, rows, w2, width), bf),
            pltpu.VMEM((2, rows, w2, width), bf),
            pltpu.VMEM((2, rows, w1, width), bf),
            pltpu.VMEM((2, rows, w1, width), bf),
            pltpu.VMEM((2, rows, w2, width), bf),
            pltpu.SemaphoreType.DMA((4,)),
            pltpu.SemaphoreType.DMA((4,)),
        ],
        compiler_params=pltpu.CompilerParams(
            collective_id=0, has_side_effects=True, vmem_limit_bytes=60 * 1024 * 1024
        ),
    )(queries, out_grad, key_grid, value_grid, l2, l1, r1, r2, bias, col_back)


def column_kernel(x_ref, o_ref):
    per = x_ref.shape[1]
    rows = x_ref.shape[2]

    def joined(which):
        return jnp.concatenate([x_ref[which, c] for c in range(per)], axis=0)

    i = lax.broadcasted_iota(jnp.int32, (per * rows, per * rows), 0) // rows
    j = lax.broadcasted_iota(jnp.int32, (per * rows, per * rows), 1) // rows
    bias = jnp.where(i == j, 0.0, -jnp.inf).astype(jnp.float32)
    grads = block_grads(joined(0), joined(3), joined(1), joined(2), bias)
    for which, full in enumerate(grads):
        for c in range(per):
            o_ref[which, c] = full[c * rows:(c + 1) * rows].astype(jnp.bfloat16)


def column_attention(whole):
    arrays, strip, rows, width = whole.shape
    per = max(1, LANES // rows)
    return pl.pallas_call(
        column_kernel,
        grid=(strip // per,),
        in_specs=[pl.BlockSpec((arrays, per, rows, width), lambda c: (0, c, 0, 0))],
        out_specs=pl.BlockSpec((3, per, rows, width), lambda c: (0, c, 0, 0)),
        out_shape=jax.ShapeDtypeStruct((3, strip, rows, width), jnp.bfloat16),
    )(whole)


def band_bias(mask_rows, offsets, first_col, grid_cols, block_cols):
    band_reach = HALF + OFFMAX
    query_cols = first_col + jnp.arange(block_cols, dtype=jnp.int32)
    key_cols = first_col - band_reach + jnp.arange(block_cols + 2 * band_reach, dtype=jnp.int32)
    inside = (key_cols >= 0) & (key_cols < grid_cols)
    key_block = jnp.clip(key_cols, 0, grid_cols - 1) // BLK
    block_ids = jnp.arange(mask_rows.shape[1], dtype=jnp.int32)
    key_open = jnp.sum(
        mask_rows[:, None, :]
        * (key_block[None, :, None] == block_ids[None, None, :]).astype(jnp.int32),
        axis=-1,
    )
    relative = key_cols[None, None, :] - query_cols[None, :, None] - offsets[:, None, None]
    same_block = key_cols[None, :] // BLK == query_cols[:, None] // BLK
    allowed = (
        (relative >= -HALF)
        & (relative < HALF)
        & inside[None, None, :]
        & ((key_open[:, None, :] > 0) | same_block[None])
    )
    return jnp.where(allowed, 0.0, -jnp.inf).astype(jnp.float32)


def body(queries, key_grid, value_grid, out_grad, tissue_mask, band_offset):
    row_count, col_count, feature_width = queries.shape
    group_count = lax.axis_size("rrow")
    band_reach = HALF + OFFMAX
    near = col_count
    far = band_reach - col_count

    stacked = jnp.stack([queries, key_grid, value_grid, out_grad]).transpose(0, 2, 1, 3)
    whole = lax.all_to_all(stacked, "rrow", split_axis=1, concat_axis=2, tiled=True)

    pair = jnp.stack([key_grid, value_grid])
    l1 = shifted(pair[:, :, col_count - near:], "rcol", 1)
    l2 = shifted(pair[:, :, col_count - far:], "rcol", 2)
    r1 = shifted(pair[:, :, :near], "rcol", -1)
    r2 = shifted(pair[:, :, :far], "rcol", -2)
    grid_cols = col_count * lax.axis_size("rcol")
    first_col = lax.axis_index("rcol") * col_count
    bias = band_bias(tissue_mask, band_offset, first_col, grid_cols, col_count)

    col_out = column_attention(whole)
    back = lax.all_to_all(col_out, "rrow", split_axis=2, concat_axis=1, tiled=True)
    back = back.transpose(0, 2, 1, 3)
    return fused_row(queries, out_grad, key_grid, value_grid, l2, l1, r1, r2, bias, back)


def solution(mesh):
    in_specs = (
        P(("slide", "rrow"), "rcol", None),
        P(("slide", "rrow"), "rcol", None),
        P(("slide", "rrow"), "rcol", None),
        P(("slide", "rrow"), "rcol", None),
        P(("slide", "rrow"), None),
        P(("slide", "rrow")),
    )
    out_specs = (
        P(("slide", "rrow"), "rcol", None),
        P(("slide", "rrow"), "rcol", None),
        P(("slide", "rrow"), "rcol", None),
    )
    return jax.shard_map(body, mesh=mesh, in_specs=in_specs, out_specs=out_specs, check_vma=False)
```

```python
import functools
import math

import jax
import jax.numpy as jnp
from jax import lax
from jax.experimental import pallas as pl
from jax.experimental.pallas import tpu as pltpu
from jax.sharding import PartitionSpec as P

HD = 64
BLK = 16
HALF = 32
OFFMAX = 16
SCALE = 1.0 / math.sqrt(HD)
LANES = 128


def shifted(block, axis, distance):
    devices = range(lax.axis_size(axis))
    route = [(i - distance, i) for i in devices if i - distance in devices]
    return lax.ppermute(block, axis, route)


def dot_nt(a, b):
    return lax.dot_general(a, b, (((1,), (1,)), ((), ())), preferred_element_type=jnp.float32)


def dot_tn(a, b):
    return lax.dot_general(a, b, (((0,), (0,)), ((), ())), preferred_element_type=jnp.float32)


def head_stack(x, heads):
    rows, width = x.shape
    lane_head = lax.broadcasted_iota(jnp.int32, (heads, 1, width), 2) // HD
    which = lax.broadcasted_iota(jnp.int32, (heads, 1, width), 0)
    kept = jnp.where(lane_head == which, x[None], jnp.zeros_like(x)[None])
    return kept.reshape(heads * rows, width)


def block_grads(q, g, k, v, bias):
    nq, width = q.shape
    heads = width // HD
    qm = head_stack(q, heads)
    gm = head_stack(g, heads)
    full_bias = jnp.broadcast_to(bias[None], (heads,) + bias.shape).reshape(heads * nq, -1)
    s = dot_nt(qm, k) * SCALE + full_bias
    mx = jnp.max(s, axis=1, keepdims=True)
    e = jnp.exp(s - mx)
    p = e / jnp.sum(e, axis=1, keepdims=True)
    pb = p.astype(jnp.bfloat16)
    gw = dot_nt(gm, v)
    delta = jnp.sum(pb.astype(jnp.float32) * gw, axis=1, keepdims=True)
    ds = (p * (gw - delta)).astype(jnp.bfloat16)
    dk = dot_tn(ds, qm) * SCALE
    dv = dot_tn(pb, gm)
    lane = lax.broadcasted_iota(jnp.int32, (1, LANES), 1)
    low = lane < HD
    tiles = []
    for pair in range(width // LANES):
        both = jnp.dot(
            ds[2 * pair * nq:(2 * pair + 2) * nq],
            k[:, pair * LANES:(pair + 1) * LANES],
            preferred_element_type=jnp.float32,
        )
        tiles.append(jnp.where(low, both[:nq], both[nq:]) * SCALE)
    dq = jnp.concatenate(tiles, axis=1)
    return dq, dk, dv


def fused_row_kernel(q_ref, g_ref, k_ref, v_ref, l2_ref, l1_ref, r1_ref, r2_ref, bias_ref, cb_ref,
                     qg_ref, kg_ref, vg_ref,
                     own_s, s_l2, s_l1, s_r1, s_r2, x_r2, x_r1, x_l1, x_l2, send_sem, recv_sem):
    rows, cc, width = q_ref.shape
    w2 = l2_ref.shape[2]
    w1 = l1_ref.shape[2]
    n = lax.axis_size("rcol")
    me = lax.axis_index("rcol")
    here = (lax.axis_index("slide"), lax.axis_index("rrow"))

    def dev(distance):
        return here + (lax.rem(me + distance + n, n),)

    barrier = pltpu.get_barrier_semaphore()
    for distance in (-2, -1, 1, 2):
        pl.semaphore_signal(barrier, 1, device_id=dev(distance), device_id_type=pl.DeviceIdType.MESH)
    pl.semaphore_wait(barrier, 4)

    routes = ((s_l2, x_r2, -2), (s_l1, x_r1, -1), (s_r1, x_l1, 1), (s_r2, x_l2, 2))

    def row_step(r, carry):
        def span(which, own_ref):
            return jnp.concatenate(
                [l2_ref[which, r], l1_ref[which, r], own_ref[r], r1_ref[which, r],
                 r2_ref[which, r]],
                axis=0,
            )

        dq, dk, dv = block_grads(q_ref[r], g_ref[r], span(0, k_ref), span(1, v_ref), bias_ref[r])
        qg_ref[r] = (dq + cb_ref[0, r].astype(jnp.float32)).astype(jnp.bfloat16)
        for which, full in ((0, dk), (1, dv)):
            s_l2[which, r] = full[:w2].astype(jnp.bfloat16)
            s_l1[which, r] = full[w2:w2 + w1].astype(jnp.bfloat16)
            own_s[which, r] = full[w2 + w1:w2 + w1 + cc]
            s_r1[which, r] = full[w2 + w1 + cc:w2 + 2 * w1 + cc].astype(jnp.bfloat16)
            s_r2[which, r] = full[w2 + 2 * w1 + cc:].astype(jnp.bfloat16)
        for slot, (src, dst, distance) in enumerate(routes):
            pltpu.make_async_remote_copy(
                src_ref=src.at[:, pl.ds(r, 1)],
                dst_ref=dst.at[:, pl.ds(r, 1)],
                send_sem=send_sem.at[slot],
                recv_sem=recv_sem.at[slot],
                device_id=dev(distance),
                device_id_type=pl.DeviceIdType.MESH,
            ).start()
        return carry

    lax.fori_loop(0, rows, row_step, 0)
    for slot, (src, dst, distance) in enumerate(routes):
        pltpu.make_async_remote_copy(
            src_ref=src, dst_ref=dst, send_sem=send_sem.at[slot], recv_sem=recv_sem.at[slot],
            device_id=dev(distance), device_id_type=pl.DeviceIdType.MESH,
        ).wait()
    f32 = jnp.float32
    for which, out_ref in ((0, kg_ref), (1, vg_ref)):
        total = own_s[which] + x_r1[which].astype(f32) + x_l1[which].astype(f32)
        total = total + cb_ref[which + 1].astype(f32)
        low = total[:, :w2] + x_l2[which].astype(f32)
        high = total[:, cc - w2:] + x_r2[which].astype(f32)
        out_ref[:, :w2] = low.astype(jnp.bfloat16)
        out_ref[:, cc - w2:] = high.astype(jnp.bfloat16)
        if cc > 2 * w2:
            out_ref[:, w2:cc - w2] = total[:, w2:cc - w2].astype(jnp.bfloat16)


def fused_row(queries, out_grad, key_grid, value_grid, l2, l1, r1, r2, bias, col_back):
    rows, cc, width = queries.shape
    w2 = l2.shape[2]
    w1 = l1.shape[2]
    vmem = pl.BlockSpec(memory_space=pltpu.VMEM)
    grads = jax.ShapeDtypeStruct((rows, cc, width), jnp.bfloat16)
    bf = jnp.bfloat16
    return pl.pallas_call(
        fused_row_kernel,
        in_specs=[vmem] * 10,
        out_specs=[vmem] * 3,
        out_shape=(grads, grads, grads),
        scratch_shapes=[
            pltpu.VMEM((2, rows, cc, width), jnp.float32),
            pltpu.VMEM((2, rows, w2, width), bf),
            pltpu.VMEM((2, rows, w1, width), bf),
            pltpu.VMEM((2, rows, w1, width), bf),
            pltpu.VMEM((2, rows, w2, width), bf),
            pltpu.VMEM((2, rows, w2, width), bf),
            pltpu.VMEM((2, rows, w1, width), bf),
            pltpu.VMEM((2, rows, w1, width), bf),
            pltpu.VMEM((2, rows, w2, width), bf),
            pltpu.SemaphoreType.DMA((4,)),
            pltpu.SemaphoreType.DMA((4,)),
        ],
        compiler_params=pltpu.CompilerParams(
            collective_id=0, has_side_effects=True, vmem_limit_bytes=60 * 1024 * 1024
        ),
    )(queries, out_grad, key_grid, value_grid, l2, l1, r1, r2, bias, col_back)


def column_kernel(x_ref, o_ref):
    per = x_ref.shape[1]
    rows = x_ref.shape[2]

    def joined(which):
        return jnp.concatenate([x_ref[which, c] for c in range(per)], axis=0)

    i = lax.broadcasted_iota(jnp.int32, (per * rows, per * rows), 0) // rows
    j = lax.broadcasted_iota(jnp.int32, (per * rows, per * rows), 1) // rows
    bias = jnp.where(i == j, 0.0, -jnp.inf).astype(jnp.float32)
    grads = block_grads(joined(0), joined(3), joined(1), joined(2), bias)
    for which, full in enumerate(grads):
        for c in range(per):
            o_ref[which, c] = full[c * rows:(c + 1) * rows].astype(jnp.bfloat16)


def column_attention(whole):
    arrays, strip, rows, width = whole.shape
    per = max(1, LANES // rows)
    return pl.pallas_call(
        column_kernel,
        grid=(strip // per,),
        in_specs=[pl.BlockSpec((arrays, per, rows, width), lambda c: (0, c, 0, 0))],
        out_specs=pl.BlockSpec((3, per, rows, width), lambda c: (0, c, 0, 0)),
        out_shape=jax.ShapeDtypeStruct((3, strip, rows, width), jnp.bfloat16),
    )(whole)


def band_bias(mask_rows, offsets, first_col, grid_cols, block_cols):
    band_reach = HALF + OFFMAX
    query_cols = first_col + jnp.arange(block_cols, dtype=jnp.int32)
    key_cols = first_col - band_reach + jnp.arange(block_cols + 2 * band_reach, dtype=jnp.int32)
    inside = (key_cols >= 0) & (key_cols < grid_cols)
    key_block = jnp.clip(key_cols, 0, grid_cols - 1) // BLK
    block_ids = jnp.arange(mask_rows.shape[1], dtype=jnp.int32)
    key_open = jnp.sum(
        mask_rows[:, None, :]
        * (key_block[None, :, None] == block_ids[None, None, :]).astype(jnp.int32),
        axis=-1,
    )
    relative = key_cols[None, None, :] - query_cols[None, :, None] - offsets[:, None, None]
    same_block = key_cols[None, :] // BLK == query_cols[:, None] // BLK
    allowed = (
        (relative >= -HALF)
        & (relative < HALF)
        & inside[None, None, :]
        & ((key_open[:, None, :] > 0) | same_block[None])
    )
    return jnp.where(allowed, 0.0, -jnp.inf).astype(jnp.float32)


def body(queries, key_grid, value_grid, out_grad, tissue_mask, band_offset):
    row_count, col_count, feature_width = queries.shape
    group_count = lax.axis_size("rrow")
    band_reach = HALF + OFFMAX
    near = col_count
    far = band_reach - col_count

    stacked = jnp.stack([queries, key_grid, value_grid, out_grad]).transpose(0, 2, 1, 3)
    whole = lax.all_to_all(stacked, "rrow", split_axis=1, concat_axis=2, tiled=True)

    pair = jnp.stack([key_grid, value_grid])
    l1 = shifted(pair[:, :, col_count - near:], "rcol", 1)
    r1 = shifted(pair[:, :, :near], "rcol", -1)
    l2 = shifted(l1[:, :, near - far:], "rcol", 1)
    r2 = shifted(r1[:, :, :far], "rcol", -1)
    grid_cols = col_count * lax.axis_size("rcol")
    first_col = lax.axis_index("rcol") * col_count
    bias = band_bias(tissue_mask, band_offset, first_col, grid_cols, col_count)

    col_out = column_attention(whole)
    back = lax.all_to_all(col_out, "rrow", split_axis=2, concat_axis=1, tiled=True)
    back = back.transpose(0, 2, 1, 3)
    return fused_row(queries, out_grad, key_grid, value_grid, l2, l1, r1, r2, bias, back)


def solution(mesh):
    in_specs = (
        P(("slide", "rrow"), "rcol", None),
        P(("slide", "rrow"), "rcol", None),
        P(("slide", "rrow"), "rcol", None),
        P(("slide", "rrow"), "rcol", None),
        P(("slide", "rrow"), None),
        P(("slide", "rrow")),
    )
    out_specs = (
        P(("slide", "rrow"), "rcol", None),
        P(("slide", "rrow"), "rcol", None),
        P(("slide", "rrow"), "rcol", None),
    )
    return jax.shard_map(body, mesh=mesh, in_specs=in_specs, out_specs=out_specs, check_vma=False)
```

```python
import functools
import math

import jax
import jax.numpy as jnp
from jax import lax
from jax.experimental import pallas as pl
from jax.experimental.pallas import tpu as pltpu
from jax.sharding import PartitionSpec as P

HD = 64
BLK = 16
HALF = 32
OFFMAX = 16
SCALE = 1.0 / math.sqrt(HD)
LANES = 128


def shifted(block, axis, distance):
    devices = range(lax.axis_size(axis))
    route = [(i - distance, i) for i in devices if i - distance in devices]
    return lax.ppermute(block, axis, route)


def dot_nt(a, b):
    return lax.dot_general(a, b, (((1,), (1,)), ((), ())), preferred_element_type=jnp.float32)


def dot_tn(a, b):
    return lax.dot_general(a, b, (((0,), (0,)), ((), ())), preferred_element_type=jnp.float32)


def head_stack(x, heads):
    rows, width = x.shape
    lane_head = lax.broadcasted_iota(jnp.int32, (heads, 1, width), 2) // HD
    which = lax.broadcasted_iota(jnp.int32, (heads, 1, width), 0)
    kept = jnp.where(lane_head == which, x[None], jnp.zeros_like(x)[None])
    return kept.reshape(heads * rows, width)


def block_grads(q, g, k, v, bias):
    nq, width = q.shape
    heads = width // HD
    qm = head_stack(q, heads)
    gm = head_stack(g, heads)
    full_bias = jnp.broadcast_to(bias[None], (heads,) + bias.shape).reshape(heads * nq, -1)
    s = dot_nt(qm, k) * SCALE + full_bias
    mx = jnp.max(s, axis=1, keepdims=True)
    e = jnp.exp(s - mx)
    p = e / jnp.sum(e, axis=1, keepdims=True)
    pb = p.astype(jnp.bfloat16)
    gw = dot_nt(gm, v)
    delta = jnp.sum(pb.astype(jnp.float32) * gw, axis=1, keepdims=True)
    ds = (p * (gw - delta)).astype(jnp.bfloat16)
    dk = dot_tn(ds, qm) * SCALE
    dv = dot_tn(pb, gm)
    lane = lax.broadcasted_iota(jnp.int32, (1, LANES), 1)
    low = lane < HD
    tiles = []
    for pair in range(width // LANES):
        both = jnp.dot(
            ds[2 * pair * nq:(2 * pair + 2) * nq],
            k[:, pair * LANES:(pair + 1) * LANES],
            preferred_element_type=jnp.float32,
        )
        tiles.append(jnp.where(low, both[:nq], both[nq:]) * SCALE)
    dq = jnp.concatenate(tiles, axis=1)
    return dq, dk, dv


def fused_row_kernel(q_ref, g_ref, k_ref, v_ref, l2_ref, l1_ref, r1_ref, r2_ref, bias_ref,
                     qg_ref, kg_ref, vg_ref,
                     own_s, s_l2, s_l1, s_r1, s_r2, x_r2, x_r1, x_l1, x_l2, send_sem, recv_sem):
    rows, cc, width = q_ref.shape
    w2 = l2_ref.shape[2]
    w1 = l1_ref.shape[2]
    n = lax.axis_size("rcol")
    me = lax.axis_index("rcol")
    here = (lax.axis_index("slide"), lax.axis_index("rrow"))

    def dev(distance):
        return here + (lax.rem(me + distance + n, n),)

    barrier = pltpu.get_barrier_semaphore()
    for distance in (-2, -1, 1, 2):
        pl.semaphore_signal(barrier, 1, device_id=dev(distance), device_id_type=pl.DeviceIdType.MESH)
    pl.semaphore_wait(barrier, 4)

    routes = ((s_l2, x_r2, -2), (s_l1, x_r1, -1), (s_r1, x_l1, 1), (s_r2, x_l2, 2))

    def row_step(r, carry):
        def span(which, own_ref):
            return jnp.concatenate(
                [l2_ref[which, r], l1_ref[which, r], own_ref[r], r1_ref[which, r],
                 r2_ref[which, r]],
                axis=0,
            )

        dq, dk, dv = block_grads(q_ref[r], g_ref[r], span(0, k_ref), span(1, v_ref), bias_ref[r])
        qg_ref[r] = dq
        for which, full in ((0, dk), (1, dv)):
            s_l2[which, r] = full[:w2].astype(jnp.bfloat16)
            s_l1[which, r] = full[w2:w2 + w1].astype(jnp.bfloat16)
            own_s[which, r] = full[w2 + w1:w2 + w1 + cc]
            s_r1[which, r] = full[w2 + w1 + cc:w2 + 2 * w1 + cc].astype(jnp.bfloat16)
            s_r2[which, r] = full[w2 + 2 * w1 + cc:].astype(jnp.bfloat16)
        for slot, (src, dst, distance) in enumerate(routes):
            pltpu.make_async_remote_copy(
                src_ref=src.at[:, pl.ds(r, 1)],
                dst_ref=dst.at[:, pl.ds(r, 1)],
                send_sem=send_sem.at[slot],
                recv_sem=recv_sem.at[slot],
                device_id=dev(distance),
                device_id_type=pl.DeviceIdType.MESH,
            ).start()
        return carry

    lax.fori_loop(0, rows, row_step, 0)
    for slot, (src, dst, distance) in enumerate(routes):
        pltpu.make_async_remote_copy(
            src_ref=src, dst_ref=dst, send_sem=send_sem.at[slot], recv_sem=recv_sem.at[slot],
            device_id=dev(distance), device_id_type=pl.DeviceIdType.MESH,
        ).wait()
    f32 = jnp.float32
    for which, out_ref in ((0, kg_ref), (1, vg_ref)):
        total = own_s[which] + x_r1[which].astype(f32) + x_l1[which].astype(f32)
        low = total[:, :w2] + x_l2[which].astype(f32)
        high = total[:, cc - w2:] + x_r2[which].astype(f32)
        out_ref[:, :w2] = low
        out_ref[:, cc - w2:] = high
        if cc > 2 * w2:
            out_ref[:, w2:cc - w2] = total[:, w2:cc - w2]


def fused_row(queries, out_grad, key_grid, value_grid, l2, l1, r1, r2, bias):
    rows, cc, width = queries.shape
    w2 = l2.shape[2]
    w1 = l1.shape[2]
    vmem = pl.BlockSpec(memory_space=pltpu.VMEM)
    grads = jax.ShapeDtypeStruct((rows, cc, width), jnp.float32)
    bf = jnp.bfloat16
    return pl.pallas_call(
        fused_row_kernel,
        in_specs=[vmem] * 9,
        out_specs=[vmem] * 3,
        out_shape=(grads, grads, grads),
        scratch_shapes=[
            pltpu.VMEM((2, rows, cc, width), jnp.float32),
            pltpu.VMEM((2, rows, w2, width), bf),
            pltpu.VMEM((2, rows, w1, width), bf),
            pltpu.VMEM((2, rows, w1, width), bf),
            pltpu.VMEM((2, rows, w2, width), bf),
            pltpu.VMEM((2, rows, w2, width), bf),
            pltpu.VMEM((2, rows, w1, width), bf),
            pltpu.VMEM((2, rows, w1, width), bf),
            pltpu.VMEM((2, rows, w2, width), bf),
            pltpu.SemaphoreType.DMA((4,)),
            pltpu.SemaphoreType.DMA((4,)),
        ],
        compiler_params=pltpu.CompilerParams(
            collective_id=0, has_side_effects=True, vmem_limit_bytes=60 * 1024 * 1024
        ),
    )(queries, out_grad, key_grid, value_grid, l2, l1, r1, r2, bias)


def column_kernel(x_ref, o_ref):
    per = x_ref.shape[1]
    rows = x_ref.shape[2]

    def joined(which):
        return jnp.concatenate([x_ref[which, c] for c in range(per)], axis=0)

    i = lax.broadcasted_iota(jnp.int32, (per * rows, per * rows), 0) // rows
    j = lax.broadcasted_iota(jnp.int32, (per * rows, per * rows), 1) // rows
    bias = jnp.where(i == j, 0.0, -jnp.inf).astype(jnp.float32)
    grads = block_grads(joined(0), joined(3), joined(1), joined(2), bias)
    for which, full in enumerate(grads):
        for c in range(per):
            o_ref[which, c] = full[c * rows:(c + 1) * rows].astype(jnp.bfloat16)


def column_attention(whole):
    arrays, strip, rows, width = whole.shape
    per = max(1, LANES // rows)
    return pl.pallas_call(
        column_kernel,
        grid=(strip // per,),
        in_specs=[pl.BlockSpec((arrays, per, rows, width), lambda c: (0, c, 0, 0))],
        out_specs=pl.BlockSpec((3, per, rows, width), lambda c: (0, c, 0, 0)),
        out_shape=jax.ShapeDtypeStruct((3, strip, rows, width), jnp.bfloat16),
    )(whole)


def band_bias(mask_rows, offsets, first_col, grid_cols, block_cols):
    band_reach = HALF + OFFMAX
    query_cols = first_col + jnp.arange(block_cols, dtype=jnp.int32)
    key_cols = first_col - band_reach + jnp.arange(block_cols + 2 * band_reach, dtype=jnp.int32)
    inside = (key_cols >= 0) & (key_cols < grid_cols)
    key_block = jnp.clip(key_cols, 0, grid_cols - 1) // BLK
    block_ids = jnp.arange(mask_rows.shape[1], dtype=jnp.int32)
    key_open = jnp.sum(
        mask_rows[:, None, :]
        * (key_block[None, :, None] == block_ids[None, None, :]).astype(jnp.int32),
        axis=-1,
    )
    relative = key_cols[None, None, :] - query_cols[None, :, None] - offsets[:, None, None]
    same_block = key_cols[None, :] // BLK == query_cols[:, None] // BLK
    allowed = (
        (relative >= -HALF)
        & (relative < HALF)
        & inside[None, None, :]
        & ((key_open[:, None, :] > 0) | same_block[None])
    )
    return jnp.where(allowed, 0.0, -jnp.inf).astype(jnp.float32)


def body(queries, key_grid, value_grid, out_grad, tissue_mask, band_offset):
    row_count, col_count, feature_width = queries.shape
    group_count = lax.axis_size("rrow")
    band_reach = HALF + OFFMAX
    near = col_count
    far = band_reach - col_count

    stacked = jnp.stack([queries, key_grid, value_grid, out_grad]).transpose(0, 2, 1, 3)
    whole = lax.all_to_all(stacked, "rrow", split_axis=1, concat_axis=2, tiled=True)

    pair = jnp.stack([key_grid, value_grid])
    l1 = shifted(pair[:, :, col_count - near:], "rcol", 1)
    r1 = shifted(pair[:, :, :near], "rcol", -1)
    l2 = shifted(l1[:, :, near - far:], "rcol", 1)
    r2 = shifted(r1[:, :, :far], "rcol", -1)
    grid_cols = col_count * lax.axis_size("rcol")
    first_col = lax.axis_index("rcol") * col_count
    bias = band_bias(tissue_mask, band_offset, first_col, grid_cols, col_count)

    col_out = column_attention(whole)
    back = lax.all_to_all(col_out, "rrow", split_axis=2, concat_axis=1, tiled=True)
    row_grads = fused_row(queries, out_grad, key_grid, value_grid, l2, l1, r1, r2, bias)
    back = back.transpose(0, 2, 1, 3).astype(jnp.float32)
    return tuple((row + col).astype(jnp.bfloat16) for row, col in zip(row_grads, back))


def solution(mesh):
    in_specs = (
        P(("slide", "rrow"), "rcol", None),
        P(("slide", "rrow"), "rcol", None),
        P(("slide", "rrow"), "rcol", None),
        P(("slide", "rrow"), "rcol", None),
        P(("slide", "rrow"), None),
        P(("slide", "rrow")),
    )
    out_specs = (
        P(("slide", "rrow"), "rcol", None),
        P(("slide", "rrow"), "rcol", None),
        P(("slide", "rrow"), "rcol", None),
    )
    return jax.shard_map(body, mesh=mesh, in_specs=in_specs, out_specs=out_specs, check_vma=False)
```

```python
import functools
import math

import jax
import jax.numpy as jnp
from jax import lax
from jax.experimental import pallas as pl
from jax.experimental.pallas import tpu as pltpu
from jax.sharding import PartitionSpec as P

HD = 64
BLK = 16
HALF = 32
OFFMAX = 16
SCALE = 1.0 / math.sqrt(HD)
LANES = 128


def shifted(block, axis, distance):
    devices = range(lax.axis_size(axis))
    route = [(i - distance, i) for i in devices if i - distance in devices]
    return lax.ppermute(block, axis, route)


def dot_nt(a, b):
    return lax.dot_general(a, b, (((1,), (1,)), ((), ())), preferred_element_type=jnp.float32)


def dot_tn(a, b):
    return lax.dot_general(a, b, (((0,), (0,)), ((), ())), preferred_element_type=jnp.float32)


def head_stack(x, heads):
    rows, width = x.shape
    lane_head = lax.broadcasted_iota(jnp.int32, (heads, 1, width), 2) // HD
    which = lax.broadcasted_iota(jnp.int32, (heads, 1, width), 0)
    kept = jnp.where(lane_head == which, x[None], jnp.zeros_like(x)[None])
    return kept.reshape(heads * rows, width)


def block_grads(q, g, k, v, bias):
    nq, width = q.shape
    heads = width // HD
    qm = head_stack(q, heads)
    gm = head_stack(g, heads)
    full_bias = jnp.broadcast_to(bias[None], (heads,) + bias.shape).reshape(heads * nq, -1)
    s = dot_nt(qm, k) * SCALE + full_bias
    mx = jnp.max(s, axis=1, keepdims=True)
    e = jnp.exp(s - mx)
    p = e / jnp.sum(e, axis=1, keepdims=True)
    pb = p.astype(jnp.bfloat16)
    gw = dot_nt(gm, v)
    delta = jnp.sum(pb.astype(jnp.float32) * gw, axis=1, keepdims=True)
    ds = (p * (gw - delta)).astype(jnp.bfloat16)
    dk = dot_tn(ds, qm) * SCALE
    dv = dot_tn(pb, gm)
    lane = lax.broadcasted_iota(jnp.int32, (1, LANES), 1)
    low = lane < HD
    tiles = []
    for pair in range(width // LANES):
        both = jnp.dot(
            ds[2 * pair * nq:(2 * pair + 2) * nq],
            k[:, pair * LANES:(pair + 1) * LANES],
            preferred_element_type=jnp.float32,
        )
        tiles.append(jnp.where(low, both[:nq], both[nq:]) * SCALE)
    dq = jnp.concatenate(tiles, axis=1)
    return dq, dk, dv


def fused_row_kernel(q_ref, g_ref, k_ref, v_ref, l2_ref, l1_ref, r1_ref, r2_ref, bias_ref,
                     qg_ref, kg_ref, vg_ref,
                     own_s, near_l, near_r, s_fl, s_fr, s_nl, s_nr, x_fr, x_fl, x_nr, x_nl,
                     far_send, far_recv_r, far_recv_l, near_send, near_recv):
    rows, cc, width = q_ref.shape
    w2 = l2_ref.shape[2]
    w1 = l1_ref.shape[2]
    n = lax.axis_size("rcol")
    me = lax.axis_index("rcol")
    here = (lax.axis_index("slide"), lax.axis_index("rrow"))
    mesh_ids = pl.DeviceIdType.MESH

    def dev(distance):
        return here + (lax.rem(me + distance + n, n),)

    barrier = pltpu.get_barrier_semaphore()
    for distance in (-1, 1):
        pl.semaphore_signal(barrier, 1, device_id=dev(distance), device_id_type=mesh_ids)
    pl.semaphore_wait(barrier, 2)

    def far_copy(r, to_left):
        if to_left:
            return pltpu.make_async_remote_copy(
                src_ref=s_fl.at[:, pl.ds(r, 1)], dst_ref=x_fr.at[:, pl.ds(r, 1)],
                send_sem=far_send.at[0], recv_sem=far_recv_r.at[r],
                device_id=dev(-1), device_id_type=mesh_ids)
        return pltpu.make_async_remote_copy(
            src_ref=s_fr.at[:, pl.ds(r, 1)], dst_ref=x_fl.at[:, pl.ds(r, 1)],
            send_sem=far_send.at[1], recv_sem=far_recv_l.at[r],
            device_id=dev(1), device_id_type=mesh_ids)

    def near_copy(r, to_left, whole=False):
        rs = slice(None) if whole else pl.ds(r, 1)
        if to_left:
            return pltpu.make_async_remote_copy(
                src_ref=s_nl.at[:, rs], dst_ref=x_nr.at[:, rs],
                send_sem=near_send.at[0], recv_sem=near_recv.at[0],
                device_id=dev(-1), device_id_type=mesh_ids)
        return pltpu.make_async_remote_copy(
            src_ref=s_nr.at[:, rs], dst_ref=x_nl.at[:, rs],
            send_sem=near_send.at[1], recv_sem=near_recv.at[1],
            device_id=dev(1), device_id_type=mesh_ids)

    def send_near(r):
        far_copy(r, True).wait_recv()
        far_copy(r, False).wait_recv()
        f32 = jnp.float32
        s_nl[:, r, :w1 - w2] = near_l[:, r, :w1 - w2].astype(jnp.bfloat16)
        s_nl[:, r, w1 - w2:] = (near_l[:, r, w1 - w2:] + x_fr[:, r].astype(f32)).astype(jnp.bfloat16)
        s_nr[:, r, :w2] = (near_r[:, r, :w2] + x_fl[:, r].astype(f32)).astype(jnp.bfloat16)
        s_nr[:, r, w2:] = near_r[:, r, w2:].astype(jnp.bfloat16)
        near_copy(r, True).start()
        near_copy(r, False).start()

    def row_step(r, carry):
        def span(which, own_ref):
            return jnp.concatenate(
                [l2_ref[which, r], l1_ref[which, r], own_ref[r], r1_ref[which, r],
                 r2_ref[which, r]],
                axis=0,
            )

        dq, dk, dv = block_grads(q_ref[r], g_ref[r], span(0, k_ref), span(1, v_ref), bias_ref[r])
        qg_ref[r] = dq
        for which, full in ((0, dk), (1, dv)):
            s_fl[which, r] = full[:w2].astype(jnp.bfloat16)
            near_l[which, r] = full[w2:w2 + w1]
            own_s[which, r] = full[w2 + w1:w2 + w1 + cc]
            near_r[which, r] = full[w2 + w1 + cc:w2 + 2 * w1 + cc]
            s_fr[which, r] = full[w2 + 2 * w1 + cc:].astype(jnp.bfloat16)
        far_copy(r, True).start()
        far_copy(r, False).start()

        @pl.when(r > 0)
        def _():
            send_near(r - 1)

        return carry

    lax.fori_loop(0, rows, row_step, 0)
    send_near(rows - 1)
    for src, dst, slot in ((s_fl, x_fr, 0), (s_fr, x_fl, 1)):
        pltpu.make_async_remote_copy(
            src_ref=src, dst_ref=dst, send_sem=far_send.at[slot], recv_sem=far_recv_r.at[0],
            device_id=dev(1 - 2 * (1 - slot)), device_id_type=mesh_ids).wait_send()
    for to_left in (True, False):
        near_copy(0, to_left, whole=True).wait()
    f32 = jnp.float32
    for which, out_ref in ((0, kg_ref), (1, vg_ref)):
        out_ref[...] = own_s[which] + x_nr[which].astype(f32) + x_nl[which].astype(f32)


def fused_row(queries, out_grad, key_grid, value_grid, l2, l1, r1, r2, bias):
    rows, cc, width = queries.shape
    w2 = l2.shape[2]
    w1 = l1.shape[2]
    vmem = pl.BlockSpec(memory_space=pltpu.VMEM)
    grads = jax.ShapeDtypeStruct((rows, cc, width), jnp.float32)
    bf = jnp.bfloat16
    f32 = jnp.float32
    return pl.pallas_call(
        fused_row_kernel,
        in_specs=[vmem] * 9,
        out_specs=[vmem] * 3,
        out_shape=(grads, grads, grads),
        scratch_shapes=[
            pltpu.VMEM((2, rows, cc, width), f32),
            pltpu.VMEM((2, rows, w1, width), f32),
            pltpu.VMEM((2, rows, w1, width), f32),
            pltpu.VMEM((2, rows, w2, width), bf),
            pltpu.VMEM((2, rows, w2, width), bf),
            pltpu.VMEM((2, rows, w1, width), bf),
            pltpu.VMEM((2, rows, w1, width), bf),
            pltpu.VMEM((2, rows, w2, width), bf),
            pltpu.VMEM((2, rows, w2, width), bf),
            pltpu.VMEM((2, rows, cc, width), bf),
            pltpu.VMEM((2, rows, cc, width), bf),
            pltpu.SemaphoreType.DMA((2,)),
            pltpu.SemaphoreType.DMA((rows,)),
            pltpu.SemaphoreType.DMA((rows,)),
            pltpu.SemaphoreType.DMA((2,)),
            pltpu.SemaphoreType.DMA((2,)),
        ],
        compiler_params=pltpu.CompilerParams(
            collective_id=0, has_side_effects=True, vmem_limit_bytes=60 * 1024 * 1024
        ),
    )(queries, out_grad, key_grid, value_grid, l2, l1, r1, r2, bias)


def column_kernel(x_ref, o_ref):
    per = x_ref.shape[1]
    rows = x_ref.shape[2]

    def joined(which):
        return jnp.concatenate([x_ref[which, c] for c in range(per)], axis=0)

    i = lax.broadcasted_iota(jnp.int32, (per * rows, per * rows), 0) // rows
    j = lax.broadcasted_iota(jnp.int32, (per * rows, per * rows), 1) // rows
    bias = jnp.where(i == j, 0.0, -jnp.inf).astype(jnp.float32)
    grads = block_grads(joined(0), joined(3), joined(1), joined(2), bias)
    for which, full in enumerate(grads):
        for c in range(per):
            o_ref[which, c] = full[c * rows:(c + 1) * rows].astype(jnp.bfloat16)


def column_attention(whole):
    arrays, strip, rows, width = whole.shape
    per = max(1, LANES // rows)
    return pl.pallas_call(
        column_kernel,
        grid=(strip // per,),
        in_specs=[pl.BlockSpec((arrays, per, rows, width), lambda c: (0, c, 0, 0))],
        out_specs=pl.BlockSpec((3, per, rows, width), lambda c: (0, c, 0, 0)),
        out_shape=jax.ShapeDtypeStruct((3, strip, rows, width), jnp.bfloat16),
    )(whole)


def band_bias(mask_rows, offsets, first_col, grid_cols, block_cols):
    band_reach = HALF + OFFMAX
    query_cols = first_col + jnp.arange(block_cols, dtype=jnp.int32)
    key_cols = first_col - band_reach + jnp.arange(block_cols + 2 * band_reach, dtype=jnp.int32)
    inside = (key_cols >= 0) & (key_cols < grid_cols)
    key_block = jnp.clip(key_cols, 0, grid_cols - 1) // BLK
    block_ids = jnp.arange(mask_rows.shape[1], dtype=jnp.int32)
    key_open = jnp.sum(
        mask_rows[:, None, :]
        * (key_block[None, :, None] == block_ids[None, None, :]).astype(jnp.int32),
        axis=-1,
    )
    relative = key_cols[None, None, :] - query_cols[None, :, None] - offsets[:, None, None]
    same_block = key_cols[None, :] // BLK == query_cols[:, None] // BLK
    allowed = (
        (relative >= -HALF)
        & (relative < HALF)
        & inside[None, None, :]
        & ((key_open[:, None, :] > 0) | same_block[None])
    )
    return jnp.where(allowed, 0.0, -jnp.inf).astype(jnp.float32)


def body(queries, key_grid, value_grid, out_grad, tissue_mask, band_offset):
    row_count, col_count, feature_width = queries.shape
    group_count = lax.axis_size("rrow")
    band_reach = HALF + OFFMAX
    near = col_count
    far = band_reach - col_count

    stacked = jnp.stack([queries, key_grid, value_grid, out_grad]).transpose(0, 2, 1, 3)
    whole = lax.all_to_all(stacked, "rrow", split_axis=1, concat_axis=2, tiled=True)

    pair = jnp.stack([key_grid, value_grid])
    l1 = shifted(pair[:, :, col_count - near:], "rcol", 1)
    r1 = shifted(pair[:, :, :near], "rcol", -1)
    l2 = shifted(l1[:, :, near - far:], "rcol", 1)
    r2 = shifted(r1[:, :, :far], "rcol", -1)
    grid_cols = col_count * lax.axis_size("rcol")
    first_col = lax.axis_index("rcol") * col_count
    bias = band_bias(tissue_mask, band_offset, first_col, grid_cols, col_count)

    col_out = column_attention(whole)
    back = lax.all_to_all(col_out, "rrow", split_axis=2, concat_axis=1, tiled=True)
    row_grads = fused_row(queries, out_grad, key_grid, value_grid, l2, l1, r1, r2, bias)
    back = back.transpose(0, 2, 1, 3).astype(jnp.float32)
    return tuple((row + col).astype(jnp.bfloat16) for row, col in zip(row_grads, back))


def solution(mesh):
    in_specs = (
        P(("slide", "rrow"), "rcol", None),
        P(("slide", "rrow"), "rcol", None),
        P(("slide", "rrow"), "rcol", None),
        P(("slide", "rrow"), "rcol", None),
        P(("slide", "rrow"), None),
        P(("slide", "rrow")),
    )
    out_specs = (
        P(("slide", "rrow"), "rcol", None),
        P(("slide", "rrow"), "rcol", None),
        P(("slide", "rrow"), "rcol", None),
    )
    return jax.shard_map(body, mesh=mesh, in_specs=in_specs, out_specs=out_specs, check_vma=False)
```

```python
import functools
import math

import jax
import jax.numpy as jnp
from jax import lax
from jax.experimental import pallas as pl
from jax.experimental.pallas import tpu as pltpu
from jax.sharding import PartitionSpec as P

HD = 64
BLK = 16
HALF = 32
OFFMAX = 16
SCALE = 1.0 / math.sqrt(HD)
LANES = 128


def shifted(block, axis, distance):
    devices = range(lax.axis_size(axis))
    route = [(i - distance, i) for i in devices if i - distance in devices]
    return lax.ppermute(block, axis, route)


def dot_nt(a, b):
    return lax.dot_general(a, b, (((1,), (1,)), ((), ())), preferred_element_type=jnp.float32)


def dot_tn(a, b):
    return lax.dot_general(a, b, (((0,), (0,)), ((), ())), preferred_element_type=jnp.float32)


def head_stack(x, heads):
    rows, width = x.shape
    lane_head = lax.broadcasted_iota(jnp.int32, (heads, 1, width), 2) // HD
    which = lax.broadcasted_iota(jnp.int32, (heads, 1, width), 0)
    kept = jnp.where(lane_head == which, x[None], jnp.zeros_like(x)[None])
    return kept.reshape(heads * rows, width)


def block_grads(q, g, k, v, bias):
    nq, width = q.shape
    heads = width // HD
    qm = head_stack(q, heads)
    gm = head_stack(g, heads)
    full_bias = jnp.broadcast_to(bias[None], (heads,) + bias.shape).reshape(heads * nq, -1)
    s = dot_nt(qm, k) * SCALE + full_bias
    mx = jnp.max(s, axis=1, keepdims=True)
    e = jnp.exp(s - mx)
    p = e / jnp.sum(e, axis=1, keepdims=True)
    pb = p.astype(jnp.bfloat16)
    gw = dot_nt(gm, v)
    delta = jnp.sum(pb.astype(jnp.float32) * gw, axis=1, keepdims=True)
    ds = (p * (gw - delta)).astype(jnp.bfloat16)
    dk = dot_tn(ds, qm) * SCALE
    dv = dot_tn(pb, gm)
    lane = lax.broadcasted_iota(jnp.int32, (1, LANES), 1)
    low = lane < HD
    tiles = []
    for pair in range(width // LANES):
        both = jnp.dot(
            ds[2 * pair * nq:(2 * pair + 2) * nq],
            k[:, pair * LANES:(pair + 1) * LANES],
            preferred_element_type=jnp.float32,
        )
        tiles.append(jnp.where(low, both[:nq], both[nq:]) * SCALE)
    dq = jnp.concatenate(tiles, axis=1)
    return dq, dk, dv


def fused_row_kernel(q_ref, g_ref, k_ref, v_ref, l2_ref, l1_ref, r1_ref, r2_ref, bias_ref,
                     qg_ref, kg_ref, vg_ref,
                     own_s, near_l, near_r, s_fl, s_fr, s_nl, s_nr, x_fr, x_fl, x_nr, x_nl,
                     far_send, far_recv_r, far_recv_l, near_send, near_recv):
    rows, cc, width = q_ref.shape
    w2 = l2_ref.shape[2]
    w1 = l1_ref.shape[2]
    n = lax.axis_size("rcol")
    me = lax.axis_index("rcol")
    here = (lax.axis_index("slide"), lax.axis_index("rrow"))
    mesh_ids = pl.DeviceIdType.MESH

    def dev(distance):
        return here + (lax.rem(me + distance + n, n),)

    barrier = pltpu.get_barrier_semaphore()
    for distance in (-1, 1):
        pl.semaphore_signal(barrier, 1, device_id=dev(distance), device_id_type=mesh_ids)
    pl.semaphore_wait(barrier, 2)

    def far_copy(r, to_left):
        if to_left:
            return pltpu.make_async_remote_copy(
                src_ref=s_fl.at[:, pl.ds(r, 1)], dst_ref=x_fr.at[:, pl.ds(r, 1)],
                send_sem=far_send.at[0], recv_sem=far_recv_r.at[r],
                device_id=dev(-1), device_id_type=mesh_ids)
        return pltpu.make_async_remote_copy(
            src_ref=s_fr.at[:, pl.ds(r, 1)], dst_ref=x_fl.at[:, pl.ds(r, 1)],
            send_sem=far_send.at[1], recv_sem=far_recv_l.at[r],
            device_id=dev(1), device_id_type=mesh_ids)

    def near_copy(r, to_left, whole=False):
        rs = slice(None) if whole else pl.ds(r, 1)
        if to_left:
            return pltpu.make_async_remote_copy(
                src_ref=s_nl.at[:, rs], dst_ref=x_nr.at[:, rs],
                send_sem=near_send.at[0], recv_sem=near_recv.at[0],
                device_id=dev(-1), device_id_type=mesh_ids)
        return pltpu.make_async_remote_copy(
            src_ref=s_nr.at[:, rs], dst_ref=x_nl.at[:, rs],
            send_sem=near_send.at[1], recv_sem=near_recv.at[1],
            device_id=dev(1), device_id_type=mesh_ids)

    def send_near(r):
        far_copy(r, True).wait_recv()
        far_copy(r, False).wait_recv()
        f32 = jnp.float32
        s_nl[:, r, :w1 - w2] = near_l[:, r, :w1 - w2].astype(jnp.bfloat16)
        s_nl[:, r, w1 - w2:] = (near_l[:, r, w1 - w2:] + x_fr[:, r].astype(f32)).astype(jnp.bfloat16)
        s_nr[:, r, :w2] = (near_r[:, r, :w2] + x_fl[:, r].astype(f32)).astype(jnp.bfloat16)
        s_nr[:, r, w2:] = near_r[:, r, w2:].astype(jnp.bfloat16)
        near_copy(r, True).start()
        near_copy(r, False).start()

    def row_step(r, carry):
        def span(which, own_ref):
            return jnp.concatenate(
                [l2_ref[which, r], l1_ref[which, r], own_ref[r], r1_ref[which, r],
                 r2_ref[which, r]],
                axis=0,
            )

        dq, dk, dv = block_grads(q_ref[r], g_ref[r], span(0, k_ref), span(1, v_ref), bias_ref[r])
        qg_ref[r] = dq
        for which, full in ((0, dk), (1, dv)):
            s_fl[which, r] = full[:w2].astype(jnp.bfloat16)
            near_l[which, r] = full[w2:w2 + w1]
            own_s[which, r] = full[w2 + w1:w2 + w1 + cc]
            near_r[which, r] = full[w2 + w1 + cc:w2 + 2 * w1 + cc]
            s_fr[which, r] = full[w2 + 2 * w1 + cc:].astype(jnp.bfloat16)
        far_copy(r, True).start()
        far_copy(r, False).start()

        @pl.when(r > 0)
        def _():
            send_near(r - 1)

        return carry

    lax.fori_loop(0, rows, row_step, 0)
    send_near(rows - 1)
    for src, dst, slot in ((s_fl, x_fr, 0), (s_fr, x_fl, 1)):
        pltpu.make_async_remote_copy(
            src_ref=src, dst_ref=dst, send_sem=far_send.at[slot], recv_sem=far_recv_r.at[0],
            device_id=dev(1 - 2 * (1 - slot)), device_id_type=mesh_ids).wait_send()
    for to_left in (True, False):
        near_copy(0, to_left, whole=True).wait()
    f32 = jnp.float32
    for which, out_ref in ((0, kg_ref), (1, vg_ref)):
        out_ref[...] = own_s[which] + x_nr[which].astype(f32) + x_nl[which].astype(f32)


def fused_row(queries, out_grad, key_grid, value_grid, l2, l1, r1, r2, bias):
    rows, cc, width = queries.shape
    w2 = l2.shape[2]
    w1 = l1.shape[2]
    vmem = pl.BlockSpec(memory_space=pltpu.VMEM)
    grads = jax.ShapeDtypeStruct((rows, cc, width), jnp.float32)
    bf = jnp.bfloat16
    f32 = jnp.float32
    return pl.pallas_call(
        fused_row_kernel,
        in_specs=[vmem] * 9,
        out_specs=[vmem] * 3,
        out_shape=(grads, grads, grads),
        scratch_shapes=[
            pltpu.VMEM((2, rows, cc, width), f32),
            pltpu.VMEM((2, rows, w1, width), f32),
            pltpu.VMEM((2, rows, w1, width), f32),
            pltpu.VMEM((2, rows, w2, width), bf),
            pltpu.VMEM((2, rows, w2, width), bf),
            pltpu.VMEM((2, rows, w1, width), bf),
            pltpu.VMEM((2, rows, w1, width), bf),
            pltpu.VMEM((2, rows, w2, width), bf),
            pltpu.VMEM((2, rows, w2, width), bf),
            pltpu.VMEM((2, rows, cc, width), bf),
            pltpu.VMEM((2, rows, cc, width), bf),
            pltpu.SemaphoreType.DMA((2,)),
            pltpu.SemaphoreType.DMA((rows,)),
            pltpu.SemaphoreType.DMA((rows,)),
            pltpu.SemaphoreType.DMA((2,)),
            pltpu.SemaphoreType.DMA((2,)),
        ],
        compiler_params=pltpu.CompilerParams(
            collective_id=0, has_side_effects=True, vmem_limit_bytes=60 * 1024 * 1024
        ),
    )(queries, out_grad, key_grid, value_grid, l2, l1, r1, r2, bias)


def column_kernel(x_ref, order_ref, o_ref):
    per = x_ref.shape[1]
    rows = x_ref.shape[2]

    def joined(which):
        return jnp.concatenate([x_ref[which, c] for c in range(per)], axis=0)

    i = lax.broadcasted_iota(jnp.int32, (per * rows, per * rows), 0) // rows
    j = lax.broadcasted_iota(jnp.int32, (per * rows, per * rows), 1) // rows
    bias = jnp.where(i == j, 0.0, -jnp.inf).astype(jnp.float32)
    grads = block_grads(joined(0), joined(3), joined(1), joined(2), bias)
    for which, full in enumerate(grads):
        for c in range(per):
            o_ref[which, c] = full[c * rows:(c + 1) * rows].astype(jnp.bfloat16)


def column_attention(whole, order):
    arrays, strip, rows, width = whole.shape
    per = max(1, LANES // rows)
    return pl.pallas_call(
        column_kernel,
        grid=(strip // per,),
        in_specs=[
            pl.BlockSpec((arrays, per, rows, width), lambda c: (0, c, 0, 0)),
            pl.BlockSpec(memory_space=pltpu.VMEM),
        ],
        out_specs=pl.BlockSpec((3, per, rows, width), lambda c: (0, c, 0, 0)),
        out_shape=jax.ShapeDtypeStruct((3, strip, rows, width), jnp.bfloat16),
    )(whole, order)


def band_bias(mask_rows, offsets, first_col, grid_cols, block_cols):
    band_reach = HALF + OFFMAX
    query_cols = first_col + jnp.arange(block_cols, dtype=jnp.int32)
    key_cols = first_col - band_reach + jnp.arange(block_cols + 2 * band_reach, dtype=jnp.int32)
    inside = (key_cols >= 0) & (key_cols < grid_cols)
    key_block = jnp.clip(key_cols, 0, grid_cols - 1) // BLK
    block_ids = jnp.arange(mask_rows.shape[1], dtype=jnp.int32)
    key_open = jnp.sum(
        mask_rows[:, None, :]
        * (key_block[None, :, None] == block_ids[None, None, :]).astype(jnp.int32),
        axis=-1,
    )
    relative = key_cols[None, None, :] - query_cols[None, :, None] - offsets[:, None, None]
    same_block = key_cols[None, :] // BLK == query_cols[:, None] // BLK
    allowed = (
        (relative >= -HALF)
        & (relative < HALF)
        & inside[None, None, :]
        & ((key_open[:, None, :] > 0) | same_block[None])
    )
    return jnp.where(allowed, 0.0, -jnp.inf).astype(jnp.float32)


def body(queries, key_grid, value_grid, out_grad, tissue_mask, band_offset):
    row_count, col_count, feature_width = queries.shape
    group_count = lax.axis_size("rrow")
    band_reach = HALF + OFFMAX
    near = col_count
    far = band_reach - col_count

    stacked = jnp.stack([queries, key_grid, value_grid, out_grad]).transpose(0, 2, 1, 3)
    whole = lax.all_to_all(stacked, "rrow", split_axis=1, concat_axis=2, tiled=True)

    pair = jnp.stack([key_grid, value_grid])
    l1 = shifted(pair[:, :, col_count - near:], "rcol", 1)
    r1 = shifted(pair[:, :, :near], "rcol", -1)
    l2 = shifted(l1[:, :, near - far:], "rcol", 1)
    r2 = shifted(r1[:, :, :far], "rcol", -1)
    grid_cols = col_count * lax.axis_size("rcol")
    first_col = lax.axis_index("rcol") * col_count
    bias = band_bias(tissue_mask, band_offset, first_col, grid_cols, col_count)

    order = jnp.concatenate([l2[0, 0, :8, :LANES], r2[0, 0, :8, :LANES]], axis=0)
    col_out = column_attention(whole, order)
    back = lax.all_to_all(col_out, "rrow", split_axis=2, concat_axis=1, tiled=True)
    row_grads = fused_row(queries, out_grad, key_grid, value_grid, l2, l1, r1, r2, bias)
    back = back.transpose(0, 2, 1, 3).astype(jnp.float32)
    return tuple((row + col).astype(jnp.bfloat16) for row, col in zip(row_grads, back))


def solution(mesh):
    in_specs = (
        P(("slide", "rrow"), "rcol", None),
        P(("slide", "rrow"), "rcol", None),
        P(("slide", "rrow"), "rcol", None),
        P(("slide", "rrow"), "rcol", None),
        P(("slide", "rrow"), None),
        P(("slide", "rrow")),
    )
    out_specs = (
        P(("slide", "rrow"), "rcol", None),
        P(("slide", "rrow"), "rcol", None),
        P(("slide", "rrow"), "rcol", None),
    )
    return jax.shard_map(body, mesh=mesh, in_specs=in_specs, out_specs=out_specs, check_vma=False)
```

```python
import functools
import math

import jax
import jax.numpy as jnp
from jax import lax
from jax.experimental import pallas as pl
from jax.experimental.pallas import tpu as pltpu
from jax.sharding import PartitionSpec as P

HD = 64
BLK = 16
HALF = 32
OFFMAX = 16
SCALE = 1.0 / math.sqrt(HD)
LANES = 128


def shifted(block, axis, distance):
    devices = range(lax.axis_size(axis))
    route = [(i - distance, i) for i in devices if i - distance in devices]
    return lax.ppermute(block, axis, route)


def dot_nt(a, b):
    return lax.dot_general(a, b, (((1,), (1,)), ((), ())), preferred_element_type=jnp.float32)


def dot_tn(a, b):
    return lax.dot_general(a, b, (((0,), (0,)), ((), ())), preferred_element_type=jnp.float32)


def head_stack(x, heads):
    rows, width = x.shape
    lane_head = lax.broadcasted_iota(jnp.int32, (heads, 1, width), 2) // HD
    which = lax.broadcasted_iota(jnp.int32, (heads, 1, width), 0)
    kept = jnp.where(lane_head == which, x[None], jnp.zeros_like(x)[None])
    return kept.reshape(heads * rows, width)


def block_grads(q, g, k, v, bias):
    nq, width = q.shape
    heads = width // HD
    qm = head_stack(q, heads)
    gm = head_stack(g, heads)
    full_bias = jnp.broadcast_to(bias[None], (heads,) + bias.shape).reshape(heads * nq, -1)
    s = dot_nt(qm, k) * SCALE + full_bias
    mx = jnp.max(s, axis=1, keepdims=True)
    e = jnp.exp(s - mx)
    p = e / jnp.sum(e, axis=1, keepdims=True)
    pb = p.astype(jnp.bfloat16)
    gw = dot_nt(gm, v)
    delta = jnp.sum(pb.astype(jnp.float32) * gw, axis=1, keepdims=True)
    ds = (p * (gw - delta)).astype(jnp.bfloat16)
    dk = dot_tn(ds, qm) * SCALE
    dv = dot_tn(pb, gm)
    lane = lax.broadcasted_iota(jnp.int32, (1, LANES), 1)
    low = lane < HD
    tiles = []
    for pair in range(width // LANES):
        both = jnp.dot(
            ds[2 * pair * nq:(2 * pair + 2) * nq],
            k[:, pair * LANES:(pair + 1) * LANES],
            preferred_element_type=jnp.float32,
        )
        tiles.append(jnp.where(low, both[:nq], both[nq:]) * SCALE)
    dq = jnp.concatenate(tiles, axis=1)
    return dq, dk, dv


def fused_row_kernel(w2, q_ref, g_ref, k_ref, v_ref, l1_ref, r1_ref, bias_ref,
                     qg_ref, kg_ref, vg_ref,
                     l2_ref, r2_ref, own_s, near_l, near_r, s_fl, s_fr, s_nl, s_nr, x_fr, x_fl,
                     x_nr, x_nl, halo_send, halo_recv, far_send, far_recv_r, far_recv_l,
                     near_send, near_recv):
    rows, cc, width = q_ref.shape
    w1 = l1_ref.shape[2]
    n = lax.axis_size("rcol")
    me = lax.axis_index("rcol")
    here = (lax.axis_index("slide"), lax.axis_index("rrow"))
    mesh_ids = pl.DeviceIdType.MESH

    def dev(distance):
        return here + (lax.rem(me + distance + n, n),)

    barrier = pltpu.get_barrier_semaphore()
    for distance in (-1, 1):
        pl.semaphore_signal(barrier, 1, device_id=dev(distance), device_id_type=mesh_ids)
    pl.semaphore_wait(barrier, 2)

    relays = (
        pltpu.make_async_remote_copy(
            src_ref=l1_ref.at[:, :, pl.ds(w1 - w2, w2)], dst_ref=l2_ref,
            send_sem=halo_send.at[0], recv_sem=halo_recv.at[0],
            device_id=dev(1), device_id_type=mesh_ids),
        pltpu.make_async_remote_copy(
            src_ref=r1_ref.at[:, :, pl.ds(0, w2)], dst_ref=r2_ref,
            send_sem=halo_send.at[1], recv_sem=halo_recv.at[1],
            device_id=dev(-1), device_id_type=mesh_ids),
    )
    for copy in relays:
        copy.start()
    for copy in relays:
        copy.wait()

    def far_copy(r, to_left):
        if to_left:
            return pltpu.make_async_remote_copy(
                src_ref=s_fl.at[:, pl.ds(r, 1)], dst_ref=x_fr.at[:, pl.ds(r, 1)],
                send_sem=far_send.at[0], recv_sem=far_recv_r.at[r],
                device_id=dev(-1), device_id_type=mesh_ids)
        return pltpu.make_async_remote_copy(
            src_ref=s_fr.at[:, pl.ds(r, 1)], dst_ref=x_fl.at[:, pl.ds(r, 1)],
            send_sem=far_send.at[1], recv_sem=far_recv_l.at[r],
            device_id=dev(1), device_id_type=mesh_ids)

    def near_copy(r, to_left, whole=False):
        rs = slice(None) if whole else pl.ds(r, 1)
        if to_left:
            return pltpu.make_async_remote_copy(
                src_ref=s_nl.at[:, rs], dst_ref=x_nr.at[:, rs],
                send_sem=near_send.at[0], recv_sem=near_recv.at[0],
                device_id=dev(-1), device_id_type=mesh_ids)
        return pltpu.make_async_remote_copy(
            src_ref=s_nr.at[:, rs], dst_ref=x_nl.at[:, rs],
            send_sem=near_send.at[1], recv_sem=near_recv.at[1],
            device_id=dev(1), device_id_type=mesh_ids)

    def send_near(r):
        far_copy(r, True).wait_recv()
        far_copy(r, False).wait_recv()
        f32 = jnp.float32
        s_nl[:, r, :w1 - w2] = near_l[:, r, :w1 - w2].astype(jnp.bfloat16)
        s_nl[:, r, w1 - w2:] = (near_l[:, r, w1 - w2:] + x_fr[:, r].astype(f32)).astype(jnp.bfloat16)
        s_nr[:, r, :w2] = (near_r[:, r, :w2] + x_fl[:, r].astype(f32)).astype(jnp.bfloat16)
        s_nr[:, r, w2:] = near_r[:, r, w2:].astype(jnp.bfloat16)
        near_copy(r, True).start()
        near_copy(r, False).start()

    def row_step(r, carry):
        def span(which, own_ref):
            return jnp.concatenate(
                [l2_ref[which, r], l1_ref[which, r], own_ref[r], r1_ref[which, r],
                 r2_ref[which, r]],
                axis=0,
            )

        dq, dk, dv = block_grads(q_ref[r], g_ref[r], span(0, k_ref), span(1, v_ref), bias_ref[r])
        qg_ref[r] = dq
        for which, full in ((0, dk), (1, dv)):
            s_fl[which, r] = full[:w2].astype(jnp.bfloat16)
            near_l[which, r] = full[w2:w2 + w1]
            own_s[which, r] = full[w2 + w1:w2 + w1 + cc]
            near_r[which, r] = full[w2 + w1 + cc:w2 + 2 * w1 + cc]
            s_fr[which, r] = full[w2 + 2 * w1 + cc:].astype(jnp.bfloat16)
        far_copy(r, True).start()
        far_copy(r, False).start()

        @pl.when(r > 0)
        def _():
            send_near(r - 1)

        return carry

    lax.fori_loop(0, rows, row_step, 0)
    send_near(rows - 1)
    for src, dst, slot in ((s_fl, x_fr, 0), (s_fr, x_fl, 1)):
        pltpu.make_async_remote_copy(
            src_ref=src, dst_ref=dst, send_sem=far_send.at[slot], recv_sem=far_recv_r.at[0],
            device_id=dev(1 - 2 * (1 - slot)), device_id_type=mesh_ids).wait_send()
    for to_left in (True, False):
        near_copy(0, to_left, whole=True).wait()
    f32 = jnp.float32
    for which, out_ref in ((0, kg_ref), (1, vg_ref)):
        out_ref[...] = own_s[which] + x_nr[which].astype(f32) + x_nl[which].astype(f32)


def fused_row(queries, out_grad, key_grid, value_grid, l1, r1, bias, w2):
    rows, cc, width = queries.shape
    w1 = l1.shape[2]
    vmem = pl.BlockSpec(memory_space=pltpu.VMEM)
    grads = jax.ShapeDtypeStruct((rows, cc, width), jnp.float32)
    bf = jnp.bfloat16
    f32 = jnp.float32
    return pl.pallas_call(
        functools.partial(fused_row_kernel, w2),
        in_specs=[vmem] * 7,
        out_specs=[vmem] * 3,
        out_shape=(grads, grads, grads),
        scratch_shapes=[
            pltpu.VMEM((2, rows, w2, width), bf),
            pltpu.VMEM((2, rows, w2, width), bf),
            pltpu.VMEM((2, rows, cc, width), f32),
            pltpu.VMEM((2, rows, w1, width), f32),
            pltpu.VMEM((2, rows, w1, width), f32),
            pltpu.VMEM((2, rows, w2, width), bf),
            pltpu.VMEM((2, rows, w2, width), bf),
            pltpu.VMEM((2, rows, w1, width), bf),
            pltpu.VMEM((2, rows, w1, width), bf),
            pltpu.VMEM((2, rows, w2, width), bf),
            pltpu.VMEM((2, rows, w2, width), bf),
            pltpu.VMEM((2, rows, cc, width), bf),
            pltpu.VMEM((2, rows, cc, width), bf),
            pltpu.SemaphoreType.DMA((2,)),
            pltpu.SemaphoreType.DMA((2,)),
            pltpu.SemaphoreType.DMA((2,)),
            pltpu.SemaphoreType.DMA((rows,)),
            pltpu.SemaphoreType.DMA((rows,)),
            pltpu.SemaphoreType.DMA((2,)),
            pltpu.SemaphoreType.DMA((2,)),
        ],
        compiler_params=pltpu.CompilerParams(
            collective_id=0, has_side_effects=True, vmem_limit_bytes=60 * 1024 * 1024
        ),
    )(queries, out_grad, key_grid, value_grid, l1, r1, bias)


def column_kernel(x_ref, o_ref):
    per = x_ref.shape[1]
    rows = x_ref.shape[2]

    def joined(which):
        return jnp.concatenate([x_ref[which, c] for c in range(per)], axis=0)

    i = lax.broadcasted_iota(jnp.int32, (per * rows, per * rows), 0) // rows
    j = lax.broadcasted_iota(jnp.int32, (per * rows, per * rows), 1) // rows
    bias = jnp.where(i == j, 0.0, -jnp.inf).astype(jnp.float32)
    grads = block_grads(joined(0), joined(3), joined(1), joined(2), bias)
    for which, full in enumerate(grads):
        for c in range(per):
            o_ref[which, c] = full[c * rows:(c + 1) * rows].astype(jnp.bfloat16)


def column_attention(whole):
    arrays, strip, rows, width = whole.shape
    per = max(1, LANES // rows)
    return pl.pallas_call(
        column_kernel,
        grid=(strip // per,),
        in_specs=[pl.BlockSpec((arrays, per, rows, width), lambda c: (0, c, 0, 0))],
        out_specs=pl.BlockSpec((3, per, rows, width), lambda c: (0, c, 0, 0)),
        out_shape=jax.ShapeDtypeStruct((3, strip, rows, width), jnp.bfloat16),
    )(whole)


def band_bias(mask_rows, offsets, first_col, grid_cols, block_cols):
    band_reach = HALF + OFFMAX
    query_cols = first_col + jnp.arange(block_cols, dtype=jnp.int32)
    key_cols = first_col - band_reach + jnp.arange(block_cols + 2 * band_reach, dtype=jnp.int32)
    inside = (key_cols >= 0) & (key_cols < grid_cols)
    key_block = jnp.clip(key_cols, 0, grid_cols - 1) // BLK
    block_ids = jnp.arange(mask_rows.shape[1], dtype=jnp.int32)
    key_open = jnp.sum(
        mask_rows[:, None, :]
        * (key_block[None, :, None] == block_ids[None, None, :]).astype(jnp.int32),
        axis=-1,
    )
    relative = key_cols[None, None, :] - query_cols[None, :, None] - offsets[:, None, None]
    same_block = key_cols[None, :] // BLK == query_cols[:, None] // BLK
    allowed = (
        (relative >= -HALF)
        & (relative < HALF)
        & inside[None, None, :]
        & ((key_open[:, None, :] > 0) | same_block[None])
    )
    return jnp.where(allowed, 0.0, -jnp.inf).astype(jnp.float32)


def body(queries, key_grid, value_grid, out_grad, tissue_mask, band_offset):
    row_count, col_count, feature_width = queries.shape
    group_count = lax.axis_size("rrow")
    band_reach = HALF + OFFMAX
    near = col_count
    far = band_reach - col_count

    stacked = jnp.stack([queries, key_grid, value_grid, out_grad]).transpose(0, 2, 1, 3)
    whole = lax.all_to_all(stacked, "rrow", split_axis=1, concat_axis=2, tiled=True)

    pair = jnp.stack([key_grid, value_grid])
    l1 = shifted(pair[:, :, col_count - near:], "rcol", 1)
    r1 = shifted(pair[:, :, :near], "rcol", -1)
    grid_cols = col_count * lax.axis_size("rcol")
    first_col = lax.axis_index("rcol") * col_count
    bias = band_bias(tissue_mask, band_offset, first_col, grid_cols, col_count)

    col_out = column_attention(whole)
    back = lax.all_to_all(col_out, "rrow", split_axis=2, concat_axis=1, tiled=True)
    row_grads = fused_row(queries, out_grad, key_grid, value_grid, l1, r1, bias, far)
    back = back.transpose(0, 2, 1, 3).astype(jnp.float32)
    return tuple((row + col).astype(jnp.bfloat16) for row, col in zip(row_grads, back))


def solution(mesh):
    in_specs = (
        P(("slide", "rrow"), "rcol", None),
        P(("slide", "rrow"), "rcol", None),
        P(("slide", "rrow"), "rcol", None),
        P(("slide", "rrow"), "rcol", None),
        P(("slide", "rrow"), None),
        P(("slide", "rrow")),
    )
    out_specs = (
        P(("slide", "rrow"), "rcol", None),
        P(("slide", "rrow"), "rcol", None),
        P(("slide", "rrow"), "rcol", None),
    )
    return jax.shard_map(body, mesh=mesh, in_specs=in_specs, out_specs=out_specs, check_vma=False)
```

```python
import functools
import math

import jax
import jax.numpy as jnp
from jax import lax
from jax.experimental import pallas as pl
from jax.experimental.pallas import tpu as pltpu
from jax.sharding import PartitionSpec as P

HD = 64
BLK = 16
HALF = 32
OFFMAX = 16
SCALE = 1.0 / math.sqrt(HD)
LANES = 128


def shifted(block, axis, distance):
    devices = range(lax.axis_size(axis))
    route = [(i - distance, i) for i in devices if i - distance in devices]
    return lax.ppermute(block, axis, route)


def dot_nt(a, b):
    return lax.dot_general(a, b, (((1,), (1,)), ((), ())), preferred_element_type=jnp.float32)


def dot_tn(a, b):
    return lax.dot_general(a, b, (((0,), (0,)), ((), ())), preferred_element_type=jnp.float32)


def head_stack(x, heads):
    rows, width = x.shape
    lane_head = lax.broadcasted_iota(jnp.int32, (heads, 1, width), 2) // HD
    which = lax.broadcasted_iota(jnp.int32, (heads, 1, width), 0)
    kept = jnp.where(lane_head == which, x[None], jnp.zeros_like(x)[None])
    return kept.reshape(heads * rows, width)


def block_grads(q, g, k, v, bias):
    nq, width = q.shape
    heads = width // HD
    qm = head_stack(q, heads)
    gm = head_stack(g, heads)
    full_bias = jnp.broadcast_to(bias[None], (heads,) + bias.shape).reshape(heads * nq, -1)
    s = dot_nt(qm, k) * SCALE + full_bias
    mx = jnp.max(s, axis=1, keepdims=True)
    e = jnp.exp(s - mx)
    p = e / jnp.sum(e, axis=1, keepdims=True)
    pb = p.astype(jnp.bfloat16)
    gw = dot_nt(gm, v)
    delta = jnp.sum(pb.astype(jnp.float32) * gw, axis=1, keepdims=True)
    ds = (p * (gw - delta)).astype(jnp.bfloat16)
    dk = dot_tn(ds, qm) * SCALE
    dv = dot_tn(pb, gm)
    lane = lax.broadcasted_iota(jnp.int32, (1, LANES), 1)
    low = lane < HD
    tiles = []
    for pair in range(width // LANES):
        both = jnp.dot(
            ds[2 * pair * nq:(2 * pair + 2) * nq],
            k[:, pair * LANES:(pair + 1) * LANES],
            preferred_element_type=jnp.float32,
        )
        tiles.append(jnp.where(low, both[:nq], both[nq:]) * SCALE)
    dq = jnp.concatenate(tiles, axis=1)
    return dq, dk, dv


def fused_row_kernel(w2, q_ref, g_ref, k_ref, v_ref, l1_ref, r1_ref, bias_ref,
                     qg_ref, kg_ref, vg_ref,
                     l2_ref, r2_ref, own_s, near_l, near_r, s_fl, s_fr, s_nl, s_nr, x_fr, x_fl,
                     x_nr, x_nl, halo_send, halo_recv, far_send, far_recv_r, far_recv_l,
                     near_send, near_recv):
    rows, cc, width = q_ref.shape
    w1 = l1_ref.shape[2]
    n = lax.axis_size("rcol")
    me = lax.axis_index("rcol")
    here = (lax.axis_index("slide"), lax.axis_index("rrow"))
    mesh_ids = pl.DeviceIdType.MESH

    def dev(distance):
        return here + (lax.rem(me + distance + n, n),)

    barrier = pltpu.get_barrier_semaphore()
    for distance in (-1, 1):
        pl.semaphore_signal(barrier, 1, device_id=dev(distance), device_id_type=mesh_ids)
    pl.semaphore_wait(barrier, 2)

    relays = (
        pltpu.make_async_remote_copy(
            src_ref=l1_ref.at[:, :, pl.ds(w1 - w2, w2)], dst_ref=l2_ref,
            send_sem=halo_send.at[0], recv_sem=halo_recv.at[0],
            device_id=dev(1), device_id_type=mesh_ids),
        pltpu.make_async_remote_copy(
            src_ref=r1_ref.at[:, :, pl.ds(0, w2)], dst_ref=r2_ref,
            send_sem=halo_send.at[1], recv_sem=halo_recv.at[1],
            device_id=dev(-1), device_id_type=mesh_ids),
    )
    for copy in relays:
        copy.start()
    for copy in relays:
        copy.wait()

    def far_copy(r, to_left):
        if to_left:
            return pltpu.make_async_remote_copy(
                src_ref=s_fl.at[:, pl.ds(r, 1)], dst_ref=x_fr.at[:, pl.ds(r, 1)],
                send_sem=far_send.at[0], recv_sem=far_recv_r.at[r],
                device_id=dev(-1), device_id_type=mesh_ids)
        return pltpu.make_async_remote_copy(
            src_ref=s_fr.at[:, pl.ds(r, 1)], dst_ref=x_fl.at[:, pl.ds(r, 1)],
            send_sem=far_send.at[1], recv_sem=far_recv_l.at[r],
            device_id=dev(1), device_id_type=mesh_ids)

    def near_copy(r, to_left, whole=False):
        rs = slice(None) if whole else pl.ds(r, 1)
        if to_left:
            return pltpu.make_async_remote_copy(
                src_ref=s_nl.at[:, rs], dst_ref=x_nr.at[:, rs],
                send_sem=near_send.at[0], recv_sem=near_recv.at[0],
                device_id=dev(-1), device_id_type=mesh_ids)
        return pltpu.make_async_remote_copy(
            src_ref=s_nr.at[:, rs], dst_ref=x_nl.at[:, rs],
            send_sem=near_send.at[1], recv_sem=near_recv.at[1],
            device_id=dev(1), device_id_type=mesh_ids)

    def send_near(r):
        far_copy(r, True).wait_recv()
        far_copy(r, False).wait_recv()
        f32 = jnp.float32
        s_nl[:, r, :w1 - w2] = near_l[:, r, :w1 - w2].astype(jnp.bfloat16)
        s_nl[:, r, w1 - w2:] = (near_l[:, r, w1 - w2:] + x_fr[:, r].astype(f32)).astype(jnp.bfloat16)
        s_nr[:, r, :w2] = (near_r[:, r, :w2] + x_fl[:, r].astype(f32)).astype(jnp.bfloat16)
        s_nr[:, r, w2:] = near_r[:, r, w2:].astype(jnp.bfloat16)
        near_copy(r, True).start()
        near_copy(r, False).start()

    def row_step(r, carry):
        def span(which, own_ref):
            return jnp.concatenate(
                [l2_ref[which, r], l1_ref[which, r], own_ref[r], r1_ref[which, r],
                 r2_ref[which, r]],
                axis=0,
            )

        dq, dk, dv = block_grads(q_ref[r], g_ref[r], span(0, k_ref), span(1, v_ref), bias_ref[r])
        qg_ref[r] = dq
        for which, full in ((0, dk), (1, dv)):
            s_fl[which, r] = full[:w2].astype(jnp.bfloat16)
            near_l[which, r] = full[w2:w2 + w1]
            own_s[which, r] = full[w2 + w1:w2 + w1 + cc]
            near_r[which, r] = full[w2 + w1 + cc:w2 + 2 * w1 + cc]
            s_fr[which, r] = full[w2 + 2 * w1 + cc:].astype(jnp.bfloat16)
        far_copy(r, True).start()
        far_copy(r, False).start()

        @pl.when(r > 0)
        def _():
            send_near(r - 1)

        return carry

    lax.fori_loop(0, rows, row_step, 0)
    send_near(rows - 1)
    for src, dst, slot in ((s_fl, x_fr, 0), (s_fr, x_fl, 1)):
        pltpu.make_async_remote_copy(
            src_ref=src, dst_ref=dst, send_sem=far_send.at[slot], recv_sem=far_recv_r.at[0],
            device_id=dev(1 - 2 * (1 - slot)), device_id_type=mesh_ids).wait_send()
    for to_left in (True, False):
        near_copy(0, to_left, whole=True).wait()
    f32 = jnp.float32
    for which, out_ref in ((0, kg_ref), (1, vg_ref)):
        out_ref[...] = own_s[which] + x_nr[which].astype(f32) + x_nl[which].astype(f32)


def fused_row(queries, out_grad, key_grid, value_grid, l1, r1, bias, w2):
    rows, cc, width = queries.shape
    w1 = l1.shape[2]
    vmem = pl.BlockSpec(memory_space=pltpu.VMEM)
    grads = jax.ShapeDtypeStruct((rows, cc, width), jnp.float32)
    bf = jnp.bfloat16
    f32 = jnp.float32
    return pl.pallas_call(
        functools.partial(fused_row_kernel, w2),
        in_specs=[vmem] * 7,
        out_specs=[vmem] * 3,
        out_shape=(grads, grads, grads),
        scratch_shapes=[
            pltpu.VMEM((2, rows, w2, width), bf),
            pltpu.VMEM((2, rows, w2, width), bf),
            pltpu.VMEM((2, rows, cc, width), f32),
            pltpu.VMEM((2, rows, w1, width), f32),
            pltpu.VMEM((2, rows, w1, width), f32),
            pltpu.VMEM((2, rows, w2, width), bf),
            pltpu.VMEM((2, rows, w2, width), bf),
            pltpu.VMEM((2, rows, w1, width), bf),
            pltpu.VMEM((2, rows, w1, width), bf),
            pltpu.VMEM((2, rows, w2, width), bf),
            pltpu.VMEM((2, rows, w2, width), bf),
            pltpu.VMEM((2, rows, cc, width), bf),
            pltpu.VMEM((2, rows, cc, width), bf),
            pltpu.SemaphoreType.DMA((2,)),
            pltpu.SemaphoreType.DMA((2,)),
            pltpu.SemaphoreType.DMA((2,)),
            pltpu.SemaphoreType.DMA((rows,)),
            pltpu.SemaphoreType.DMA((rows,)),
            pltpu.SemaphoreType.DMA((2,)),
            pltpu.SemaphoreType.DMA((2,)),
        ],
        compiler_params=pltpu.CompilerParams(
            collective_id=0, has_side_effects=True, vmem_limit_bytes=60 * 1024 * 1024
        ),
    )(queries, out_grad, key_grid, value_grid, l1, r1, bias)


def column_kernel(x_ref, o_ref):
    groups, arrays, strip, rows, width = x_ref.shape
    per = max(1, LANES // (groups * rows))

    def joined(which):
        return jnp.concatenate(
            [x_ref[s, which, c] for c in range(per) for s in range(groups)], axis=0
        )

    whole_rows = groups * rows
    i = lax.broadcasted_iota(jnp.int32, (per * whole_rows, per * whole_rows), 0) // whole_rows
    j = lax.broadcasted_iota(jnp.int32, (per * whole_rows, per * whole_rows), 1) // whole_rows
    bias = jnp.where(i == j, 0.0, -jnp.inf).astype(jnp.float32)
    for step in range(strip // per):
        def pick(which):
            return jnp.concatenate(
                [x_ref[s, which, step * per + c] for c in range(per) for s in range(groups)],
                axis=0,
            )

        grads = block_grads(pick(0), pick(3), pick(1), pick(2), bias)
        for which, full in enumerate(grads):
            low = full.astype(jnp.bfloat16)
            for c in range(per):
                for s in range(groups):
                    start = c * whole_rows + s * rows
                    o_ref[s, which, step * per + c] = low[start:start + rows]


def column_attention(whole):
    groups, arrays, strip, rows, width = whole.shape
    vmem = pl.BlockSpec(memory_space=pltpu.VMEM)
    return pl.pallas_call(
        column_kernel,
        in_specs=[vmem],
        out_specs=vmem,
        out_shape=jax.ShapeDtypeStruct((groups, 3, strip, rows, width), jnp.bfloat16),
    )(whole)


def band_bias(mask_rows, offsets, first_col, grid_cols, block_cols):
    band_reach = HALF + OFFMAX
    query_cols = first_col + jnp.arange(block_cols, dtype=jnp.int32)
    key_cols = first_col - band_reach + jnp.arange(block_cols + 2 * band_reach, dtype=jnp.int32)
    inside = (key_cols >= 0) & (key_cols < grid_cols)
    key_block = jnp.clip(key_cols, 0, grid_cols - 1) // BLK
    block_ids = jnp.arange(mask_rows.shape[1], dtype=jnp.int32)
    key_open = jnp.sum(
        mask_rows[:, None, :]
        * (key_block[None, :, None] == block_ids[None, None, :]).astype(jnp.int32),
        axis=-1,
    )
    relative = key_cols[None, None, :] - query_cols[None, :, None] - offsets[:, None, None]
    same_block = key_cols[None, :] // BLK == query_cols[:, None] // BLK
    allowed = (
        (relative >= -HALF)
        & (relative < HALF)
        & inside[None, None, :]
        & ((key_open[:, None, :] > 0) | same_block[None])
    )
    return jnp.where(allowed, 0.0, -jnp.inf).astype(jnp.float32)


def body(queries, key_grid, value_grid, out_grad, tissue_mask, band_offset):
    row_count, col_count, feature_width = queries.shape
    group_count = lax.axis_size("rrow")
    band_reach = HALF + OFFMAX
    near = col_count
    far = band_reach - col_count

    strip = col_count // group_count
    stacked = (
        jnp.stack([queries, key_grid, value_grid, out_grad])
        .reshape(4, row_count, group_count, strip, feature_width)
        .transpose(2, 0, 3, 1, 4)
    )
    whole = lax.all_to_all(stacked, "rrow", split_axis=0, concat_axis=0, tiled=True)

    pair = jnp.stack([key_grid, value_grid])
    l1 = shifted(pair[:, :, col_count - near:], "rcol", 1)
    r1 = shifted(pair[:, :, :near], "rcol", -1)
    grid_cols = col_count * lax.axis_size("rcol")
    first_col = lax.axis_index("rcol") * col_count
    bias = band_bias(tissue_mask, band_offset, first_col, grid_cols, col_count)

    col_out = column_attention(whole)
    back = lax.all_to_all(col_out, "rrow", split_axis=0, concat_axis=0, tiled=True)
    row_grads = fused_row(queries, out_grad, key_grid, value_grid, l1, r1, bias, far)
    back = back.transpose(1, 3, 0, 2, 4).reshape(3, row_count, col_count, feature_width)
    back = back.astype(jnp.float32)
    return tuple((row + col).astype(jnp.bfloat16) for row, col in zip(row_grads, back))


def solution(mesh):
    in_specs = (
        P(("slide", "rrow"), "rcol", None),
        P(("slide", "rrow"), "rcol", None),
        P(("slide", "rrow"), "rcol", None),
        P(("slide", "rrow"), "rcol", None),
        P(("slide", "rrow"), None),
        P(("slide", "rrow")),
    )
    out_specs = (
        P(("slide", "rrow"), "rcol", None),
        P(("slide", "rrow"), "rcol", None),
        P(("slide", "rrow"), "rcol", None),
    )
    return jax.shard_map(body, mesh=mesh, in_specs=in_specs, out_specs=out_specs, check_vma=False)
```

```python
import functools
import math

import jax
import jax.numpy as jnp
from jax import lax
from jax.experimental import pallas as pl
from jax.experimental.pallas import tpu as pltpu
from jax.sharding import PartitionSpec as P

HD = 64
BLK = 16
HALF = 32
OFFMAX = 16
SCALE = 1.0 / math.sqrt(HD)
LANES = 128


def shifted(block, axis, distance):
    devices = range(lax.axis_size(axis))
    route = [(i - distance, i) for i in devices if i - distance in devices]
    return lax.ppermute(block, axis, route)


def dot_nt(a, b):
    return lax.dot_general(a, b, (((1,), (1,)), ((), ())), preferred_element_type=jnp.float32)


def dot_tn(a, b):
    return lax.dot_general(a, b, (((0,), (0,)), ((), ())), preferred_element_type=jnp.float32)


def head_stack(x, heads):
    rows, width = x.shape
    lane_head = lax.broadcasted_iota(jnp.int32, (heads, 1, width), 2) // HD
    which = lax.broadcasted_iota(jnp.int32, (heads, 1, width), 0)
    kept = jnp.where(lane_head == which, x[None], jnp.zeros_like(x)[None])
    return kept.reshape(heads * rows, width)


def block_grads(q, g, k, v, bias):
    nq, width = q.shape
    heads = width // HD
    group = min(width, 2 * LANES)
    per_group = group // HD
    lanes = [slice(t * group, (t + 1) * group) for t in range(width // group)]
    qm = [head_stack(q[:, part], per_group) for part in lanes]
    gm = [head_stack(g[:, part], per_group) for part in lanes]
    full_bias = jnp.broadcast_to(bias[None], (heads,) + bias.shape).reshape(heads * nq, -1)
    s = jnp.concatenate([dot_nt(a, k[:, part]) for a, part in zip(qm, lanes)], axis=0)
    s = s * SCALE + full_bias
    mx = jnp.max(s, axis=1, keepdims=True)
    e = jnp.exp(s - mx)
    p = e / jnp.sum(e, axis=1, keepdims=True)
    pb = p.astype(jnp.bfloat16)
    gw = jnp.concatenate([dot_nt(a, v[:, part]) for a, part in zip(gm, lanes)], axis=0)
    delta = jnp.sum(pb.astype(jnp.float32) * gw, axis=1, keepdims=True)
    ds = (p * (gw - delta)).astype(jnp.bfloat16)
    rows = per_group * nq
    dk = jnp.concatenate(
        [dot_tn(ds[t * rows:(t + 1) * rows], a) for t, a in enumerate(qm)], axis=1
    ) * SCALE
    dv = jnp.concatenate(
        [dot_tn(pb[t * rows:(t + 1) * rows], a) for t, a in enumerate(gm)], axis=1
    )
    lane = lax.broadcasted_iota(jnp.int32, (1, LANES), 1)
    low = lane < HD
    tiles = []
    for pair in range(width // LANES):
        both = jnp.dot(
            ds[2 * pair * nq:(2 * pair + 2) * nq],
            k[:, pair * LANES:(pair + 1) * LANES],
            preferred_element_type=jnp.float32,
        )
        tiles.append(jnp.where(low, both[:nq], both[nq:]) * SCALE)
    dq = jnp.concatenate(tiles, axis=1)
    return dq, dk, dv


def fused_row_kernel(w2, q_ref, g_ref, k_ref, v_ref, l1_ref, r1_ref, bias_ref,
                     qg_ref, kg_ref, vg_ref,
                     l2_ref, r2_ref, own_s, near_l, near_r, s_fl, s_fr, s_nl, s_nr, x_fr, x_fl,
                     x_nr, x_nl, halo_send, halo_recv, far_send, far_recv_r, far_recv_l,
                     near_send, near_recv):
    rows, cc, width = q_ref.shape
    w1 = l1_ref.shape[2]
    n = lax.axis_size("rcol")
    me = lax.axis_index("rcol")
    here = (lax.axis_index("slide"), lax.axis_index("rrow"))
    mesh_ids = pl.DeviceIdType.MESH

    def dev(distance):
        return here + (lax.rem(me + distance + n, n),)

    barrier = pltpu.get_barrier_semaphore()
    for distance in (-1, 1):
        pl.semaphore_signal(barrier, 1, device_id=dev(distance), device_id_type=mesh_ids)
    pl.semaphore_wait(barrier, 2)

    relays = (
        pltpu.make_async_remote_copy(
            src_ref=l1_ref.at[:, :, pl.ds(w1 - w2, w2)], dst_ref=l2_ref,
            send_sem=halo_send.at[0], recv_sem=halo_recv.at[0],
            device_id=dev(1), device_id_type=mesh_ids),
        pltpu.make_async_remote_copy(
            src_ref=r1_ref.at[:, :, pl.ds(0, w2)], dst_ref=r2_ref,
            send_sem=halo_send.at[1], recv_sem=halo_recv.at[1],
            device_id=dev(-1), device_id_type=mesh_ids),
    )
    for copy in relays:
        copy.start()
    for copy in relays:
        copy.wait()

    def far_copy(r, to_left):
        if to_left:
            return pltpu.make_async_remote_copy(
                src_ref=s_fl.at[:, pl.ds(r, 1)], dst_ref=x_fr.at[:, pl.ds(r, 1)],
                send_sem=far_send.at[0], recv_sem=far_recv_r.at[r],
                device_id=dev(-1), device_id_type=mesh_ids)
        return pltpu.make_async_remote_copy(
            src_ref=s_fr.at[:, pl.ds(r, 1)], dst_ref=x_fl.at[:, pl.ds(r, 1)],
            send_sem=far_send.at[1], recv_sem=far_recv_l.at[r],
            device_id=dev(1), device_id_type=mesh_ids)

    def near_copy(r, to_left, whole=False):
        rs = slice(None) if whole else pl.ds(r, 1)
        if to_left:
            return pltpu.make_async_remote_copy(
                src_ref=s_nl.at[:, rs], dst_ref=x_nr.at[:, rs],
                send_sem=near_send.at[0], recv_sem=near_recv.at[0],
                device_id=dev(-1), device_id_type=mesh_ids)
        return pltpu.make_async_remote_copy(
            src_ref=s_nr.at[:, rs], dst_ref=x_nl.at[:, rs],
            send_sem=near_send.at[1], recv_sem=near_recv.at[1],
            device_id=dev(1), device_id_type=mesh_ids)

    def send_near(r):
        far_copy(r, True).wait_recv()
        far_copy(r, False).wait_recv()
        f32 = jnp.float32
        s_nl[:, r, :w1 - w2] = near_l[:, r, :w1 - w2].astype(jnp.bfloat16)
        s_nl[:, r, w1 - w2:] = (near_l[:, r, w1 - w2:] + x_fr[:, r].astype(f32)).astype(jnp.bfloat16)
        s_nr[:, r, :w2] = (near_r[:, r, :w2] + x_fl[:, r].astype(f32)).astype(jnp.bfloat16)
        s_nr[:, r, w2:] = near_r[:, r, w2:].astype(jnp.bfloat16)
        near_copy(r, True).start()
        near_copy(r, False).start()

    def row_step(r, carry):
        def span(which, own_ref):
            return jnp.concatenate(
                [l2_ref[which, r], l1_ref[which, r], own_ref[r], r1_ref[which, r],
                 r2_ref[which, r]],
                axis=0,
            )

        dq, dk, dv = block_grads(q_ref[r], g_ref[r], span(0, k_ref), span(1, v_ref), bias_ref[r])
        qg_ref[r] = dq
        for which, full in ((0, dk), (1, dv)):
            s_fl[which, r] = full[:w2].astype(jnp.bfloat16)
            near_l[which, r] = full[w2:w2 + w1]
            own_s[which, r] = full[w2 + w1:w2 + w1 + cc]
            near_r[which, r] = full[w2 + w1 + cc:w2 + 2 * w1 + cc]
            s_fr[which, r] = full[w2 + 2 * w1 + cc:].astype(jnp.bfloat16)
        far_copy(r, True).start()
        far_copy(r, False).start()

        @pl.when(r > 0)
        def _():
            send_near(r - 1)

        return carry

    lax.fori_loop(0, rows, row_step, 0)
    send_near(rows - 1)
    for src, dst, slot in ((s_fl, x_fr, 0), (s_fr, x_fl, 1)):
        pltpu.make_async_remote_copy(
            src_ref=src, dst_ref=dst, send_sem=far_send.at[slot], recv_sem=far_recv_r.at[0],
            device_id=dev(1 - 2 * (1 - slot)), device_id_type=mesh_ids).wait_send()
    for to_left in (True, False):
        near_copy(0, to_left, whole=True).wait()
    f32 = jnp.float32
    for which, out_ref in ((0, kg_ref), (1, vg_ref)):
        out_ref[...] = own_s[which] + x_nr[which].astype(f32) + x_nl[which].astype(f32)


def fused_row(queries, out_grad, key_grid, value_grid, l1, r1, bias, w2):
    rows, cc, width = queries.shape
    w1 = l1.shape[2]
    vmem = pl.BlockSpec(memory_space=pltpu.VMEM)
    grads = jax.ShapeDtypeStruct((rows, cc, width), jnp.float32)
    bf = jnp.bfloat16
    f32 = jnp.float32
    return pl.pallas_call(
        functools.partial(fused_row_kernel, w2),
        in_specs=[vmem] * 7,
        out_specs=[vmem] * 3,
        out_shape=(grads, grads, grads),
        scratch_shapes=[
            pltpu.VMEM((2, rows, w2, width), bf),
            pltpu.VMEM((2, rows, w2, width), bf),
            pltpu.VMEM((2, rows, cc, width), f32),
            pltpu.VMEM((2, rows, w1, width), f32),
            pltpu.VMEM((2, rows, w1, width), f32),
            pltpu.VMEM((2, rows, w2, width), bf),
            pltpu.VMEM((2, rows, w2, width), bf),
            pltpu.VMEM((2, rows, w1, width), bf),
            pltpu.VMEM((2, rows, w1, width), bf),
            pltpu.VMEM((2, rows, w2, width), bf),
            pltpu.VMEM((2, rows, w2, width), bf),
            pltpu.VMEM((2, rows, cc, width), bf),
            pltpu.VMEM((2, rows, cc, width), bf),
            pltpu.SemaphoreType.DMA((2,)),
            pltpu.SemaphoreType.DMA((2,)),
            pltpu.SemaphoreType.DMA((2,)),
            pltpu.SemaphoreType.DMA((rows,)),
            pltpu.SemaphoreType.DMA((rows,)),
            pltpu.SemaphoreType.DMA((2,)),
            pltpu.SemaphoreType.DMA((2,)),
        ],
        compiler_params=pltpu.CompilerParams(
            collective_id=0, has_side_effects=True, vmem_limit_bytes=60 * 1024 * 1024
        ),
    )(queries, out_grad, key_grid, value_grid, l1, r1, bias)


def column_kernel(x_ref, o_ref):
    groups, arrays, strip, rows, width = x_ref.shape
    per = max(1, LANES // (groups * rows))

    def joined(which):
        return jnp.concatenate(
            [x_ref[s, which, c] for c in range(per) for s in range(groups)], axis=0
        )

    whole_rows = groups * rows
    i = lax.broadcasted_iota(jnp.int32, (per * whole_rows, per * whole_rows), 0) // whole_rows
    j = lax.broadcasted_iota(jnp.int32, (per * whole_rows, per * whole_rows), 1) // whole_rows
    bias = jnp.where(i == j, 0.0, -jnp.inf).astype(jnp.float32)
    for step in range(strip // per):
        def pick(which):
            return jnp.concatenate(
                [x_ref[s, which, step * per + c] for c in range(per) for s in range(groups)],
                axis=0,
            )

        grads = block_grads(pick(0), pick(3), pick(1), pick(2), bias)
        for which, full in enumerate(grads):
            low = full.astype(jnp.bfloat16)
            for c in range(per):
                for s in range(groups):
                    start = c * whole_rows + s * rows
                    o_ref[s, which, step * per + c] = low[start:start + rows]


def column_attention(whole):
    groups, arrays, strip, rows, width = whole.shape
    vmem = pl.BlockSpec(memory_space=pltpu.VMEM)
    return pl.pallas_call(
        column_kernel,
        in_specs=[vmem],
        out_specs=vmem,
        out_shape=jax.ShapeDtypeStruct((groups, 3, strip, rows, width), jnp.bfloat16),
    )(whole)


def band_bias(mask_rows, offsets, first_col, grid_cols, block_cols):
    band_reach = HALF + OFFMAX
    query_cols = first_col + jnp.arange(block_cols, dtype=jnp.int32)
    key_cols = first_col - band_reach + jnp.arange(block_cols + 2 * band_reach, dtype=jnp.int32)
    inside = (key_cols >= 0) & (key_cols < grid_cols)
    key_block = jnp.clip(key_cols, 0, grid_cols - 1) // BLK
    block_ids = jnp.arange(mask_rows.shape[1], dtype=jnp.int32)
    key_open = jnp.sum(
        mask_rows[:, None, :]
        * (key_block[None, :, None] == block_ids[None, None, :]).astype(jnp.int32),
        axis=-1,
    )
    relative = key_cols[None, None, :] - query_cols[None, :, None] - offsets[:, None, None]
    same_block = key_cols[None, :] // BLK == query_cols[:, None] // BLK
    allowed = (
        (relative >= -HALF)
        & (relative < HALF)
        & inside[None, None, :]
        & ((key_open[:, None, :] > 0) | same_block[None])
    )
    return jnp.where(allowed, 0.0, -jnp.inf).astype(jnp.float32)


def body(queries, key_grid, value_grid, out_grad, tissue_mask, band_offset):
    row_count, col_count, feature_width = queries.shape
    group_count = lax.axis_size("rrow")
    band_reach = HALF + OFFMAX
    near = col_count
    far = band_reach - col_count

    strip = col_count // group_count
    stacked = (
        jnp.stack([queries, key_grid, value_grid, out_grad])
        .reshape(4, row_count, group_count, strip, feature_width)
        .transpose(2, 0, 3, 1, 4)
    )
    whole = lax.all_to_all(stacked, "rrow", split_axis=0, concat_axis=0, tiled=True)

    pair = jnp.stack([key_grid, value_grid])
    l1 = shifted(pair[:, :, col_count - near:], "rcol", 1)
    r1 = shifted(pair[:, :, :near], "rcol", -1)
    grid_cols = col_count * lax.axis_size("rcol")
    first_col = lax.axis_index("rcol") * col_count
    bias = band_bias(tissue_mask, band_offset, first_col, grid_cols, col_count)

    col_out = column_attention(whole)
    back = lax.all_to_all(col_out, "rrow", split_axis=0, concat_axis=0, tiled=True)
    row_grads = fused_row(queries, out_grad, key_grid, value_grid, l1, r1, bias, far)
    back = back.transpose(1, 3, 0, 2, 4).reshape(3, row_count, col_count, feature_width)
    back = back.astype(jnp.float32)
    return tuple((row + col).astype(jnp.bfloat16) for row, col in zip(row_grads, back))


def solution(mesh):
    in_specs = (
        P(("slide", "rrow"), "rcol", None),
        P(("slide", "rrow"), "rcol", None),
        P(("slide", "rrow"), "rcol", None),
        P(("slide", "rrow"), "rcol", None),
        P(("slide", "rrow"), None),
        P(("slide", "rrow")),
    )
    out_specs = (
        P(("slide", "rrow"), "rcol", None),
        P(("slide", "rrow"), "rcol", None),
        P(("slide", "rrow"), "rcol", None),
    )
    return jax.shard_map(body, mesh=mesh, in_specs=in_specs, out_specs=out_specs, check_vma=False)
```

```python
import functools
import math

import jax
import jax.numpy as jnp
from jax import lax
from jax.experimental import pallas as pl
from jax.experimental.pallas import tpu as pltpu
from jax.sharding import PartitionSpec as P

HD = 64
BLK = 16
HALF = 32
OFFMAX = 16
SCALE = 1.0 / math.sqrt(HD)
LANES = 128


def shifted(block, axis, distance):
    devices = range(lax.axis_size(axis))
    route = [(i - distance, i) for i in devices if i - distance in devices]
    return lax.ppermute(block, axis, route)


def dot_nt(a, b):
    return lax.dot_general(a, b, (((1,), (1,)), ((), ())), preferred_element_type=jnp.float32)


def dot_tn(a, b):
    return lax.dot_general(a, b, (((0,), (0,)), ((), ())), preferred_element_type=jnp.float32)


def head_stack(x, heads):
    rows, width = x.shape
    lane_head = lax.broadcasted_iota(jnp.int32, (heads, 1, width), 2) // HD
    which = lax.broadcasted_iota(jnp.int32, (heads, 1, width), 0)
    kept = jnp.where(lane_head == which, x[None], jnp.zeros_like(x)[None])
    return kept.reshape(heads * rows, width)


def block_grads(q, g, k, v, bias):
    nq, width = q.shape
    heads = width // HD
    group = min(width, 2 * LANES)
    per_group = group // HD
    lanes = [slice(t * group, (t + 1) * group) for t in range(width // group)]
    qm = [head_stack(q[:, part], per_group) for part in lanes]
    gm = [head_stack(g[:, part], per_group) for part in lanes]
    full_bias = jnp.broadcast_to(bias[None], (heads,) + bias.shape).reshape(heads * nq, -1)
    s = jnp.concatenate([dot_nt(a, k[:, part]) for a, part in zip(qm, lanes)], axis=0)
    s = s * SCALE + full_bias
    mx = jnp.max(s, axis=1, keepdims=True)
    e = jnp.exp(s - mx)
    p = e / jnp.sum(e, axis=1, keepdims=True)
    pb = p.astype(jnp.bfloat16)
    gw = jnp.concatenate([dot_nt(a, v[:, part]) for a, part in zip(gm, lanes)], axis=0)
    delta = jnp.sum(pb.astype(jnp.float32) * gw, axis=1, keepdims=True)
    ds = (p * (gw - delta)).astype(jnp.bfloat16)
    rows = per_group * nq
    dk = jnp.concatenate(
        [dot_tn(ds[t * rows:(t + 1) * rows], a) for t, a in enumerate(qm)], axis=1
    ) * SCALE
    dv = jnp.concatenate(
        [dot_tn(pb[t * rows:(t + 1) * rows], a) for t, a in enumerate(gm)], axis=1
    )
    lane = lax.broadcasted_iota(jnp.int32, (1, LANES), 1)
    low = lane < HD
    tiles = []
    for pair in range(width // LANES):
        both = jnp.dot(
            ds[2 * pair * nq:(2 * pair + 2) * nq],
            k[:, pair * LANES:(pair + 1) * LANES],
            preferred_element_type=jnp.float32,
        )
        tiles.append(jnp.where(low, both[:nq], both[nq:]) * SCALE)
    dq = jnp.concatenate(tiles, axis=1)
    return dq, dk, dv


def fused_row_kernel(q_ref, g_ref, k_ref, v_ref, l2_ref, l1_ref, r1_ref, r2_ref, bias_ref,
                     qg_ref, kg_ref, vg_ref,
                     own_s, near_l, near_r, s_fl, s_fr, s_nl, s_nr, x_fr, x_fl,
                     x_nr, x_nl, far_send, far_recv_r, far_recv_l, near_send, near_recv):
    rows, cc, width = q_ref.shape
    w2 = l2_ref.shape[2]
    w1 = l1_ref.shape[2]
    n = lax.axis_size("rcol")
    me = lax.axis_index("rcol")
    here = (lax.axis_index("slide"), lax.axis_index("rrow"))
    mesh_ids = pl.DeviceIdType.MESH

    def dev(distance):
        return here + (lax.rem(me + distance + n, n),)

    barrier = pltpu.get_barrier_semaphore()
    for distance in (-1, 1):
        pl.semaphore_signal(barrier, 1, device_id=dev(distance), device_id_type=mesh_ids)
    pl.semaphore_wait(barrier, 2)

    def far_copy(r, to_left):
        if to_left:
            return pltpu.make_async_remote_copy(
                src_ref=s_fl.at[:, pl.ds(r, 1)], dst_ref=x_fr.at[:, pl.ds(r, 1)],
                send_sem=far_send.at[0], recv_sem=far_recv_r.at[r],
                device_id=dev(-1), device_id_type=mesh_ids)
        return pltpu.make_async_remote_copy(
            src_ref=s_fr.at[:, pl.ds(r, 1)], dst_ref=x_fl.at[:, pl.ds(r, 1)],
            send_sem=far_send.at[1], recv_sem=far_recv_l.at[r],
            device_id=dev(1), device_id_type=mesh_ids)

    def near_copy(r, to_left, whole=False):
        rs = slice(None) if whole else pl.ds(r, 1)
        if to_left:
            return pltpu.make_async_remote_copy(
                src_ref=s_nl.at[:, rs], dst_ref=x_nr.at[:, rs],
                send_sem=near_send.at[0], recv_sem=near_recv.at[0],
                device_id=dev(-1), device_id_type=mesh_ids)
        return pltpu.make_async_remote_copy(
            src_ref=s_nr.at[:, rs], dst_ref=x_nl.at[:, rs],
            send_sem=near_send.at[1], recv_sem=near_recv.at[1],
            device_id=dev(1), device_id_type=mesh_ids)

    def send_near(r):
        far_copy(r, True).wait_recv()
        far_copy(r, False).wait_recv()
        f32 = jnp.float32
        s_nl[:, r, :w1 - w2] = near_l[:, r, :w1 - w2].astype(jnp.bfloat16)
        s_nl[:, r, w1 - w2:] = (near_l[:, r, w1 - w2:] + x_fr[:, r].astype(f32)).astype(jnp.bfloat16)
        s_nr[:, r, :w2] = (near_r[:, r, :w2] + x_fl[:, r].astype(f32)).astype(jnp.bfloat16)
        s_nr[:, r, w2:] = near_r[:, r, w2:].astype(jnp.bfloat16)
        near_copy(r, True).start()
        near_copy(r, False).start()

    def row_step(r, carry):
        def span(which, own_ref):
            return jnp.concatenate(
                [l2_ref[which, r], l1_ref[which, r], own_ref[r], r1_ref[which, r],
                 r2_ref[which, r]],
                axis=0,
            )

        dq, dk, dv = block_grads(q_ref[r], g_ref[r], span(0, k_ref), span(1, v_ref), bias_ref[r])
        qg_ref[r] = dq
        for which, full in ((0, dk), (1, dv)):
            s_fl[which, r] = full[:w2].astype(jnp.bfloat16)
            near_l[which, r] = full[w2:w2 + w1]
            own_s[which, r] = full[w2 + w1:w2 + w1 + cc]
            near_r[which, r] = full[w2 + w1 + cc:w2 + 2 * w1 + cc]
            s_fr[which, r] = full[w2 + 2 * w1 + cc:].astype(jnp.bfloat16)
        far_copy(r, True).start()
        far_copy(r, False).start()

        @pl.when(r > 0)
        def _():
            send_near(r - 1)

        return carry

    lax.fori_loop(0, rows, row_step, 0)
    send_near(rows - 1)
    for src, dst, slot in ((s_fl, x_fr, 0), (s_fr, x_fl, 1)):
        pltpu.make_async_remote_copy(
            src_ref=src, dst_ref=dst, send_sem=far_send.at[slot], recv_sem=far_recv_r.at[0],
            device_id=dev(1 - 2 * (1 - slot)), device_id_type=mesh_ids).wait_send()
    for to_left in (True, False):
        near_copy(0, to_left, whole=True).wait()
    f32 = jnp.float32
    for which, out_ref in ((0, kg_ref), (1, vg_ref)):
        out_ref[...] = own_s[which] + x_nr[which].astype(f32) + x_nl[which].astype(f32)


def fused_row(queries, out_grad, key_grid, value_grid, l2, l1, r1, r2, bias):
    rows, cc, width = queries.shape
    w2 = l2.shape[2]
    w1 = l1.shape[2]
    vmem = pl.BlockSpec(memory_space=pltpu.VMEM)
    grads = jax.ShapeDtypeStruct((rows, cc, width), jnp.float32)
    bf = jnp.bfloat16
    f32 = jnp.float32
    return pl.pallas_call(
        fused_row_kernel,
        in_specs=[vmem] * 9,
        out_specs=[vmem] * 3,
        out_shape=(grads, grads, grads),
        scratch_shapes=[
            pltpu.VMEM((2, rows, cc, width), f32),
            pltpu.VMEM((2, rows, w1, width), f32),
            pltpu.VMEM((2, rows, w1, width), f32),
            pltpu.VMEM((2, rows, w2, width), bf),
            pltpu.VMEM((2, rows, w2, width), bf),
            pltpu.VMEM((2, rows, w1, width), bf),
            pltpu.VMEM((2, rows, w1, width), bf),
            pltpu.VMEM((2, rows, w2, width), bf),
            pltpu.VMEM((2, rows, w2, width), bf),
            pltpu.VMEM((2, rows, cc, width), bf),
            pltpu.VMEM((2, rows, cc, width), bf),
            pltpu.SemaphoreType.DMA((2,)),
            pltpu.SemaphoreType.DMA((rows,)),
            pltpu.SemaphoreType.DMA((rows,)),
            pltpu.SemaphoreType.DMA((2,)),
            pltpu.SemaphoreType.DMA((2,)),
        ],
        compiler_params=pltpu.CompilerParams(
            collective_id=0, has_side_effects=True, vmem_limit_bytes=60 * 1024 * 1024
        ),
    )(queries, out_grad, key_grid, value_grid, l2, l1, r1, r2, bias)


def column_kernel(x_ref, o_ref):
    groups, arrays, strip, rows, width = x_ref.shape
    per = max(1, LANES // (groups * rows))

    def joined(which):
        return jnp.concatenate(
            [x_ref[s, which, c] for c in range(per) for s in range(groups)], axis=0
        )

    whole_rows = groups * rows
    i = lax.broadcasted_iota(jnp.int32, (per * whole_rows, per * whole_rows), 0) // whole_rows
    j = lax.broadcasted_iota(jnp.int32, (per * whole_rows, per * whole_rows), 1) // whole_rows
    bias = jnp.where(i == j, 0.0, -jnp.inf).astype(jnp.float32)
    for step in range(strip // per):
        def pick(which):
            return jnp.concatenate(
                [x_ref[s, which, step * per + c] for c in range(per) for s in range(groups)],
                axis=0,
            )

        grads = block_grads(pick(0), pick(3), pick(1), pick(2), bias)
        for which, full in enumerate(grads):
            low = full.astype(jnp.bfloat16)
            for c in range(per):
                for s in range(groups):
                    start = c * whole_rows + s * rows
                    o_ref[s, which, step * per + c] = low[start:start + rows]


def column_attention(whole):
    groups, arrays, strip, rows, width = whole.shape
    vmem = pl.BlockSpec(memory_space=pltpu.VMEM)
    return pl.pallas_call(
        column_kernel,
        in_specs=[vmem],
        out_specs=vmem,
        out_shape=jax.ShapeDtypeStruct((groups, 3, strip, rows, width), jnp.bfloat16),
    )(whole)


def band_bias(mask_rows, offsets, first_col, grid_cols, block_cols):
    band_reach = HALF + OFFMAX
    query_cols = first_col + jnp.arange(block_cols, dtype=jnp.int32)
    key_cols = first_col - band_reach + jnp.arange(block_cols + 2 * band_reach, dtype=jnp.int32)
    inside = (key_cols >= 0) & (key_cols < grid_cols)
    key_block = jnp.clip(key_cols, 0, grid_cols - 1) // BLK
    block_ids = jnp.arange(mask_rows.shape[1], dtype=jnp.int32)
    key_open = jnp.sum(
        mask_rows[:, None, :]
        * (key_block[None, :, None] == block_ids[None, None, :]).astype(jnp.int32),
        axis=-1,
    )
    relative = key_cols[None, None, :] - query_cols[None, :, None] - offsets[:, None, None]
    same_block = key_cols[None, :] // BLK == query_cols[:, None] // BLK
    allowed = (
        (relative >= -HALF)
        & (relative < HALF)
        & inside[None, None, :]
        & ((key_open[:, None, :] > 0) | same_block[None])
    )
    return jnp.where(allowed, 0.0, -jnp.inf).astype(jnp.float32)


def body(queries, key_grid, value_grid, out_grad, tissue_mask, band_offset):
    row_count, col_count, feature_width = queries.shape
    group_count = lax.axis_size("rrow")
    band_reach = HALF + OFFMAX
    near = col_count
    far = band_reach - col_count

    strip = col_count // group_count
    stacked = (
        jnp.stack([queries, key_grid, value_grid, out_grad])
        .reshape(4, row_count, group_count, strip, feature_width)
        .transpose(2, 0, 3, 1, 4)
    )
    whole = lax.all_to_all(stacked, "rrow", split_axis=0, concat_axis=0, tiled=True)

    pair = jnp.stack([key_grid, value_grid])
    l1 = shifted(pair[:, :, col_count - near:], "rcol", 1)
    r1 = shifted(pair[:, :, :near], "rcol", -1)
    l2 = shifted(pair[:, :, col_count - far:], "rcol", 2)
    r2 = shifted(pair[:, :, :far], "rcol", -2)
    grid_cols = col_count * lax.axis_size("rcol")
    first_col = lax.axis_index("rcol") * col_count
    bias = band_bias(tissue_mask, band_offset, first_col, grid_cols, col_count)

    col_out = column_attention(whole)
    back = lax.all_to_all(col_out, "rrow", split_axis=0, concat_axis=0, tiled=True)
    row_grads = fused_row(queries, out_grad, key_grid, value_grid, l2, l1, r1, r2, bias)
    back = back.transpose(1, 3, 0, 2, 4).reshape(3, row_count, col_count, feature_width)
    back = back.astype(jnp.float32)
    return tuple((row + col).astype(jnp.bfloat16) for row, col in zip(row_grads, back))


def solution(mesh):
    in_specs = (
        P(("slide", "rrow"), "rcol", None),
        P(("slide", "rrow"), "rcol", None),
        P(("slide", "rrow"), "rcol", None),
        P(("slide", "rrow"), "rcol", None),
        P(("slide", "rrow"), None),
        P(("slide", "rrow")),
    )
    out_specs = (
        P(("slide", "rrow"), "rcol", None),
        P(("slide", "rrow"), "rcol", None),
        P(("slide", "rrow"), "rcol", None),
    )
    return jax.shard_map(body, mesh=mesh, in_specs=in_specs, out_specs=out_specs, check_vma=False)
```

```python
import functools
import math

import jax
import jax.numpy as jnp
from jax import lax
from jax.experimental import pallas as pl
from jax.experimental.pallas import tpu as pltpu
from jax.sharding import PartitionSpec as P

HD = 64
BLK = 16
HALF = 32
OFFMAX = 16
SCALE = 1.0 / math.sqrt(HD)
LANES = 128


def shifted(block, axis, distance):
    devices = range(lax.axis_size(axis))
    route = [(i - distance, i) for i in devices if i - distance in devices]
    return lax.ppermute(block, axis, route)


def dot_nt(a, b):
    return lax.dot_general(a, b, (((1,), (1,)), ((), ())), preferred_element_type=jnp.float32)


def dot_tn(a, b):
    return lax.dot_general(a, b, (((0,), (0,)), ((), ())), preferred_element_type=jnp.float32)


def head_stack(x, heads):
    rows, width = x.shape
    lane_head = lax.broadcasted_iota(jnp.int32, (heads, 1, width), 2) // HD
    which = lax.broadcasted_iota(jnp.int32, (heads, 1, width), 0)
    kept = jnp.where(lane_head == which, x[None], jnp.zeros_like(x)[None])
    return kept.reshape(heads * rows, width)


def block_grads(q, g, k, v, bias):
    nq, width = q.shape
    heads = width // HD
    group = min(width, 2 * LANES)
    per_group = group // HD
    lanes = [slice(t * group, (t + 1) * group) for t in range(width // group)]
    qm = [head_stack(q[:, part], per_group) for part in lanes]
    gm = [head_stack(g[:, part], per_group) for part in lanes]
    full_bias = jnp.broadcast_to(bias[None], (heads,) + bias.shape).reshape(heads * nq, -1)
    s = jnp.concatenate([dot_nt(a, k[:, part]) for a, part in zip(qm, lanes)], axis=0)
    s = s * SCALE + full_bias
    mx = jnp.max(s, axis=1, keepdims=True)
    e = jnp.exp(s - mx)
    p = e / jnp.sum(e, axis=1, keepdims=True)
    pb = p.astype(jnp.bfloat16)
    gw = jnp.concatenate([dot_nt(a, v[:, part]) for a, part in zip(gm, lanes)], axis=0)
    delta = jnp.sum(pb.astype(jnp.float32) * gw, axis=1, keepdims=True)
    ds = (p * (gw - delta)).astype(jnp.bfloat16)
    rows = per_group * nq
    dk = jnp.concatenate(
        [dot_tn(ds[t * rows:(t + 1) * rows], a) for t, a in enumerate(qm)], axis=1
    ) * SCALE
    dv = jnp.concatenate(
        [dot_tn(pb[t * rows:(t + 1) * rows], a) for t, a in enumerate(gm)], axis=1
    )
    lane = lax.broadcasted_iota(jnp.int32, (1, LANES), 1)
    low = lane < HD
    tiles = []
    for pair in range(width // LANES):
        both = jnp.dot(
            ds[2 * pair * nq:(2 * pair + 2) * nq],
            k[:, pair * LANES:(pair + 1) * LANES],
            preferred_element_type=jnp.float32,
        )
        tiles.append(jnp.where(low, both[:nq], both[nq:]) * SCALE)
    dq = jnp.concatenate(tiles, axis=1)
    return dq, dk, dv


def fused_row_kernel(w2, q_ref, g_ref, k_ref, v_ref, l1_ref, r1_ref, bias_ref,
                     qg_ref, kg_ref, vg_ref,
                     l2_ref, r2_ref, own_s, near_l, near_r, s_fl, s_fr, s_nl, s_nr, x_fr, x_fl,
                     x_nr, x_nl, halo_send, halo_recv_l, halo_recv_r, far_send, far_recv_r, far_recv_l,
                     near_send, near_recv):
    rows, cc, width = q_ref.shape
    w1 = l1_ref.shape[2]
    n = lax.axis_size("rcol")
    me = lax.axis_index("rcol")
    here = (lax.axis_index("slide"), lax.axis_index("rrow"))
    mesh_ids = pl.DeviceIdType.MESH

    def dev(distance):
        return here + (lax.rem(me + distance + n, n),)

    barrier = pltpu.get_barrier_semaphore()
    for distance in (-1, 1):
        pl.semaphore_signal(barrier, 1, device_id=dev(distance), device_id_type=mesh_ids)
    pl.semaphore_wait(barrier, 2)

    def relays(r, whole=False):
        rs = slice(None) if whole else pl.ds(r, 1)
        return (
            pltpu.make_async_remote_copy(
                src_ref=l1_ref.at[:, rs, pl.ds(w1 - w2, w2)], dst_ref=l2_ref.at[:, rs],
                send_sem=halo_send.at[0], recv_sem=halo_recv_l.at[r],
                device_id=dev(1), device_id_type=mesh_ids),
            pltpu.make_async_remote_copy(
                src_ref=r1_ref.at[:, rs, pl.ds(0, w2)], dst_ref=r2_ref.at[:, rs],
                send_sem=halo_send.at[1], recv_sem=halo_recv_r.at[r],
                device_id=dev(-1), device_id_type=mesh_ids),
        )

    for r in range(rows):
        for copy in relays(r):
            copy.start()

    def far_copy(r, to_left):
        if to_left:
            return pltpu.make_async_remote_copy(
                src_ref=s_fl.at[:, pl.ds(r, 1)], dst_ref=x_fr.at[:, pl.ds(r, 1)],
                send_sem=far_send.at[0], recv_sem=far_recv_r.at[r],
                device_id=dev(-1), device_id_type=mesh_ids)
        return pltpu.make_async_remote_copy(
            src_ref=s_fr.at[:, pl.ds(r, 1)], dst_ref=x_fl.at[:, pl.ds(r, 1)],
            send_sem=far_send.at[1], recv_sem=far_recv_l.at[r],
            device_id=dev(1), device_id_type=mesh_ids)

    def near_copy(r, to_left, whole=False):
        rs = slice(None) if whole else pl.ds(r, 1)
        if to_left:
            return pltpu.make_async_remote_copy(
                src_ref=s_nl.at[:, rs], dst_ref=x_nr.at[:, rs],
                send_sem=near_send.at[0], recv_sem=near_recv.at[0],
                device_id=dev(-1), device_id_type=mesh_ids)
        return pltpu.make_async_remote_copy(
            src_ref=s_nr.at[:, rs], dst_ref=x_nl.at[:, rs],
            send_sem=near_send.at[1], recv_sem=near_recv.at[1],
            device_id=dev(1), device_id_type=mesh_ids)

    def send_near(r):
        far_copy(r, True).wait_recv()
        far_copy(r, False).wait_recv()
        f32 = jnp.float32
        s_nl[:, r, :w1 - w2] = near_l[:, r, :w1 - w2].astype(jnp.bfloat16)
        s_nl[:, r, w1 - w2:] = (near_l[:, r, w1 - w2:] + x_fr[:, r].astype(f32)).astype(jnp.bfloat16)
        s_nr[:, r, :w2] = (near_r[:, r, :w2] + x_fl[:, r].astype(f32)).astype(jnp.bfloat16)
        s_nr[:, r, w2:] = near_r[:, r, w2:].astype(jnp.bfloat16)
        near_copy(r, True).start()
        near_copy(r, False).start()

    def row_step(r, carry):
        for copy in relays(r):
            copy.wait_recv()

        def span(which, own_ref):
            return jnp.concatenate(
                [l2_ref[which, r], l1_ref[which, r], own_ref[r], r1_ref[which, r],
                 r2_ref[which, r]],
                axis=0,
            )

        dq, dk, dv = block_grads(q_ref[r], g_ref[r], span(0, k_ref), span(1, v_ref), bias_ref[r])
        qg_ref[r] = dq
        for which, full in ((0, dk), (1, dv)):
            s_fl[which, r] = full[:w2].astype(jnp.bfloat16)
            near_l[which, r] = full[w2:w2 + w1]
            own_s[which, r] = full[w2 + w1:w2 + w1 + cc]
            near_r[which, r] = full[w2 + w1 + cc:w2 + 2 * w1 + cc]
            s_fr[which, r] = full[w2 + 2 * w1 + cc:].astype(jnp.bfloat16)
        far_copy(r, True).start()
        far_copy(r, False).start()

        @pl.when(r > 0)
        def _():
            send_near(r - 1)

        return carry

    lax.fori_loop(0, rows, row_step, 0)
    send_near(rows - 1)
    for copy in relays(0, whole=True):
        copy.wait_send()
    for src, dst, slot in ((s_fl, x_fr, 0), (s_fr, x_fl, 1)):
        pltpu.make_async_remote_copy(
            src_ref=src, dst_ref=dst, send_sem=far_send.at[slot], recv_sem=far_recv_r.at[0],
            device_id=dev(1 - 2 * (1 - slot)), device_id_type=mesh_ids).wait_send()
    for to_left in (True, False):
        near_copy(0, to_left, whole=True).wait()
    f32 = jnp.float32
    for which, out_ref in ((0, kg_ref), (1, vg_ref)):
        out_ref[...] = own_s[which] + x_nr[which].astype(f32) + x_nl[which].astype(f32)


def fused_row(queries, out_grad, key_grid, value_grid, l1, r1, bias, w2):
    rows, cc, width = queries.shape
    w1 = l1.shape[2]
    vmem = pl.BlockSpec(memory_space=pltpu.VMEM)
    grads = jax.ShapeDtypeStruct((rows, cc, width), jnp.float32)
    bf = jnp.bfloat16
    f32 = jnp.float32
    return pl.pallas_call(
        functools.partial(fused_row_kernel, w2),
        in_specs=[vmem] * 7,
        out_specs=[vmem] * 3,
        out_shape=(grads, grads, grads),
        scratch_shapes=[
            pltpu.VMEM((2, rows, w2, width), bf),
            pltpu.VMEM((2, rows, w2, width), bf),
            pltpu.VMEM((2, rows, cc, width), f32),
            pltpu.VMEM((2, rows, w1, width), f32),
            pltpu.VMEM((2, rows, w1, width), f32),
            pltpu.VMEM((2, rows, w2, width), bf),
            pltpu.VMEM((2, rows, w2, width), bf),
            pltpu.VMEM((2, rows, w1, width), bf),
            pltpu.VMEM((2, rows, w1, width), bf),
            pltpu.VMEM((2, rows, w2, width), bf),
            pltpu.VMEM((2, rows, w2, width), bf),
            pltpu.VMEM((2, rows, cc, width), bf),
            pltpu.VMEM((2, rows, cc, width), bf),
            pltpu.SemaphoreType.DMA((2,)),
            pltpu.SemaphoreType.DMA((rows,)),
            pltpu.SemaphoreType.DMA((rows,)),
            pltpu.SemaphoreType.DMA((2,)),
            pltpu.SemaphoreType.DMA((rows,)),
            pltpu.SemaphoreType.DMA((rows,)),
            pltpu.SemaphoreType.DMA((2,)),
            pltpu.SemaphoreType.DMA((2,)),
        ],
        compiler_params=pltpu.CompilerParams(
            collective_id=0, has_side_effects=True, vmem_limit_bytes=60 * 1024 * 1024
        ),
    )(queries, out_grad, key_grid, value_grid, l1, r1, bias)


def column_kernel(x_ref, o_ref):
    groups, arrays, strip, rows, width = x_ref.shape
    per = max(1, LANES // (groups * rows))

    def joined(which):
        return jnp.concatenate(
            [x_ref[s, which, c] for c in range(per) for s in range(groups)], axis=0
        )

    whole_rows = groups * rows
    i = lax.broadcasted_iota(jnp.int32, (per * whole_rows, per * whole_rows), 0) // whole_rows
    j = lax.broadcasted_iota(jnp.int32, (per * whole_rows, per * whole_rows), 1) // whole_rows
    bias = jnp.where(i == j, 0.0, -jnp.inf).astype(jnp.float32)
    for step in range(strip // per):
        def pick(which):
            return jnp.concatenate(
                [x_ref[s, which, step * per + c] for c in range(per) for s in range(groups)],
                axis=0,
            )

        grads = block_grads(pick(0), pick(3), pick(1), pick(2), bias)
        for which, full in enumerate(grads):
            low = full.astype(jnp.bfloat16)
            for c in range(per):
                for s in range(groups):
                    start = c * whole_rows + s * rows
                    o_ref[s, which, step * per + c] = low[start:start + rows]


def column_attention(whole):
    groups, arrays, strip, rows, width = whole.shape
    vmem = pl.BlockSpec(memory_space=pltpu.VMEM)
    return pl.pallas_call(
        column_kernel,
        in_specs=[vmem],
        out_specs=vmem,
        out_shape=jax.ShapeDtypeStruct((groups, 3, strip, rows, width), jnp.bfloat16),
    )(whole)


def band_bias(mask_rows, offsets, first_col, grid_cols, block_cols):
    band_reach = HALF + OFFMAX
    query_cols = first_col + jnp.arange(block_cols, dtype=jnp.int32)
    key_cols = first_col - band_reach + jnp.arange(block_cols + 2 * band_reach, dtype=jnp.int32)
    inside = (key_cols >= 0) & (key_cols < grid_cols)
    key_block = jnp.clip(key_cols, 0, grid_cols - 1) // BLK
    block_ids = jnp.arange(mask_rows.shape[1], dtype=jnp.int32)
    key_open = jnp.sum(
        mask_rows[:, None, :]
        * (key_block[None, :, None] == block_ids[None, None, :]).astype(jnp.int32),
        axis=-1,
    )
    relative = key_cols[None, None, :] - query_cols[None, :, None] - offsets[:, None, None]
    same_block = key_cols[None, :] // BLK == query_cols[:, None] // BLK
    allowed = (
        (relative >= -HALF)
        & (relative < HALF)
        & inside[None, None, :]
        & ((key_open[:, None, :] > 0) | same_block[None])
    )
    return jnp.where(allowed, 0.0, -jnp.inf).astype(jnp.float32)


def body(queries, key_grid, value_grid, out_grad, tissue_mask, band_offset):
    row_count, col_count, feature_width = queries.shape
    group_count = lax.axis_size("rrow")
    band_reach = HALF + OFFMAX
    near = col_count
    far = band_reach - col_count

    strip = col_count // group_count
    stacked = (
        jnp.stack([queries, key_grid, value_grid, out_grad])
        .reshape(4, row_count, group_count, strip, feature_width)
        .transpose(2, 0, 3, 1, 4)
    )
    whole = lax.all_to_all(stacked, "rrow", split_axis=0, concat_axis=0, tiled=True)

    pair = jnp.stack([key_grid, value_grid])
    l1 = shifted(pair[:, :, col_count - near:], "rcol", 1)
    r1 = shifted(pair[:, :, :near], "rcol", -1)
    grid_cols = col_count * lax.axis_size("rcol")
    first_col = lax.axis_index("rcol") * col_count
    bias = band_bias(tissue_mask, band_offset, first_col, grid_cols, col_count)

    col_out = column_attention(whole)
    back = lax.all_to_all(col_out, "rrow", split_axis=0, concat_axis=0, tiled=True)
    row_grads = fused_row(queries, out_grad, key_grid, value_grid, l1, r1, bias, far)
    back = back.transpose(1, 3, 0, 2, 4).reshape(3, row_count, col_count, feature_width)
    back = back.astype(jnp.float32)
    return tuple((row + col).astype(jnp.bfloat16) for row, col in zip(row_grads, back))


def solution(mesh):
    in_specs = (
        P(("slide", "rrow"), "rcol", None),
        P(("slide", "rrow"), "rcol", None),
        P(("slide", "rrow"), "rcol", None),
        P(("slide", "rrow"), "rcol", None),
        P(("slide", "rrow"), None),
        P(("slide", "rrow")),
    )
    out_specs = (
        P(("slide", "rrow"), "rcol", None),
        P(("slide", "rrow"), "rcol", None),
        P(("slide", "rrow"), "rcol", None),
    )
    return jax.shard_map(body, mesh=mesh, in_specs=in_specs, out_specs=out_specs, check_vma=False)
```

```python
import functools
import math

import jax
import jax.numpy as jnp
from jax import lax
from jax.experimental import pallas as pl
from jax.experimental.pallas import tpu as pltpu
from jax.sharding import PartitionSpec as P

HD = 64
BLK = 16
HALF = 32
OFFMAX = 16
SCALE = 1.0 / math.sqrt(HD)
LANES = 128


def shifted(block, axis, distance):
    devices = range(lax.axis_size(axis))
    route = [(i - distance, i) for i in devices if i - distance in devices]
    return lax.ppermute(block, axis, route)


def dot_nt(a, b):
    return lax.dot_general(a, b, (((1,), (1,)), ((), ())), preferred_element_type=jnp.float32)


def dot_tn(a, b):
    return lax.dot_general(a, b, (((0,), (0,)), ((), ())), preferred_element_type=jnp.float32)


def head_stack(x, heads):
    rows, width = x.shape
    lane_head = lax.broadcasted_iota(jnp.int32, (heads, 1, width), 2) // HD
    which = lax.broadcasted_iota(jnp.int32, (heads, 1, width), 0)
    kept = jnp.where(lane_head == which, x[None], jnp.zeros_like(x)[None])
    return kept.reshape(heads * rows, width)


def block_grads(q, g, k, v, bias):
    nq, width = q.shape
    heads = width // HD
    group = min(width, LANES)
    per_group = group // HD
    lanes = [slice(t * group, (t + 1) * group) for t in range(width // group)]
    qm = [head_stack(q[:, part], per_group) for part in lanes]
    gm = [head_stack(g[:, part], per_group) for part in lanes]
    full_bias = jnp.broadcast_to(bias[None], (heads,) + bias.shape).reshape(heads * nq, -1)
    s = jnp.concatenate([dot_nt(a, k[:, part]) for a, part in zip(qm, lanes)], axis=0)
    s = s * SCALE + full_bias
    mx = jnp.max(s, axis=1, keepdims=True)
    e = jnp.exp(s - mx)
    p = e / jnp.sum(e, axis=1, keepdims=True)
    pb = p.astype(jnp.bfloat16)
    gw = jnp.concatenate([dot_nt(a, v[:, part]) for a, part in zip(gm, lanes)], axis=0)
    delta = jnp.sum(pb.astype(jnp.float32) * gw, axis=1, keepdims=True)
    ds = (p * (gw - delta)).astype(jnp.bfloat16)
    rows = per_group * nq
    dk = jnp.concatenate(
        [dot_tn(ds[t * rows:(t + 1) * rows], a) for t, a in enumerate(qm)], axis=1
    ) * SCALE
    dv = jnp.concatenate(
        [dot_tn(pb[t * rows:(t + 1) * rows], a) for t, a in enumerate(gm)], axis=1
    )
    lane = lax.broadcasted_iota(jnp.int32, (1, LANES), 1)
    low = lane < HD
    tiles = []
    for pair in range(width // LANES):
        both = jnp.dot(
            ds[2 * pair * nq:(2 * pair + 2) * nq],
            k[:, pair * LANES:(pair + 1) * LANES],
            preferred_element_type=jnp.float32,
        )
        tiles.append(jnp.where(low, both[:nq], both[nq:]) * SCALE)
    dq = jnp.concatenate(tiles, axis=1)
    return dq, dk, dv


def fused_row_kernel(w2, q_ref, g_ref, k_ref, v_ref, l1_ref, r1_ref, bias_ref,
                     qg_ref, kg_ref, vg_ref,
                     l2_ref, r2_ref, own_s, near_l, near_r, s_fl, s_fr, s_nl, s_nr, x_fr, x_fl,
                     x_nr, x_nl, halo_send, halo_recv_l, halo_recv_r, far_send, far_recv_r, far_recv_l,
                     near_send, near_recv):
    rows, cc, width = q_ref.shape
    w1 = l1_ref.shape[2]
    n = lax.axis_size("rcol")
    me = lax.axis_index("rcol")
    here = (lax.axis_index("slide"), lax.axis_index("rrow"))
    mesh_ids = pl.DeviceIdType.MESH

    def dev(distance):
        return here + (lax.rem(me + distance + n, n),)

    barrier = pltpu.get_barrier_semaphore()
    for distance in (-1, 1):
        pl.semaphore_signal(barrier, 1, device_id=dev(distance), device_id_type=mesh_ids)
    pl.semaphore_wait(barrier, 2)

    def relays(r, whole=False):
        rs = slice(None) if whole else pl.ds(r, 1)
        return (
            pltpu.make_async_remote_copy(
                src_ref=l1_ref.at[:, rs, pl.ds(w1 - w2, w2)], dst_ref=l2_ref.at[:, rs],
                send_sem=halo_send.at[0], recv_sem=halo_recv_l.at[r],
                device_id=dev(1), device_id_type=mesh_ids),
            pltpu.make_async_remote_copy(
                src_ref=r1_ref.at[:, rs, pl.ds(0, w2)], dst_ref=r2_ref.at[:, rs],
                send_sem=halo_send.at[1], recv_sem=halo_recv_r.at[r],
                device_id=dev(-1), device_id_type=mesh_ids),
        )

    for r in range(rows):
        for copy in relays(r):
            copy.start()

    def far_copy(r, to_left):
        if to_left:
            return pltpu.make_async_remote_copy(
                src_ref=s_fl.at[:, pl.ds(r, 1)], dst_ref=x_fr.at[:, pl.ds(r, 1)],
                send_sem=far_send.at[0], recv_sem=far_recv_r.at[r],
                device_id=dev(-1), device_id_type=mesh_ids)
        return pltpu.make_async_remote_copy(
            src_ref=s_fr.at[:, pl.ds(r, 1)], dst_ref=x_fl.at[:, pl.ds(r, 1)],
            send_sem=far_send.at[1], recv_sem=far_recv_l.at[r],
            device_id=dev(1), device_id_type=mesh_ids)

    def near_copy(r, to_left, whole=False):
        rs = slice(None) if whole else pl.ds(r, 1)
        if to_left:
            return pltpu.make_async_remote_copy(
                src_ref=s_nl.at[:, rs], dst_ref=x_nr.at[:, rs],
                send_sem=near_send.at[0], recv_sem=near_recv.at[0],
                device_id=dev(-1), device_id_type=mesh_ids)
        return pltpu.make_async_remote_copy(
            src_ref=s_nr.at[:, rs], dst_ref=x_nl.at[:, rs],
            send_sem=near_send.at[1], recv_sem=near_recv.at[1],
            device_id=dev(1), device_id_type=mesh_ids)

    def send_near(r):
        far_copy(r, True).wait_recv()
        far_copy(r, False).wait_recv()
        f32 = jnp.float32
        s_nl[:, r, :w1 - w2] = near_l[:, r, :w1 - w2].astype(jnp.bfloat16)
        s_nl[:, r, w1 - w2:] = (near_l[:, r, w1 - w2:] + x_fr[:, r].astype(f32)).astype(jnp.bfloat16)
        s_nr[:, r, :w2] = (near_r[:, r, :w2] + x_fl[:, r].astype(f32)).astype(jnp.bfloat16)
        s_nr[:, r, w2:] = near_r[:, r, w2:].astype(jnp.bfloat16)
        near_copy(r, True).start()
        near_copy(r, False).start()

    def row_step(r, carry):
        for copy in relays(r):
            copy.wait_recv()

        def span(which, own_ref):
            return jnp.concatenate(
                [l2_ref[which, r], l1_ref[which, r], own_ref[r], r1_ref[which, r],
                 r2_ref[which, r]],
                axis=0,
            )

        dq, dk, dv = block_grads(q_ref[r], g_ref[r], span(0, k_ref), span(1, v_ref), bias_ref[r])
        qg_ref[r] = dq
        for which, full in ((0, dk), (1, dv)):
            s_fl[which, r] = full[:w2].astype(jnp.bfloat16)
            near_l[which, r] = full[w2:w2 + w1]
            own_s[which, r] = full[w2 + w1:w2 + w1 + cc]
            near_r[which, r] = full[w2 + w1 + cc:w2 + 2 * w1 + cc]
            s_fr[which, r] = full[w2 + 2 * w1 + cc:].astype(jnp.bfloat16)
        far_copy(r, True).start()
        far_copy(r, False).start()

        @pl.when(r > 0)
        def _():
            send_near(r - 1)

        return carry

    lax.fori_loop(0, rows, row_step, 0)
    send_near(rows - 1)
    for copy in relays(0, whole=True):
        copy.wait_send()
    for src, dst, slot in ((s_fl, x_fr, 0), (s_fr, x_fl, 1)):
        pltpu.make_async_remote_copy(
            src_ref=src, dst_ref=dst, send_sem=far_send.at[slot], recv_sem=far_recv_r.at[0],
            device_id=dev(1 - 2 * (1 - slot)), device_id_type=mesh_ids).wait_send()
    for to_left in (True, False):
        near_copy(0, to_left, whole=True).wait()
    f32 = jnp.float32
    for which, out_ref in ((0, kg_ref), (1, vg_ref)):
        out_ref[...] = own_s[which] + x_nr[which].astype(f32) + x_nl[which].astype(f32)


def fused_row(queries, out_grad, key_grid, value_grid, l1, r1, bias, w2):
    rows, cc, width = queries.shape
    w1 = l1.shape[2]
    vmem = pl.BlockSpec(memory_space=pltpu.VMEM)
    grads = jax.ShapeDtypeStruct((rows, cc, width), jnp.float32)
    bf = jnp.bfloat16
    f32 = jnp.float32
    return pl.pallas_call(
        functools.partial(fused_row_kernel, w2),
        in_specs=[vmem] * 7,
        out_specs=[vmem] * 3,
        out_shape=(grads, grads, grads),
        scratch_shapes=[
            pltpu.VMEM((2, rows, w2, width), bf),
            pltpu.VMEM((2, rows, w2, width), bf),
            pltpu.VMEM((2, rows, cc, width), f32),
            pltpu.VMEM((2, rows, w1, width), f32),
            pltpu.VMEM((2, rows, w1, width), f32),
            pltpu.VMEM((2, rows, w2, width), bf),
            pltpu.VMEM((2, rows, w2, width), bf),
            pltpu.VMEM((2, rows, w1, width), bf),
            pltpu.VMEM((2, rows, w1, width), bf),
            pltpu.VMEM((2, rows, w2, width), bf),
            pltpu.VMEM((2, rows, w2, width), bf),
            pltpu.VMEM((2, rows, cc, width), bf),
            pltpu.VMEM((2, rows, cc, width), bf),
            pltpu.SemaphoreType.DMA((2,)),
            pltpu.SemaphoreType.DMA((rows,)),
            pltpu.SemaphoreType.DMA((rows,)),
            pltpu.SemaphoreType.DMA((2,)),
            pltpu.SemaphoreType.DMA((rows,)),
            pltpu.SemaphoreType.DMA((rows,)),
            pltpu.SemaphoreType.DMA((2,)),
            pltpu.SemaphoreType.DMA((2,)),
        ],
        compiler_params=pltpu.CompilerParams(
            collective_id=0, has_side_effects=True, vmem_limit_bytes=60 * 1024 * 1024
        ),
    )(queries, out_grad, key_grid, value_grid, l1, r1, bias)


def column_kernel(x_ref, o_ref):
    groups, arrays, strip, rows, width = x_ref.shape
    per = max(1, LANES // (groups * rows))

    def joined(which):
        return jnp.concatenate(
            [x_ref[s, which, c] for c in range(per) for s in range(groups)], axis=0
        )

    whole_rows = groups * rows
    i = lax.broadcasted_iota(jnp.int32, (per * whole_rows, per * whole_rows), 0) // whole_rows
    j = lax.broadcasted_iota(jnp.int32, (per * whole_rows, per * whole_rows), 1) // whole_rows
    bias = jnp.where(i == j, 0.0, -jnp.inf).astype(jnp.float32)
    for step in range(strip // per):
        def pick(which):
            return jnp.concatenate(
                [x_ref[s, which, step * per + c] for c in range(per) for s in range(groups)],
                axis=0,
            )

        grads = block_grads(pick(0), pick(3), pick(1), pick(2), bias)
        for which, full in enumerate(grads):
            low = full.astype(jnp.bfloat16)
            for c in range(per):
                for s in range(groups):
                    start = c * whole_rows + s * rows
                    o_ref[s, which, step * per + c] = low[start:start + rows]


def column_attention(whole):
    groups, arrays, strip, rows, width = whole.shape
    vmem = pl.BlockSpec(memory_space=pltpu.VMEM)
    return pl.pallas_call(
        column_kernel,
        in_specs=[vmem],
        out_specs=vmem,
        out_shape=jax.ShapeDtypeStruct((groups, 3, strip, rows, width), jnp.bfloat16),
    )(whole)


def band_bias(mask_rows, offsets, first_col, grid_cols, block_cols):
    band_reach = HALF + OFFMAX
    query_cols = first_col + jnp.arange(block_cols, dtype=jnp.int32)
    key_cols = first_col - band_reach + jnp.arange(block_cols + 2 * band_reach, dtype=jnp.int32)
    inside = (key_cols >= 0) & (key_cols < grid_cols)
    key_block = jnp.clip(key_cols, 0, grid_cols - 1) // BLK
    block_ids = jnp.arange(mask_rows.shape[1], dtype=jnp.int32)
    key_open = jnp.sum(
        mask_rows[:, None, :]
        * (key_block[None, :, None] == block_ids[None, None, :]).astype(jnp.int32),
        axis=-1,
    )
    relative = key_cols[None, None, :] - query_cols[None, :, None] - offsets[:, None, None]
    same_block = key_cols[None, :] // BLK == query_cols[:, None] // BLK
    allowed = (
        (relative >= -HALF)
        & (relative < HALF)
        & inside[None, None, :]
        & ((key_open[:, None, :] > 0) | same_block[None])
    )
    return jnp.where(allowed, 0.0, -jnp.inf).astype(jnp.float32)


def body(queries, key_grid, value_grid, out_grad, tissue_mask, band_offset):
    row_count, col_count, feature_width = queries.shape
    group_count = lax.axis_size("rrow")
    band_reach = HALF + OFFMAX
    near = col_count
    far = band_reach - col_count

    strip = col_count // group_count
    stacked = (
        jnp.stack([queries, key_grid, value_grid, out_grad])
        .reshape(4, row_count, group_count, strip, feature_width)
        .transpose(2, 0, 3, 1, 4)
    )
    whole = lax.all_to_all(stacked, "rrow", split_axis=0, concat_axis=0, tiled=True)

    pair = jnp.stack([key_grid, value_grid])
    l1 = shifted(pair[:, :, col_count - near:], "rcol", 1)
    r1 = shifted(pair[:, :, :near], "rcol", -1)
    grid_cols = col_count * lax.axis_size("rcol")
    first_col = lax.axis_index("rcol") * col_count
    bias = band_bias(tissue_mask, band_offset, first_col, grid_cols, col_count)

    col_out = column_attention(whole)
    back = lax.all_to_all(col_out, "rrow", split_axis=0, concat_axis=0, tiled=True)
    row_grads = fused_row(queries, out_grad, key_grid, value_grid, l1, r1, bias, far)
    back = back.transpose(1, 3, 0, 2, 4).reshape(3, row_count, col_count, feature_width)
    back = back.astype(jnp.float32)
    return tuple((row + col).astype(jnp.bfloat16) for row, col in zip(row_grads, back))


def solution(mesh):
    in_specs = (
        P(("slide", "rrow"), "rcol", None),
        P(("slide", "rrow"), "rcol", None),
        P(("slide", "rrow"), "rcol", None),
        P(("slide", "rrow"), "rcol", None),
        P(("slide", "rrow"), None),
        P(("slide", "rrow")),
    )
    out_specs = (
        P(("slide", "rrow"), "rcol", None),
        P(("slide", "rrow"), "rcol", None),
        P(("slide", "rrow"), "rcol", None),
    )
    return jax.shard_map(body, mesh=mesh, in_specs=in_specs, out_specs=out_specs, check_vma=False)
```

```python
import functools
import math

import jax
import jax.numpy as jnp
from jax import lax
from jax.experimental import pallas as pl
from jax.experimental.pallas import tpu as pltpu
from jax.sharding import PartitionSpec as P

HD = 64
BLK = 16
HALF = 32
OFFMAX = 16
SCALE = 1.0 / math.sqrt(HD)
LANES = 128


def shifted(block, axis, distance):
    devices = range(lax.axis_size(axis))
    route = [(i - distance, i) for i in devices if i - distance in devices]
    return lax.ppermute(block, axis, route)


def dot_nt(a, b):
    return lax.dot_general(a, b, (((1,), (1,)), ((), ())), preferred_element_type=jnp.float32)


def dot_tn(a, b):
    return lax.dot_general(a, b, (((0,), (0,)), ((), ())), preferred_element_type=jnp.float32)


def head_stack(x, heads):
    rows, width = x.shape
    lane_head = lax.broadcasted_iota(jnp.int32, (heads, 1, width), 2) // HD
    which = lax.broadcasted_iota(jnp.int32, (heads, 1, width), 0)
    kept = jnp.where(lane_head == which, x[None], jnp.zeros_like(x)[None])
    return kept.reshape(heads * rows, width)


def block_grads(q, g, k, v, bias):
    nq, width = q.shape
    heads = width // HD
    group = min(width, 2 * LANES)
    per_group = group // HD
    lanes = [slice(t * group, (t + 1) * group) for t in range(width // group)]
    qm = [head_stack(q[:, part], per_group) for part in lanes]
    gm = [head_stack(g[:, part], per_group) for part in lanes]
    full_bias = jnp.broadcast_to(bias[None], (heads,) + bias.shape).reshape(heads * nq, -1)
    s = jnp.concatenate([dot_nt(a, k[:, part]) for a, part in zip(qm, lanes)], axis=0)
    s = s * SCALE + full_bias
    mx = jnp.max(s, axis=1, keepdims=True)
    e = jnp.exp(s - mx)
    p = e / jnp.sum(e, axis=1, keepdims=True)
    pb = p.astype(jnp.bfloat16)
    gw = jnp.concatenate([dot_nt(a, v[:, part]) for a, part in zip(gm, lanes)], axis=0)
    delta = jnp.sum(pb.astype(jnp.float32) * gw, axis=1, keepdims=True)
    ds = (p * (gw - delta)).astype(jnp.bfloat16)
    rows = per_group * nq
    dk = jnp.concatenate(
        [dot_tn(ds[t * rows:(t + 1) * rows], a) for t, a in enumerate(qm)], axis=1
    ) * SCALE
    dv = jnp.concatenate(
        [dot_tn(pb[t * rows:(t + 1) * rows], a) for t, a in enumerate(gm)], axis=1
    )
    lane = lax.broadcasted_iota(jnp.int32, (1, LANES), 1)
    low = lane < HD
    tiles = []
    for pair in range(width // LANES):
        both = jnp.dot(
            ds[2 * pair * nq:(2 * pair + 2) * nq],
            k[:, pair * LANES:(pair + 1) * LANES],
            preferred_element_type=jnp.float32,
        )
        tiles.append(jnp.where(low, both[:nq], both[nq:]) * SCALE)
    dq = jnp.concatenate(tiles, axis=1)
    return dq, dk, dv


def fused_row_kernel(w2, q_ref, g_ref, k_ref, v_ref, l1_ref, r1_ref, bias_ref,
                     out_ref,
                     l2_ref, r2_ref, own_s, near_l, near_r, s_fl, s_fr, s_nl, s_nr, x_fr, x_fl,
                     x_nr, x_nl, halo_send, halo_recv_l, halo_recv_r, far_send, far_recv_r, far_recv_l,
                     near_send, near_recv):
    rows, cc, width = q_ref.shape
    w1 = l1_ref.shape[2]
    n = lax.axis_size("rcol")
    me = lax.axis_index("rcol")
    here = (lax.axis_index("slide"), lax.axis_index("rrow"))
    mesh_ids = pl.DeviceIdType.MESH

    def dev(distance):
        return here + (lax.rem(me + distance + n, n),)

    barrier = pltpu.get_barrier_semaphore()
    for distance in (-1, 1):
        pl.semaphore_signal(barrier, 1, device_id=dev(distance), device_id_type=mesh_ids)
    pl.semaphore_wait(barrier, 2)

    def relays(r, whole=False):
        rs = slice(None) if whole else pl.ds(r, 1)
        return (
            pltpu.make_async_remote_copy(
                src_ref=l1_ref.at[:, rs, pl.ds(w1 - w2, w2)], dst_ref=l2_ref.at[:, rs],
                send_sem=halo_send.at[0], recv_sem=halo_recv_l.at[r],
                device_id=dev(1), device_id_type=mesh_ids),
            pltpu.make_async_remote_copy(
                src_ref=r1_ref.at[:, rs, pl.ds(0, w2)], dst_ref=r2_ref.at[:, rs],
                send_sem=halo_send.at[1], recv_sem=halo_recv_r.at[r],
                device_id=dev(-1), device_id_type=mesh_ids),
        )

    for r in range(rows):
        for copy in relays(r):
            copy.start()

    def far_copy(r, to_left):
        if to_left:
            return pltpu.make_async_remote_copy(
                src_ref=s_fl.at[:, pl.ds(r, 1)], dst_ref=x_fr.at[:, pl.ds(r, 1)],
                send_sem=far_send.at[0], recv_sem=far_recv_r.at[r],
                device_id=dev(-1), device_id_type=mesh_ids)
        return pltpu.make_async_remote_copy(
            src_ref=s_fr.at[:, pl.ds(r, 1)], dst_ref=x_fl.at[:, pl.ds(r, 1)],
            send_sem=far_send.at[1], recv_sem=far_recv_l.at[r],
            device_id=dev(1), device_id_type=mesh_ids)

    def near_copy(r, to_left, whole=False):
        rs = slice(None) if whole else pl.ds(r, 1)
        if to_left:
            return pltpu.make_async_remote_copy(
                src_ref=s_nl.at[:, rs], dst_ref=x_nr.at[:, rs],
                send_sem=near_send.at[0], recv_sem=near_recv.at[0],
                device_id=dev(-1), device_id_type=mesh_ids)
        return pltpu.make_async_remote_copy(
            src_ref=s_nr.at[:, rs], dst_ref=x_nl.at[:, rs],
            send_sem=near_send.at[1], recv_sem=near_recv.at[1],
            device_id=dev(1), device_id_type=mesh_ids)

    def send_near(r):
        far_copy(r, True).wait_recv()
        far_copy(r, False).wait_recv()
        f32 = jnp.float32
        s_nl[:, r, :w1 - w2] = near_l[:, r, :w1 - w2].astype(jnp.bfloat16)
        s_nl[:, r, w1 - w2:] = (near_l[:, r, w1 - w2:] + x_fr[:, r].astype(f32)).astype(jnp.bfloat16)
        s_nr[:, r, :w2] = (near_r[:, r, :w2] + x_fl[:, r].astype(f32)).astype(jnp.bfloat16)
        s_nr[:, r, w2:] = near_r[:, r, w2:].astype(jnp.bfloat16)
        near_copy(r, True).start()
        near_copy(r, False).start()

    def row_step(r, carry):
        for copy in relays(r):
            copy.wait_recv()

        def span(which, own_ref):
            return jnp.concatenate(
                [l2_ref[which, r], l1_ref[which, r], own_ref[r], r1_ref[which, r],
                 r2_ref[which, r]],
                axis=0,
            )

        dq, dk, dv = block_grads(q_ref[r], g_ref[r], span(0, k_ref), span(1, v_ref), bias_ref[r])
        out_ref[0, r] = dq
        for which, full in ((0, dk), (1, dv)):
            s_fl[which, r] = full[:w2].astype(jnp.bfloat16)
            near_l[which, r] = full[w2:w2 + w1]
            own_s[which, r] = full[w2 + w1:w2 + w1 + cc]
            near_r[which, r] = full[w2 + w1 + cc:w2 + 2 * w1 + cc]
            s_fr[which, r] = full[w2 + 2 * w1 + cc:].astype(jnp.bfloat16)
        far_copy(r, True).start()
        far_copy(r, False).start()

        @pl.when(r > 0)
        def _():
            send_near(r - 1)

        return carry

    lax.fori_loop(0, rows, row_step, 0)
    send_near(rows - 1)
    for copy in relays(0, whole=True):
        copy.wait_send()
    for src, dst, slot in ((s_fl, x_fr, 0), (s_fr, x_fl, 1)):
        pltpu.make_async_remote_copy(
            src_ref=src, dst_ref=dst, send_sem=far_send.at[slot], recv_sem=far_recv_r.at[0],
            device_id=dev(1 - 2 * (1 - slot)), device_id_type=mesh_ids).wait_send()
    for to_left in (True, False):
        near_copy(0, to_left, whole=True).wait()
    f32 = jnp.float32
    for which in (0, 1):
        out_ref[which + 1] = own_s[which] + x_nr[which].astype(f32) + x_nl[which].astype(f32)


def fused_row(queries, out_grad, key_grid, value_grid, l1, r1, bias, w2):
    rows, cc, width = queries.shape
    w1 = l1.shape[2]
    vmem = pl.BlockSpec(memory_space=pltpu.VMEM)
    grads = jax.ShapeDtypeStruct((3, rows, cc, width), jnp.float32)
    bf = jnp.bfloat16
    f32 = jnp.float32
    return pl.pallas_call(
        functools.partial(fused_row_kernel, w2),
        in_specs=[vmem] * 7,
        out_specs=vmem,
        out_shape=grads,
        scratch_shapes=[
            pltpu.VMEM((2, rows, w2, width), bf),
            pltpu.VMEM((2, rows, w2, width), bf),
            pltpu.VMEM((2, rows, cc, width), f32),
            pltpu.VMEM((2, rows, w1, width), f32),
            pltpu.VMEM((2, rows, w1, width), f32),
            pltpu.VMEM((2, rows, w2, width), bf),
            pltpu.VMEM((2, rows, w2, width), bf),
            pltpu.VMEM((2, rows, w1, width), bf),
            pltpu.VMEM((2, rows, w1, width), bf),
            pltpu.VMEM((2, rows, w2, width), bf),
            pltpu.VMEM((2, rows, w2, width), bf),
            pltpu.VMEM((2, rows, cc, width), bf),
            pltpu.VMEM((2, rows, cc, width), bf),
            pltpu.SemaphoreType.DMA((2,)),
            pltpu.SemaphoreType.DMA((rows,)),
            pltpu.SemaphoreType.DMA((rows,)),
            pltpu.SemaphoreType.DMA((2,)),
            pltpu.SemaphoreType.DMA((rows,)),
            pltpu.SemaphoreType.DMA((rows,)),
            pltpu.SemaphoreType.DMA((2,)),
            pltpu.SemaphoreType.DMA((2,)),
        ],
        compiler_params=pltpu.CompilerParams(
            collective_id=0, has_side_effects=True, vmem_limit_bytes=60 * 1024 * 1024
        ),
    )(queries, out_grad, key_grid, value_grid, l1, r1, bias)


def column_kernel(x_ref, o_ref):
    groups, arrays, strip, rows, width = x_ref.shape
    per = max(1, LANES // (groups * rows))

    def joined(which):
        return jnp.concatenate(
            [x_ref[s, which, c] for c in range(per) for s in range(groups)], axis=0
        )

    whole_rows = groups * rows
    i = lax.broadcasted_iota(jnp.int32, (per * whole_rows, per * whole_rows), 0) // whole_rows
    j = lax.broadcasted_iota(jnp.int32, (per * whole_rows, per * whole_rows), 1) // whole_rows
    bias = jnp.where(i == j, 0.0, -jnp.inf).astype(jnp.float32)
    for step in range(strip // per):
        def pick(which):
            return jnp.concatenate(
                [x_ref[s, which, step * per + c] for c in range(per) for s in range(groups)],
                axis=0,
            )

        grads = block_grads(pick(0), pick(3), pick(1), pick(2), bias)
        for which, full in enumerate(grads):
            low = full.astype(jnp.bfloat16)
            for c in range(per):
                for s in range(groups):
                    start = c * whole_rows + s * rows
                    o_ref[s, which, step * per + c] = low[start:start + rows]


def column_attention(whole):
    groups, arrays, strip, rows, width = whole.shape
    vmem = pl.BlockSpec(memory_space=pltpu.VMEM)
    return pl.pallas_call(
        column_kernel,
        in_specs=[vmem],
        out_specs=vmem,
        out_shape=jax.ShapeDtypeStruct((groups, 3, strip, rows, width), jnp.bfloat16),
    )(whole)


def band_bias(mask_rows, offsets, first_col, grid_cols, block_cols):
    band_reach = HALF + OFFMAX
    query_cols = first_col + jnp.arange(block_cols, dtype=jnp.int32)
    key_cols = first_col - band_reach + jnp.arange(block_cols + 2 * band_reach, dtype=jnp.int32)
    inside = (key_cols >= 0) & (key_cols < grid_cols)
    key_block = jnp.clip(key_cols, 0, grid_cols - 1) // BLK
    block_ids = jnp.arange(mask_rows.shape[1], dtype=jnp.int32)
    key_open = jnp.sum(
        mask_rows[:, None, :]
        * (key_block[None, :, None] == block_ids[None, None, :]).astype(jnp.int32),
        axis=-1,
    )
    relative = key_cols[None, None, :] - query_cols[None, :, None] - offsets[:, None, None]
    same_block = key_cols[None, :] // BLK == query_cols[:, None] // BLK
    allowed = (
        (relative >= -HALF)
        & (relative < HALF)
        & inside[None, None, :]
        & ((key_open[:, None, :] > 0) | same_block[None])
    )
    return jnp.where(allowed, 0.0, -jnp.inf).astype(jnp.float32)


def body(queries, key_grid, value_grid, out_grad, tissue_mask, band_offset):
    row_count, col_count, feature_width = queries.shape
    group_count = lax.axis_size("rrow")
    band_reach = HALF + OFFMAX
    near = col_count
    far = band_reach - col_count

    strip = col_count // group_count
    stacked = (
        jnp.stack([queries, key_grid, value_grid, out_grad])
        .reshape(4, row_count, group_count, strip, feature_width)
        .transpose(2, 0, 3, 1, 4)
    )
    whole = lax.all_to_all(stacked, "rrow", split_axis=0, concat_axis=0, tiled=True)

    pair = jnp.stack([key_grid, value_grid])
    l1 = shifted(pair[:, :, col_count - near:], "rcol", 1)
    r1 = shifted(pair[:, :, :near], "rcol", -1)
    grid_cols = col_count * lax.axis_size("rcol")
    first_col = lax.axis_index("rcol") * col_count
    bias = band_bias(tissue_mask, band_offset, first_col, grid_cols, col_count)

    col_out = column_attention(whole)
    back = lax.all_to_all(col_out, "rrow", split_axis=0, concat_axis=0, tiled=True)
    row_grads = fused_row(queries, out_grad, key_grid, value_grid, l1, r1, bias, far)
    back = back.transpose(1, 3, 0, 2, 4).reshape(3, row_count, col_count, feature_width)
    back = back.astype(jnp.float32)
    total = (row_grads + back).astype(jnp.bfloat16)
    return (total[0], total[1], total[2])


def solution(mesh):
    in_specs = (
        P(("slide", "rrow"), "rcol", None),
        P(("slide", "rrow"), "rcol", None),
        P(("slide", "rrow"), "rcol", None),
        P(("slide", "rrow"), "rcol", None),
        P(("slide", "rrow"), None),
        P(("slide", "rrow")),
    )
    out_specs = (
        P(("slide", "rrow"), "rcol", None),
        P(("slide", "rrow"), "rcol", None),
        P(("slide", "rrow"), "rcol", None),
    )
    return jax.shard_map(body, mesh=mesh, in_specs=in_specs, out_specs=out_specs, check_vma=False)
```

```python
import functools
import math

import jax
import jax.numpy as jnp
from jax import lax
from jax.experimental import pallas as pl
from jax.experimental.pallas import tpu as pltpu
from jax.sharding import PartitionSpec as P

HD = 64
BLK = 16
HALF = 32
OFFMAX = 16
SCALE = 1.0 / math.sqrt(HD)
LANES = 128


def shifted(block, axis, distance):
    devices = range(lax.axis_size(axis))
    route = [(i - distance, i) for i in devices if i - distance in devices]
    return lax.ppermute(block, axis, route)


def dot_nt(a, b):
    return lax.dot_general(a, b, (((1,), (1,)), ((), ())), preferred_element_type=jnp.float32)


def dot_tn(a, b):
    return lax.dot_general(a, b, (((0,), (0,)), ((), ())), preferred_element_type=jnp.float32)


def head_stack(x, heads):
    rows, width = x.shape
    lane_head = lax.broadcasted_iota(jnp.int32, (heads, 1, width), 2) // HD
    which = lax.broadcasted_iota(jnp.int32, (heads, 1, width), 0)
    kept = jnp.where(lane_head == which, x[None], jnp.zeros_like(x)[None])
    return kept.reshape(heads * rows, width)


def block_grads(q, g, k, v, bias):
    nq, width = q.shape
    heads = width // HD
    group = min(width, 2 * LANES)
    per_group = group // HD
    lanes = [slice(t * group, (t + 1) * group) for t in range(width // group)]
    qm = [head_stack(q[:, part], per_group) for part in lanes]
    gm = [head_stack(g[:, part], per_group) for part in lanes]
    full_bias = jnp.broadcast_to(bias[None], (heads,) + bias.shape).reshape(heads * nq, -1)
    s = jnp.concatenate([dot_nt(a, k[:, part]) for a, part in zip(qm, lanes)], axis=0)
    s = s * SCALE + full_bias
    mx = jnp.max(s, axis=1, keepdims=True)
    e = jnp.exp(s - mx)
    p = e / jnp.sum(e, axis=1, keepdims=True)
    pb = p.astype(jnp.bfloat16)
    gw = jnp.concatenate([dot_nt(a, v[:, part]) for a, part in zip(gm, lanes)], axis=0)
    delta = jnp.sum(pb.astype(jnp.float32) * gw, axis=1, keepdims=True)
    ds = (p * (gw - delta)).astype(jnp.bfloat16)
    rows = per_group * nq
    dk = jnp.concatenate(
        [dot_tn(ds[t * rows:(t + 1) * rows], a) for t, a in enumerate(qm)], axis=1
    ) * SCALE
    dv = jnp.concatenate(
        [dot_tn(pb[t * rows:(t + 1) * rows], a) for t, a in enumerate(gm)], axis=1
    )
    lane = lax.broadcasted_iota(jnp.int32, (1, LANES), 1)
    low = lane < HD
    tiles = []
    for pair in range(width // LANES):
        both = jnp.dot(
            ds[2 * pair * nq:(2 * pair + 2) * nq],
            k[:, pair * LANES:(pair + 1) * LANES],
            preferred_element_type=jnp.float32,
        )
        tiles.append(jnp.where(low, both[:nq], both[nq:]) * SCALE)
    dq = jnp.concatenate(tiles, axis=1)
    return dq, dk, dv


def fused_row_kernel(w2, q_ref, g_ref, k_ref, v_ref, l1_ref, r1_ref, bias_ref,
                     qg_ref, kg_ref, vg_ref,
                     l2_ref, r2_ref, own_s, near_l, near_r, s_fl, s_fr, s_nl, s_nr, x_fr, x_fl,
                     x_nr, x_nl, halo_send, halo_recv_l, halo_recv_r, far_send, far_recv_r, far_recv_l,
                     near_send, near_recv):
    rows, cc, width = q_ref.shape
    w1 = l1_ref.shape[2]
    n = lax.axis_size("rcol")
    me = lax.axis_index("rcol")
    here = (lax.axis_index("slide"), lax.axis_index("rrow"))
    mesh_ids = pl.DeviceIdType.MESH

    def dev(distance):
        return here + (lax.rem(me + distance + n, n),)

    barrier = pltpu.get_barrier_semaphore()
    for distance in (-1, 1):
        pl.semaphore_signal(barrier, 1, device_id=dev(distance), device_id_type=mesh_ids)
    pl.semaphore_wait(barrier, 2)

    def relays(r, whole=False):
        rs = slice(None) if whole else pl.ds(r, 1)
        return (
            pltpu.make_async_remote_copy(
                src_ref=l1_ref.at[:, rs, pl.ds(w1 - w2, w2)], dst_ref=l2_ref.at[:, rs],
                send_sem=halo_send.at[0], recv_sem=halo_recv_l.at[r],
                device_id=dev(1), device_id_type=mesh_ids),
            pltpu.make_async_remote_copy(
                src_ref=r1_ref.at[:, rs, pl.ds(0, w2)], dst_ref=r2_ref.at[:, rs],
                send_sem=halo_send.at[1], recv_sem=halo_recv_r.at[r],
                device_id=dev(-1), device_id_type=mesh_ids),
        )

    for r in range(rows):
        for copy in relays(r):
            copy.start()

    def far_copy(r, to_left):
        if to_left:
            return pltpu.make_async_remote_copy(
                src_ref=s_fl.at[:, pl.ds(r, 1)], dst_ref=x_fr.at[:, pl.ds(r, 1)],
                send_sem=far_send.at[0], recv_sem=far_recv_r.at[r],
                device_id=dev(-1), device_id_type=mesh_ids)
        return pltpu.make_async_remote_copy(
            src_ref=s_fr.at[:, pl.ds(r, 1)], dst_ref=x_fl.at[:, pl.ds(r, 1)],
            send_sem=far_send.at[1], recv_sem=far_recv_l.at[r],
            device_id=dev(1), device_id_type=mesh_ids)

    def near_copy(r, to_left, whole=False):
        rs = slice(None) if whole else pl.ds(r, 1)
        if to_left:
            return pltpu.make_async_remote_copy(
                src_ref=s_nl.at[:, rs], dst_ref=x_nr.at[:, rs],
                send_sem=near_send.at[0], recv_sem=near_recv.at[0],
                device_id=dev(-1), device_id_type=mesh_ids)
        return pltpu.make_async_remote_copy(
            src_ref=s_nr.at[:, rs], dst_ref=x_nl.at[:, rs],
            send_sem=near_send.at[1], recv_sem=near_recv.at[1],
            device_id=dev(1), device_id_type=mesh_ids)

    def send_near(r):
        far_copy(r, True).wait_recv()
        far_copy(r, False).wait_recv()
        f32 = jnp.float32
        s_nl[:, r, :w1 - w2] = near_l[:, r, :w1 - w2].astype(jnp.bfloat16)
        s_nl[:, r, w1 - w2:] = (near_l[:, r, w1 - w2:] + x_fr[:, r].astype(f32)).astype(jnp.bfloat16)
        s_nr[:, r, :w2] = (near_r[:, r, :w2] + x_fl[:, r].astype(f32)).astype(jnp.bfloat16)
        s_nr[:, r, w2:] = near_r[:, r, w2:].astype(jnp.bfloat16)
        near_copy(r, True).start()
        near_copy(r, False).start()

    def row_step(r, carry):
        for copy in relays(r):
            copy.wait_recv()

        def span(which, own_ref):
            return jnp.concatenate(
                [l2_ref[which, r], l1_ref[which, r], own_ref[r], r1_ref[which, r],
                 r2_ref[which, r]],
                axis=0,
            )

        dq, dk, dv = block_grads(q_ref[r], g_ref[r], span(0, k_ref), span(1, v_ref), bias_ref[r])
        qg_ref[r] = dq
        for which, full in ((0, dk), (1, dv)):
            s_fl[which, r] = full[:w2].astype(jnp.bfloat16)
            near_l[which, r] = full[w2:w2 + w1]
            own_s[which, r] = full[w2 + w1:w2 + w1 + cc]
            near_r[which, r] = full[w2 + w1 + cc:w2 + 2 * w1 + cc]
            s_fr[which, r] = full[w2 + 2 * w1 + cc:].astype(jnp.bfloat16)
        far_copy(r, True).start()
        far_copy(r, False).start()

        @pl.when(r > 0)
        def _():
            send_near(r - 1)

        return carry

    lax.fori_loop(0, rows, row_step, 0)
    send_near(rows - 1)
    for copy in relays(0, whole=True):
        copy.wait_send()
    for src, dst, slot in ((s_fl, x_fr, 0), (s_fr, x_fl, 1)):
        pltpu.make_async_remote_copy(
            src_ref=src, dst_ref=dst, send_sem=far_send.at[slot], recv_sem=far_recv_r.at[0],
            device_id=dev(1 - 2 * (1 - slot)), device_id_type=mesh_ids).wait_send()
    for to_left in (True, False):
        near_copy(0, to_left, whole=True).wait()
    f32 = jnp.float32
    for which, out_ref in ((0, kg_ref), (1, vg_ref)):
        out_ref[...] = own_s[which] + x_nr[which].astype(f32) + x_nl[which].astype(f32)


def fused_row(queries, out_grad, key_grid, value_grid, l1, r1, bias, w2):
    rows, cc, width = queries.shape
    w1 = l1.shape[2]
    vmem = pl.BlockSpec(memory_space=pltpu.VMEM)
    grads = jax.ShapeDtypeStruct((rows, cc, width), jnp.float32)
    bf = jnp.bfloat16
    f32 = jnp.float32
    return pl.pallas_call(
        functools.partial(fused_row_kernel, w2),
        in_specs=[vmem] * 7,
        out_specs=[vmem] * 3,
        out_shape=(grads, grads, grads),
        scratch_shapes=[
            pltpu.VMEM((2, rows, w2, width), bf),
            pltpu.VMEM((2, rows, w2, width), bf),
            pltpu.VMEM((2, rows, cc, width), f32),
            pltpu.VMEM((2, rows, w1, width), f32),
            pltpu.VMEM((2, rows, w1, width), f32),
            pltpu.VMEM((2, rows, w2, width), bf),
            pltpu.VMEM((2, rows, w2, width), bf),
            pltpu.VMEM((2, rows, w1, width), bf),
            pltpu.VMEM((2, rows, w1, width), bf),
            pltpu.VMEM((2, rows, w2, width), bf),
            pltpu.VMEM((2, rows, w2, width), bf),
            pltpu.VMEM((2, rows, cc, width), bf),
            pltpu.VMEM((2, rows, cc, width), bf),
            pltpu.SemaphoreType.DMA((2,)),
            pltpu.SemaphoreType.DMA((rows,)),
            pltpu.SemaphoreType.DMA((rows,)),
            pltpu.SemaphoreType.DMA((2,)),
            pltpu.SemaphoreType.DMA((rows,)),
            pltpu.SemaphoreType.DMA((rows,)),
            pltpu.SemaphoreType.DMA((2,)),
            pltpu.SemaphoreType.DMA((2,)),
        ],
        compiler_params=pltpu.CompilerParams(
            collective_id=0, has_side_effects=True, vmem_limit_bytes=60 * 1024 * 1024
        ),
    )(queries, out_grad, key_grid, value_grid, l1, r1, bias)


def column_kernel(x_ref, o_ref):
    groups, arrays, strip, rows, width = x_ref.shape
    per = max(1, LANES // (groups * rows))

    def joined(which):
        return jnp.concatenate(
            [x_ref[s, which, c] for c in range(per) for s in range(groups)], axis=0
        )

    whole_rows = groups * rows
    i = lax.broadcasted_iota(jnp.int32, (per * whole_rows, per * whole_rows), 0) // whole_rows
    j = lax.broadcasted_iota(jnp.int32, (per * whole_rows, per * whole_rows), 1) // whole_rows
    bias = jnp.where(i == j, 0.0, -jnp.inf).astype(jnp.float32)
    for step in range(strip // per):
        def pick(which):
            return jnp.concatenate(
                [x_ref[s, which, step * per + c] for c in range(per) for s in range(groups)],
                axis=0,
            )

        grads = block_grads(pick(0), pick(3), pick(1), pick(2), bias)
        for which, full in enumerate(grads):
            low = full.astype(jnp.bfloat16)
            for c in range(per):
                for s in range(groups):
                    start = c * whole_rows + s * rows
                    o_ref[s, which, step * per + c] = low[start:start + rows]


def column_attention(whole):
    groups, arrays, strip, rows, width = whole.shape
    vmem = pl.BlockSpec(memory_space=pltpu.VMEM)
    return pl.pallas_call(
        column_kernel,
        in_specs=[vmem],
        out_specs=vmem,
        out_shape=jax.ShapeDtypeStruct((groups, 3, strip, rows, width), jnp.bfloat16),
    )(whole)


def regroup_kernel(q_ref, k_ref, v_ref, g_ref, o_ref):
    groups, arrays, strip, rows, width = o_ref.shape
    for which, ref in enumerate((q_ref, k_ref, v_ref, g_ref)):
        for group in range(groups):
            for c in range(strip):
                o_ref[group, which, c] = ref[:, group * strip + c, :]


def regroup(queries, key_grid, value_grid, out_grad, groups):
    rows, cols, width = queries.shape
    vmem = pl.BlockSpec(memory_space=pltpu.VMEM)
    return pl.pallas_call(
        regroup_kernel,
        in_specs=[vmem] * 4,
        out_specs=vmem,
        out_shape=jax.ShapeDtypeStruct((groups, 4, cols // groups, rows, width), queries.dtype),
    )(queries, key_grid, value_grid, out_grad)


def band_bias(mask_rows, offsets, first_col, grid_cols, block_cols):
    band_reach = HALF + OFFMAX
    query_cols = first_col + jnp.arange(block_cols, dtype=jnp.int32)
    key_cols = first_col - band_reach + jnp.arange(block_cols + 2 * band_reach, dtype=jnp.int32)
    inside = (key_cols >= 0) & (key_cols < grid_cols)
    key_block = jnp.clip(key_cols, 0, grid_cols - 1) // BLK
    block_ids = jnp.arange(mask_rows.shape[1], dtype=jnp.int32)
    key_open = jnp.sum(
        mask_rows[:, None, :]
        * (key_block[None, :, None] == block_ids[None, None, :]).astype(jnp.int32),
        axis=-1,
    )
    relative = key_cols[None, None, :] - query_cols[None, :, None] - offsets[:, None, None]
    same_block = key_cols[None, :] // BLK == query_cols[:, None] // BLK
    allowed = (
        (relative >= -HALF)
        & (relative < HALF)
        & inside[None, None, :]
        & ((key_open[:, None, :] > 0) | same_block[None])
    )
    return jnp.where(allowed, 0.0, -jnp.inf).astype(jnp.float32)


def body(queries, key_grid, value_grid, out_grad, tissue_mask, band_offset):
    row_count, col_count, feature_width = queries.shape
    group_count = lax.axis_size("rrow")
    band_reach = HALF + OFFMAX
    near = col_count
    far = band_reach - col_count

    strip = col_count // group_count
    stacked = regroup(queries, key_grid, value_grid, out_grad, group_count)
    whole = lax.all_to_all(stacked, "rrow", split_axis=0, concat_axis=0, tiled=True)

    pair = jnp.stack([key_grid, value_grid])
    l1 = shifted(pair[:, :, col_count - near:], "rcol", 1)
    r1 = shifted(pair[:, :, :near], "rcol", -1)
    grid_cols = col_count * lax.axis_size("rcol")
    first_col = lax.axis_index("rcol") * col_count
    bias = band_bias(tissue_mask, band_offset, first_col, grid_cols, col_count)

    col_out = column_attention(whole)
    back = lax.all_to_all(col_out, "rrow", split_axis=0, concat_axis=0, tiled=True)
    row_grads = fused_row(queries, out_grad, key_grid, value_grid, l1, r1, bias, far)
    back = back.transpose(1, 3, 0, 2, 4).reshape(3, row_count, col_count, feature_width)
    back = back.astype(jnp.float32)
    return tuple((row + col).astype(jnp.bfloat16) for row, col in zip(row_grads, back))


def solution(mesh):
    in_specs = (
        P(("slide", "rrow"), "rcol", None),
        P(("slide", "rrow"), "rcol", None),
        P(("slide", "rrow"), "rcol", None),
        P(("slide", "rrow"), "rcol", None),
        P(("slide", "rrow"), None),
        P(("slide", "rrow")),
    )
    out_specs = (
        P(("slide", "rrow"), "rcol", None),
        P(("slide", "rrow"), "rcol", None),
        P(("slide", "rrow"), "rcol", None),
    )
    return jax.shard_map(body, mesh=mesh, in_specs=in_specs, out_specs=out_specs, check_vma=False)
```

```python
import functools
import math

import jax
import jax.numpy as jnp
from jax import lax
from jax.experimental import pallas as pl
from jax.experimental.pallas import tpu as pltpu
from jax.sharding import PartitionSpec as P

HD = 64
BLK = 16
HALF = 32
OFFMAX = 16
SCALE = 1.0 / math.sqrt(HD)
LANES = 128


def shifted(block, axis, distance):
    devices = range(lax.axis_size(axis))
    route = [(i - distance, i) for i in devices if i - distance in devices]
    return lax.ppermute(block, axis, route)


def dot_nt(a, b):
    return lax.dot_general(a, b, (((1,), (1,)), ((), ())), preferred_element_type=jnp.float32)


def dot_tn(a, b):
    return lax.dot_general(a, b, (((0,), (0,)), ((), ())), preferred_element_type=jnp.float32)


def head_stack(x, heads):
    rows, width = x.shape
    lane_head = lax.broadcasted_iota(jnp.int32, (heads, 1, width), 2) // HD
    which = lax.broadcasted_iota(jnp.int32, (heads, 1, width), 0)
    kept = jnp.where(lane_head == which, x[None], jnp.zeros_like(x)[None])
    return kept.reshape(heads * rows, width)


def block_grads(q, g, k, v, bias):
    nq, width = q.shape
    heads = width // HD
    group = min(width, 2 * LANES)
    per_group = group // HD
    lanes = [slice(t * group, (t + 1) * group) for t in range(width // group)]
    qm = [head_stack(q[:, part], per_group) for part in lanes]
    gm = [head_stack(g[:, part], per_group) for part in lanes]
    full_bias = jnp.broadcast_to(bias[None], (heads,) + bias.shape).reshape(heads * nq, -1)
    s = jnp.concatenate([dot_nt(a, k[:, part]) for a, part in zip(qm, lanes)], axis=0)
    s = s * SCALE + full_bias
    mx = jnp.max(s, axis=1, keepdims=True)
    e = jnp.exp(s - mx)
    p = e / jnp.sum(e, axis=1, keepdims=True)
    pb = p.astype(jnp.bfloat16)
    gw = jnp.concatenate([dot_nt(a, v[:, part]) for a, part in zip(gm, lanes)], axis=0)
    delta = jnp.sum(pb.astype(jnp.float32) * gw, axis=1, keepdims=True)
    ds = (p * (gw - delta)).astype(jnp.bfloat16)
    rows = per_group * nq
    dk = jnp.concatenate(
        [dot_tn(ds[t * rows:(t + 1) * rows], a) for t, a in enumerate(qm)], axis=1
    ) * SCALE
    dv = jnp.concatenate(
        [dot_tn(pb[t * rows:(t + 1) * rows], a) for t, a in enumerate(gm)], axis=1
    )
    lane = lax.broadcasted_iota(jnp.int32, (1, LANES), 1)
    low = lane < HD
    tiles = []
    for pair in range(width // LANES):
        both = jnp.dot(
            ds[2 * pair * nq:(2 * pair + 2) * nq],
            k[:, pair * LANES:(pair + 1) * LANES],
            preferred_element_type=jnp.float32,
        )
        tiles.append(jnp.where(low, both[:nq], both[nq:]) * SCALE)
    dq = jnp.concatenate(tiles, axis=1)
    return dq, dk, dv


def fused_row_kernel(w2, q_ref, g_ref, k_ref, v_ref, l1_ref, r1_ref, bias_ref,
                     qg_ref, kg_ref, vg_ref,
                     l2_ref, r2_ref, own_s, near_l, near_r, s_fl, s_fr, s_nl, s_nr, x_fr, x_fl,
                     x_nr, x_nl, halo_send, halo_recv_l, halo_recv_r, far_send, far_recv_r, far_recv_l,
                     near_send, near_recv):
    rows, cc, width = q_ref.shape
    w1 = l1_ref.shape[2]
    n = lax.axis_size("rcol")
    me = lax.axis_index("rcol")
    here = (lax.axis_index("slide"), lax.axis_index("rrow"))
    mesh_ids = pl.DeviceIdType.MESH

    def dev(distance):
        return here + (lax.rem(me + distance + n, n),)

    barrier = pltpu.get_barrier_semaphore()
    for distance in (-1, 1):
        pl.semaphore_signal(barrier, 1, device_id=dev(distance), device_id_type=mesh_ids)
    pl.semaphore_wait(barrier, 2)

    def relays(r, whole=False):
        rs = slice(None) if whole else pl.ds(r, 1)
        return (
            pltpu.make_async_remote_copy(
                src_ref=l1_ref.at[:, rs, pl.ds(w1 - w2, w2)], dst_ref=l2_ref.at[:, rs],
                send_sem=halo_send.at[0], recv_sem=halo_recv_l.at[r],
                device_id=dev(1), device_id_type=mesh_ids),
            pltpu.make_async_remote_copy(
                src_ref=r1_ref.at[:, rs, pl.ds(0, w2)], dst_ref=r2_ref.at[:, rs],
                send_sem=halo_send.at[1], recv_sem=halo_recv_r.at[r],
                device_id=dev(-1), device_id_type=mesh_ids),
        )

    for r in range(rows):
        for copy in relays(r):
            copy.start()

    def far_copy(r, to_left):
        if to_left:
            return pltpu.make_async_remote_copy(
                src_ref=s_fl.at[:, pl.ds(r, 1)], dst_ref=x_fr.at[:, pl.ds(r, 1)],
                send_sem=far_send.at[0], recv_sem=far_recv_r.at[r],
                device_id=dev(-1), device_id_type=mesh_ids)
        return pltpu.make_async_remote_copy(
            src_ref=s_fr.at[:, pl.ds(r, 1)], dst_ref=x_fl.at[:, pl.ds(r, 1)],
            send_sem=far_send.at[1], recv_sem=far_recv_l.at[r],
            device_id=dev(1), device_id_type=mesh_ids)

    def near_copy(r, to_left, whole=False):
        rs = slice(None) if whole else pl.ds(r, 1)
        if to_left:
            return pltpu.make_async_remote_copy(
                src_ref=s_nl.at[:, rs], dst_ref=x_nr.at[:, rs],
                send_sem=near_send.at[0], recv_sem=near_recv.at[0],
                device_id=dev(-1), device_id_type=mesh_ids)
        return pltpu.make_async_remote_copy(
            src_ref=s_nr.at[:, rs], dst_ref=x_nl.at[:, rs],
            send_sem=near_send.at[1], recv_sem=near_recv.at[1],
            device_id=dev(1), device_id_type=mesh_ids)

    def send_near(r):
        far_copy(r, True).wait_recv()
        far_copy(r, False).wait_recv()
        f32 = jnp.float32
        s_nl[:, r, :w1 - w2] = near_l[:, r, :w1 - w2].astype(jnp.bfloat16)
        s_nl[:, r, w1 - w2:] = (near_l[:, r, w1 - w2:] + x_fr[:, r].astype(f32)).astype(jnp.bfloat16)
        s_nr[:, r, :w2] = (near_r[:, r, :w2] + x_fl[:, r].astype(f32)).astype(jnp.bfloat16)
        s_nr[:, r, w2:] = near_r[:, r, w2:].astype(jnp.bfloat16)
        near_copy(r, True).start()
        near_copy(r, False).start()

    def row_step(r, carry):
        for copy in relays(r):
            copy.wait_recv()

        def span(which, own_ref):
            return jnp.concatenate(
                [l2_ref[which, r], l1_ref[which, r], own_ref[r], r1_ref[which, r],
                 r2_ref[which, r]],
                axis=0,
            )

        dq, dk, dv = block_grads(q_ref[r], g_ref[r], span(0, k_ref), span(1, v_ref), bias_ref[r])
        qg_ref[r] = dq
        for which, full in ((0, dk), (1, dv)):
            s_fl[which, r] = full[:w2].astype(jnp.bfloat16)
            near_l[which, r] = full[w2:w2 + w1]
            own_s[which, r] = full[w2 + w1:w2 + w1 + cc]
            near_r[which, r] = full[w2 + w1 + cc:w2 + 2 * w1 + cc]
            s_fr[which, r] = full[w2 + 2 * w1 + cc:].astype(jnp.bfloat16)
        far_copy(r, True).start()
        far_copy(r, False).start()

        send_near(r)
        return carry

    lax.fori_loop(0, rows, row_step, 0)
    for copy in relays(0, whole=True):
        copy.wait_send()
    for src, dst, slot in ((s_fl, x_fr, 0), (s_fr, x_fl, 1)):
        pltpu.make_async_remote_copy(
            src_ref=src, dst_ref=dst, send_sem=far_send.at[slot], recv_sem=far_recv_r.at[0],
            device_id=dev(1 - 2 * (1 - slot)), device_id_type=mesh_ids).wait_send()
    for to_left in (True, False):
        near_copy(0, to_left, whole=True).wait()
    f32 = jnp.float32
    for which, out_ref in ((0, kg_ref), (1, vg_ref)):
        out_ref[...] = own_s[which] + x_nr[which].astype(f32) + x_nl[which].astype(f32)


def fused_row(queries, out_grad, key_grid, value_grid, l1, r1, bias, w2):
    rows, cc, width = queries.shape
    w1 = l1.shape[2]
    vmem = pl.BlockSpec(memory_space=pltpu.VMEM)
    grads = jax.ShapeDtypeStruct((rows, cc, width), jnp.float32)
    bf = jnp.bfloat16
    f32 = jnp.float32
    return pl.pallas_call(
        functools.partial(fused_row_kernel, w2),
        in_specs=[vmem] * 7,
        out_specs=[vmem] * 3,
        out_shape=(grads, grads, grads),
        scratch_shapes=[
            pltpu.VMEM((2, rows, w2, width), bf),
            pltpu.VMEM((2, rows, w2, width), bf),
            pltpu.VMEM((2, rows, cc, width), f32),
            pltpu.VMEM((2, rows, w1, width), f32),
            pltpu.VMEM((2, rows, w1, width), f32),
            pltpu.VMEM((2, rows, w2, width), bf),
            pltpu.VMEM((2, rows, w2, width), bf),
            pltpu.VMEM((2, rows, w1, width), bf),
            pltpu.VMEM((2, rows, w1, width), bf),
            pltpu.VMEM((2, rows, w2, width), bf),
            pltpu.VMEM((2, rows, w2, width), bf),
            pltpu.VMEM((2, rows, cc, width), bf),
            pltpu.VMEM((2, rows, cc, width), bf),
            pltpu.SemaphoreType.DMA((2,)),
            pltpu.SemaphoreType.DMA((rows,)),
            pltpu.SemaphoreType.DMA((rows,)),
            pltpu.SemaphoreType.DMA((2,)),
            pltpu.SemaphoreType.DMA((rows,)),
            pltpu.SemaphoreType.DMA((rows,)),
            pltpu.SemaphoreType.DMA((2,)),
            pltpu.SemaphoreType.DMA((2,)),
        ],
        compiler_params=pltpu.CompilerParams(
            collective_id=0, has_side_effects=True, vmem_limit_bytes=60 * 1024 * 1024
        ),
    )(queries, out_grad, key_grid, value_grid, l1, r1, bias)


def column_kernel(x_ref, o_ref):
    groups, arrays, strip, rows, width = x_ref.shape
    per = max(1, LANES // (groups * rows))

    def joined(which):
        return jnp.concatenate(
            [x_ref[s, which, c] for c in range(per) for s in range(groups)], axis=0
        )

    whole_rows = groups * rows
    i = lax.broadcasted_iota(jnp.int32, (per * whole_rows, per * whole_rows), 0) // whole_rows
    j = lax.broadcasted_iota(jnp.int32, (per * whole_rows, per * whole_rows), 1) // whole_rows
    bias = jnp.where(i == j, 0.0, -jnp.inf).astype(jnp.float32)
    for step in range(strip // per):
        def pick(which):
            return jnp.concatenate(
                [x_ref[s, which, step * per + c] for c in range(per) for s in range(groups)],
                axis=0,
            )

        grads = block_grads(pick(0), pick(3), pick(1), pick(2), bias)
        for which, full in enumerate(grads):
            low = full.astype(jnp.bfloat16)
            for c in range(per):
                for s in range(groups):
                    start = c * whole_rows + s * rows
                    o_ref[s, which, step * per + c] = low[start:start + rows]


def column_attention(whole):
    groups, arrays, strip, rows, width = whole.shape
    vmem = pl.BlockSpec(memory_space=pltpu.VMEM)
    return pl.pallas_call(
        column_kernel,
        in_specs=[vmem],
        out_specs=vmem,
        out_shape=jax.ShapeDtypeStruct((groups, 3, strip, rows, width), jnp.bfloat16),
    )(whole)


def band_bias(mask_rows, offsets, first_col, grid_cols, block_cols):
    band_reach = HALF + OFFMAX
    query_cols = first_col + jnp.arange(block_cols, dtype=jnp.int32)
    key_cols = first_col - band_reach + jnp.arange(block_cols + 2 * band_reach, dtype=jnp.int32)
    inside = (key_cols >= 0) & (key_cols < grid_cols)
    key_block = jnp.clip(key_cols, 0, grid_cols - 1) // BLK
    block_ids = jnp.arange(mask_rows.shape[1], dtype=jnp.int32)
    key_open = jnp.sum(
        mask_rows[:, None, :]
        * (key_block[None, :, None] == block_ids[None, None, :]).astype(jnp.int32),
        axis=-1,
    )
    relative = key_cols[None, None, :] - query_cols[None, :, None] - offsets[:, None, None]
    same_block = key_cols[None, :] // BLK == query_cols[:, None] // BLK
    allowed = (
        (relative >= -HALF)
        & (relative < HALF)
        & inside[None, None, :]
        & ((key_open[:, None, :] > 0) | same_block[None])
    )
    return jnp.where(allowed, 0.0, -jnp.inf).astype(jnp.float32)


def body(queries, key_grid, value_grid, out_grad, tissue_mask, band_offset):
    row_count, col_count, feature_width = queries.shape
    group_count = lax.axis_size("rrow")
    band_reach = HALF + OFFMAX
    near = col_count
    far = band_reach - col_count

    strip = col_count // group_count
    stacked = (
        jnp.stack([queries, key_grid, value_grid, out_grad])
        .reshape(4, row_count, group_count, strip, feature_width)
        .transpose(2, 0, 3, 1, 4)
    )
    whole = lax.all_to_all(stacked, "rrow", split_axis=0, concat_axis=0, tiled=True)

    pair = jnp.stack([key_grid, value_grid])
    l1 = shifted(pair[:, :, col_count - near:], "rcol", 1)
    r1 = shifted(pair[:, :, :near], "rcol", -1)
    grid_cols = col_count * lax.axis_size("rcol")
    first_col = lax.axis_index("rcol") * col_count
    bias = band_bias(tissue_mask, band_offset, first_col, grid_cols, col_count)

    col_out = column_attention(whole)
    back = lax.all_to_all(col_out, "rrow", split_axis=0, concat_axis=0, tiled=True)
    row_grads = fused_row(queries, out_grad, key_grid, value_grid, l1, r1, bias, far)
    back = back.transpose(1, 3, 0, 2, 4).reshape(3, row_count, col_count, feature_width)
    back = back.astype(jnp.float32)
    return tuple((row + col).astype(jnp.bfloat16) for row, col in zip(row_grads, back))


def solution(mesh):
    in_specs = (
        P(("slide", "rrow"), "rcol", None),
        P(("slide", "rrow"), "rcol", None),
        P(("slide", "rrow"), "rcol", None),
        P(("slide", "rrow"), "rcol", None),
        P(("slide", "rrow"), None),
        P(("slide", "rrow")),
    )
    out_specs = (
        P(("slide", "rrow"), "rcol", None),
        P(("slide", "rrow"), "rcol", None),
        P(("slide", "rrow"), "rcol", None),
    )
    return jax.shard_map(body, mesh=mesh, in_specs=in_specs, out_specs=out_specs, check_vma=False)
```

```python
import functools
import math

import jax
import jax.numpy as jnp
from jax import lax
from jax.experimental import pallas as pl
from jax.experimental.pallas import tpu as pltpu
from jax.sharding import PartitionSpec as P

HD = 64
BLK = 16
HALF = 32
OFFMAX = 16
SCALE = 1.0 / math.sqrt(HD)
LANES = 128


def shifted(block, axis, distance):
    devices = range(lax.axis_size(axis))
    route = [(i - distance, i) for i in devices if i - distance in devices]
    return lax.ppermute(block, axis, route)


def dot_nt(a, b):
    return lax.dot_general(a, b, (((1,), (1,)), ((), ())), preferred_element_type=jnp.float32)


def dot_tn(a, b):
    return lax.dot_general(a, b, (((0,), (0,)), ((), ())), preferred_element_type=jnp.float32)


def head_stack(x, heads):
    rows, width = x.shape
    lane_head = lax.broadcasted_iota(jnp.int32, (heads, 1, width), 2) // HD
    which = lax.broadcasted_iota(jnp.int32, (heads, 1, width), 0)
    kept = jnp.where(lane_head == which, x[None], jnp.zeros_like(x)[None])
    return kept.reshape(heads * rows, width)


def block_grads(q, g, k, v, bias):
    nq, width = q.shape
    heads = width // HD
    group = min(width, 2 * LANES)
    per_group = group // HD
    lanes = [slice(t * group, (t + 1) * group) for t in range(width // group)]
    qm = [head_stack(q[:, part], per_group) for part in lanes]
    gm = [head_stack(g[:, part], per_group) for part in lanes]
    full_bias = jnp.broadcast_to(bias[None], (heads,) + bias.shape).reshape(heads * nq, -1)
    s = jnp.concatenate([dot_nt(a, k[:, part]) for a, part in zip(qm, lanes)], axis=0)
    s = s * SCALE + full_bias
    mx = jnp.max(s, axis=1, keepdims=True)
    e = jnp.exp(s - mx)
    p = e / jnp.sum(e, axis=1, keepdims=True)
    pb = p.astype(jnp.bfloat16)
    gw = jnp.concatenate([dot_nt(a, v[:, part]) for a, part in zip(gm, lanes)], axis=0)
    delta = jnp.sum(pb.astype(jnp.float32) * gw, axis=1, keepdims=True)
    ds = (p * (gw - delta)).astype(jnp.bfloat16)
    rows = per_group * nq
    dk = jnp.concatenate(
        [dot_tn(ds[t * rows:(t + 1) * rows], a) for t, a in enumerate(qm)], axis=1
    ) * SCALE
    dv = jnp.concatenate(
        [dot_tn(pb[t * rows:(t + 1) * rows], a) for t, a in enumerate(gm)], axis=1
    )
    lane = lax.broadcasted_iota(jnp.int32, (1, LANES), 1)
    low = lane < HD
    tiles = []
    for pair in range(width // LANES):
        both = jnp.dot(
            ds[2 * pair * nq:(2 * pair + 2) * nq],
            k[:, pair * LANES:(pair + 1) * LANES],
            preferred_element_type=jnp.float32,
        )
        tiles.append(jnp.where(low, both[:nq], both[nq:]) * SCALE)
    dq = jnp.concatenate(tiles, axis=1)
    return dq, dk, dv


def fused_row_kernel(w2, q_ref, g_ref, k_ref, v_ref, l1_ref, r1_ref, bias_ref,
                     qg_ref, kg_ref, vg_ref,
                     l2_ref, r2_ref, own_s, near_l, near_r, s_fl, s_fr, s_nl, s_nr, x_fr, x_fl,
                     x_nr, x_nl, halo_send, halo_recv_l, halo_recv_r, far_send, far_recv_r, far_recv_l,
                     near_send, near_recv):
    rows, cc, width = q_ref.shape
    w1 = l1_ref.shape[2]
    n = lax.axis_size("rcol")
    me = lax.axis_index("rcol")
    here = (lax.axis_index("slide"), lax.axis_index("rrow"))
    mesh_ids = pl.DeviceIdType.MESH

    def dev(distance):
        return here + (lax.rem(me + distance + n, n),)

    barrier = pltpu.get_barrier_semaphore()
    for distance in (-1, 1):
        pl.semaphore_signal(barrier, 1, device_id=dev(distance), device_id_type=mesh_ids)
    pl.semaphore_wait(barrier, 2)

    def relays(r, whole=False):
        rs = slice(None) if whole else pl.ds(r, 1)
        return (
            pltpu.make_async_remote_copy(
                src_ref=l1_ref.at[:, rs, pl.ds(w1 - w2, w2)], dst_ref=l2_ref.at[:, rs],
                send_sem=halo_send.at[0], recv_sem=halo_recv_l.at[r],
                device_id=dev(1), device_id_type=mesh_ids),
            pltpu.make_async_remote_copy(
                src_ref=r1_ref.at[:, rs, pl.ds(0, w2)], dst_ref=r2_ref.at[:, rs],
                send_sem=halo_send.at[1], recv_sem=halo_recv_r.at[r],
                device_id=dev(-1), device_id_type=mesh_ids),
        )

    for r in range(rows):
        for copy in relays(r):
            copy.start()

    def far_copy(r, to_left):
        if to_left:
            return pltpu.make_async_remote_copy(
                src_ref=s_fl.at[:, pl.ds(r, 1)], dst_ref=x_fr.at[:, pl.ds(r, 1)],
                send_sem=far_send.at[0], recv_sem=far_recv_r.at[r],
                device_id=dev(-1), device_id_type=mesh_ids)
        return pltpu.make_async_remote_copy(
            src_ref=s_fr.at[:, pl.ds(r, 1)], dst_ref=x_fl.at[:, pl.ds(r, 1)],
            send_sem=far_send.at[1], recv_sem=far_recv_l.at[r],
            device_id=dev(1), device_id_type=mesh_ids)

    def near_copy(r, to_left, whole=False):
        rs = slice(None) if whole else pl.ds(r, 1)
        if to_left:
            return pltpu.make_async_remote_copy(
                src_ref=s_nl.at[:, rs], dst_ref=x_nr.at[:, rs],
                send_sem=near_send.at[0], recv_sem=near_recv.at[0],
                device_id=dev(-1), device_id_type=mesh_ids)
        return pltpu.make_async_remote_copy(
            src_ref=s_nr.at[:, rs], dst_ref=x_nl.at[:, rs],
            send_sem=near_send.at[1], recv_sem=near_recv.at[1],
            device_id=dev(1), device_id_type=mesh_ids)

    def send_near(r):
        far_copy(r, True).wait_recv()
        far_copy(r, False).wait_recv()
        f32 = jnp.float32
        s_nl[:, r, :w1 - w2] = near_l[:, r, :w1 - w2].astype(jnp.bfloat16)
        s_nl[:, r, w1 - w2:] = (near_l[:, r, w1 - w2:] + x_fr[:, r].astype(f32)).astype(jnp.bfloat16)
        s_nr[:, r, :w2] = (near_r[:, r, :w2] + x_fl[:, r].astype(f32)).astype(jnp.bfloat16)
        s_nr[:, r, w2:] = near_r[:, r, w2:].astype(jnp.bfloat16)
        near_copy(r, True).start()
        near_copy(r, False).start()

    def row_step(r, carry):
        for copy in relays(r):
            copy.wait_recv()

        def span(which, own_ref):
            return jnp.concatenate(
                [l2_ref[which, r], l1_ref[which, r], own_ref[r], r1_ref[which, r],
                 r2_ref[which, r]],
                axis=0,
            )

        dq, dk, dv = block_grads(q_ref[r], g_ref[r], span(0, k_ref), span(1, v_ref), bias_ref[r])
        qg_ref[r] = dq
        for which, full in ((0, dk), (1, dv)):
            s_fl[which, r] = full[:w2].astype(jnp.bfloat16)
            near_l[which, r] = full[w2:w2 + w1]
            own_s[which, r] = full[w2 + w1:w2 + w1 + cc]
            near_r[which, r] = full[w2 + w1 + cc:w2 + 2 * w1 + cc]
            s_fr[which, r] = full[w2 + 2 * w1 + cc:].astype(jnp.bfloat16)
        far_copy(r, True).start()
        far_copy(r, False).start()

        @pl.when(r > 1)
        def _():
            send_near(r - 2)

        return carry

    lax.fori_loop(0, rows, row_step, 0)
    send_near(rows - 2)
    send_near(rows - 1)
    for copy in relays(0, whole=True):
        copy.wait_send()
    for src, dst, slot in ((s_fl, x_fr, 0), (s_fr, x_fl, 1)):
        pltpu.make_async_remote_copy(
            src_ref=src, dst_ref=dst, send_sem=far_send.at[slot], recv_sem=far_recv_r.at[0],
            device_id=dev(1 - 2 * (1 - slot)), device_id_type=mesh_ids).wait_send()
    for to_left in (True, False):
        near_copy(0, to_left, whole=True).wait()
    f32 = jnp.float32
    for which, out_ref in ((0, kg_ref), (1, vg_ref)):
        out_ref[...] = own_s[which] + x_nr[which].astype(f32) + x_nl[which].astype(f32)


def fused_row(queries, out_grad, key_grid, value_grid, l1, r1, bias, w2):
    rows, cc, width = queries.shape
    w1 = l1.shape[2]
    vmem = pl.BlockSpec(memory_space=pltpu.VMEM)
    grads = jax.ShapeDtypeStruct((rows, cc, width), jnp.float32)
    bf = jnp.bfloat16
    f32 = jnp.float32
    return pl.pallas_call(
        functools.partial(fused_row_kernel, w2),
        in_specs=[vmem] * 7,
        out_specs=[vmem] * 3,
        out_shape=(grads, grads, grads),
        scratch_shapes=[
            pltpu.VMEM((2, rows, w2, width), bf),
            pltpu.VMEM((2, rows, w2, width), bf),
            pltpu.VMEM((2, rows, cc, width), f32),
            pltpu.VMEM((2, rows, w1, width), f32),
            pltpu.VMEM((2, rows, w1, width), f32),
            pltpu.VMEM((2, rows, w2, width), bf),
            pltpu.VMEM((2, rows, w2, width), bf),
            pltpu.VMEM((2, rows, w1, width), bf),
            pltpu.VMEM((2, rows, w1, width), bf),
            pltpu.VMEM((2, rows, w2, width), bf),
            pltpu.VMEM((2, rows, w2, width), bf),
            pltpu.VMEM((2, rows, cc, width), bf),
            pltpu.VMEM((2, rows, cc, width), bf),
            pltpu.SemaphoreType.DMA((2,)),
            pltpu.SemaphoreType.DMA((rows,)),
            pltpu.SemaphoreType.DMA((rows,)),
            pltpu.SemaphoreType.DMA((2,)),
            pltpu.SemaphoreType.DMA((rows,)),
            pltpu.SemaphoreType.DMA((rows,)),
            pltpu.SemaphoreType.DMA((2,)),
            pltpu.SemaphoreType.DMA((2,)),
        ],
        compiler_params=pltpu.CompilerParams(
            collective_id=0, has_side_effects=True, vmem_limit_bytes=60 * 1024 * 1024
        ),
    )(queries, out_grad, key_grid, value_grid, l1, r1, bias)


def column_kernel(x_ref, o_ref):
    groups, arrays, strip, rows, width = x_ref.shape
    per = max(1, LANES // (groups * rows))

    def joined(which):
        return jnp.concatenate(
            [x_ref[s, which, c] for c in range(per) for s in range(groups)], axis=0
        )

    whole_rows = groups * rows
    i = lax.broadcasted_iota(jnp.int32, (per * whole_rows, per * whole_rows), 0) // whole_rows
    j = lax.broadcasted_iota(jnp.int32, (per * whole_rows, per * whole_rows), 1) // whole_rows
    bias = jnp.where(i == j, 0.0, -jnp.inf).astype(jnp.float32)
    for step in range(strip // per):
        def pick(which):
            return jnp.concatenate(
                [x_ref[s, which, step * per + c] for c in range(per) for s in range(groups)],
                axis=0,
            )

        grads = block_grads(pick(0), pick(3), pick(1), pick(2), bias)
        for which, full in enumerate(grads):
            low = full.astype(jnp.bfloat16)
            for c in range(per):
                for s in range(groups):
                    start = c * whole_rows + s * rows
                    o_ref[s, which, step * per + c] = low[start:start + rows]


def column_attention(whole):
    groups, arrays, strip, rows, width = whole.shape
    vmem = pl.BlockSpec(memory_space=pltpu.VMEM)
    return pl.pallas_call(
        column_kernel,
        in_specs=[vmem],
        out_specs=vmem,
        out_shape=jax.ShapeDtypeStruct((groups, 3, strip, rows, width), jnp.bfloat16),
    )(whole)


def band_bias(mask_rows, offsets, first_col, grid_cols, block_cols):
    band_reach = HALF + OFFMAX
    query_cols = first_col + jnp.arange(block_cols, dtype=jnp.int32)
    key_cols = first_col - band_reach + jnp.arange(block_cols + 2 * band_reach, dtype=jnp.int32)
    inside = (key_cols >= 0) & (key_cols < grid_cols)
    key_block = jnp.clip(key_cols, 0, grid_cols - 1) // BLK
    block_ids = jnp.arange(mask_rows.shape[1], dtype=jnp.int32)
    key_open = jnp.sum(
        mask_rows[:, None, :]
        * (key_block[None, :, None] == block_ids[None, None, :]).astype(jnp.int32),
        axis=-1,
    )
    relative = key_cols[None, None, :] - query_cols[None, :, None] - offsets[:, None, None]
    same_block = key_cols[None, :] // BLK == query_cols[:, None] // BLK
    allowed = (
        (relative >= -HALF)
        & (relative < HALF)
        & inside[None, None, :]
        & ((key_open[:, None, :] > 0) | same_block[None])
    )
    return jnp.where(allowed, 0.0, -jnp.inf).astype(jnp.float32)


def body(queries, key_grid, value_grid, out_grad, tissue_mask, band_offset):
    row_count, col_count, feature_width = queries.shape
    group_count = lax.axis_size("rrow")
    band_reach = HALF + OFFMAX
    near = col_count
    far = band_reach - col_count

    strip = col_count // group_count
    stacked = (
        jnp.stack([queries, key_grid, value_grid, out_grad])
        .reshape(4, row_count, group_count, strip, feature_width)
        .transpose(2, 0, 3, 1, 4)
    )
    whole = lax.all_to_all(stacked, "rrow", split_axis=0, concat_axis=0, tiled=True)

    pair = jnp.stack([key_grid, value_grid])
    l1 = shifted(pair[:, :, col_count - near:], "rcol", 1)
    r1 = shifted(pair[:, :, :near], "rcol", -1)
    grid_cols = col_count * lax.axis_size("rcol")
    first_col = lax.axis_index("rcol") * col_count
    bias = band_bias(tissue_mask, band_offset, first_col, grid_cols, col_count)

    col_out = column_attention(whole)
    back = lax.all_to_all(col_out, "rrow", split_axis=0, concat_axis=0, tiled=True)
    row_grads = fused_row(queries, out_grad, key_grid, value_grid, l1, r1, bias, far)
    back = back.transpose(1, 3, 0, 2, 4).reshape(3, row_count, col_count, feature_width)
    back = back.astype(jnp.float32)
    return tuple((row + col).astype(jnp.bfloat16) for row, col in zip(row_grads, back))


def solution(mesh):
    in_specs = (
        P(("slide", "rrow"), "rcol", None),
        P(("slide", "rrow"), "rcol", None),
        P(("slide", "rrow"), "rcol", None),
        P(("slide", "rrow"), "rcol", None),
        P(("slide", "rrow"), None),
        P(("slide", "rrow")),
    )
    out_specs = (
        P(("slide", "rrow"), "rcol", None),
        P(("slide", "rrow"), "rcol", None),
        P(("slide", "rrow"), "rcol", None),
    )
    return jax.shard_map(body, mesh=mesh, in_specs=in_specs, out_specs=out_specs, check_vma=False)
```

```python
import functools
import math

import jax
import jax.numpy as jnp
from jax import lax
from jax.experimental import pallas as pl
from jax.experimental.pallas import tpu as pltpu
from jax.sharding import PartitionSpec as P

HD = 64
BLK = 16
HALF = 32
OFFMAX = 16
SCALE = 1.0 / math.sqrt(HD)
LANES = 128


def shifted(block, axis, distance):
    devices = range(lax.axis_size(axis))
    route = [(i - distance, i) for i in devices if i - distance in devices]
    return lax.ppermute(block, axis, route)


def dot_nt(a, b):
    return lax.dot_general(a, b, (((1,), (1,)), ((), ())), preferred_element_type=jnp.float32)


def dot_tn(a, b):
    return lax.dot_general(a, b, (((0,), (0,)), ((), ())), preferred_element_type=jnp.float32)


def head_stack(x, heads):
    rows, width = x.shape
    lane_head = lax.broadcasted_iota(jnp.int32, (heads, 1, width), 2) // HD
    which = lax.broadcasted_iota(jnp.int32, (heads, 1, width), 0)
    kept = jnp.where(lane_head == which, x[None], jnp.zeros_like(x)[None])
    return kept.reshape(heads * rows, width)


def block_grads(q, g, k, v, bias):
    nq, width = q.shape
    heads = width // HD
    group = min(width, 2 * LANES)
    per_group = group // HD
    lanes = [slice(t * group, (t + 1) * group) for t in range(width // group)]
    qm = [head_stack(q[:, part], per_group) for part in lanes]
    gm = [head_stack(g[:, part], per_group) for part in lanes]
    full_bias = jnp.broadcast_to(bias[None], (heads,) + bias.shape).reshape(heads * nq, -1)
    s = jnp.concatenate([dot_nt(a, k[:, part]) for a, part in zip(qm, lanes)], axis=0)
    s = s * SCALE + full_bias
    mx = jnp.max(s, axis=1, keepdims=True)
    e = jnp.exp(s - mx)
    p = e / jnp.sum(e, axis=1, keepdims=True)
    pb = p.astype(jnp.bfloat16)
    gw = jnp.concatenate([dot_nt(a, v[:, part]) for a, part in zip(gm, lanes)], axis=0)
    delta = jnp.sum(pb.astype(jnp.float32) * gw, axis=1, keepdims=True)
    ds = (p * (gw - delta)).astype(jnp.bfloat16)
    rows = per_group * nq
    dk = jnp.concatenate(
        [dot_tn(ds[t * rows:(t + 1) * rows], a) for t, a in enumerate(qm)], axis=1
    ) * SCALE
    dv = jnp.concatenate(
        [dot_tn(pb[t * rows:(t + 1) * rows], a) for t, a in enumerate(gm)], axis=1
    )
    lane = lax.broadcasted_iota(jnp.int32, (1, LANES), 1)
    low = lane < HD
    tiles = []
    for pair in range(width // LANES):
        both = jnp.dot(
            ds[2 * pair * nq:(2 * pair + 2) * nq],
            k[:, pair * LANES:(pair + 1) * LANES],
            preferred_element_type=jnp.float32,
        )
        tiles.append(jnp.where(low, both[:nq], both[nq:]) * SCALE)
    dq = jnp.concatenate(tiles, axis=1)
    return dq, dk, dv


def fused_row_kernel(w2, q_ref, g_ref, k_ref, v_ref, l1_ref, r1_ref, bias_ref,
                     qg_ref, kg_ref, vg_ref,
                     l2_ref, r2_ref, own_s, near_l, near_r, s_fl, s_fr, s_nl, s_nr, x_fr, x_fl,
                     x_nr, x_nl, halo_send, halo_recv_l, halo_recv_r, far_send, far_recv_r, far_recv_l,
                     near_send, near_recv):
    rows, cc, width = q_ref.shape
    w1 = l1_ref.shape[2]
    n = lax.axis_size("rcol")
    me = lax.axis_index("rcol")
    here = (lax.axis_index("slide"), lax.axis_index("rrow"))
    mesh_ids = pl.DeviceIdType.MESH

    def dev(distance):
        return here + (lax.rem(me + distance + n, n),)

    barrier = pltpu.get_barrier_semaphore()
    for distance in (-1, 1):
        pl.semaphore_signal(barrier, 1, device_id=dev(distance), device_id_type=mesh_ids)
    pl.semaphore_wait(barrier, 2)

    def relays(r, whole=False):
        rs = slice(None) if whole else pl.ds(r, 1)
        return (
            pltpu.make_async_remote_copy(
                src_ref=l1_ref.at[:, rs, pl.ds(w1 - w2, w2)], dst_ref=l2_ref.at[:, rs],
                send_sem=halo_send.at[0], recv_sem=halo_recv_l.at[r],
                device_id=dev(1), device_id_type=mesh_ids),
            pltpu.make_async_remote_copy(
                src_ref=r1_ref.at[:, rs, pl.ds(0, w2)], dst_ref=r2_ref.at[:, rs],
                send_sem=halo_send.at[1], recv_sem=halo_recv_r.at[r],
                device_id=dev(-1), device_id_type=mesh_ids),
        )

    for r in range(rows):
        for copy in relays(r):
            copy.start()

    def far_copy(r, to_left):
        if to_left:
            return pltpu.make_async_remote_copy(
                src_ref=s_fl.at[:, pl.ds(r, 1)], dst_ref=x_fr.at[:, pl.ds(r, 1)],
                send_sem=far_send.at[0], recv_sem=far_recv_r.at[r],
                device_id=dev(-1), device_id_type=mesh_ids)
        return pltpu.make_async_remote_copy(
            src_ref=s_fr.at[:, pl.ds(r, 1)], dst_ref=x_fl.at[:, pl.ds(r, 1)],
            send_sem=far_send.at[1], recv_sem=far_recv_l.at[r],
            device_id=dev(1), device_id_type=mesh_ids)

    def near_copy(r, to_left, whole=False):
        rs = slice(None) if whole else pl.ds(r, 1)
        if to_left:
            return pltpu.make_async_remote_copy(
                src_ref=s_nl.at[:, rs], dst_ref=x_nr.at[:, rs],
                send_sem=near_send.at[0], recv_sem=near_recv.at[0],
                device_id=dev(-1), device_id_type=mesh_ids)
        return pltpu.make_async_remote_copy(
            src_ref=s_nr.at[:, rs], dst_ref=x_nl.at[:, rs],
            send_sem=near_send.at[1], recv_sem=near_recv.at[1],
            device_id=dev(1), device_id_type=mesh_ids)

    def send_near(r):
        far_copy(r, True).wait_recv()
        far_copy(r, False).wait_recv()
        f32 = jnp.float32
        s_nl[:, r, :w1 - w2] = near_l[:, r, :w1 - w2].astype(jnp.bfloat16)
        s_nl[:, r, w1 - w2:] = (near_l[:, r, w1 - w2:] + x_fr[:, r].astype(f32)).astype(jnp.bfloat16)
        s_nr[:, r, :w2] = (near_r[:, r, :w2] + x_fl[:, r].astype(f32)).astype(jnp.bfloat16)
        s_nr[:, r, w2:] = near_r[:, r, w2:].astype(jnp.bfloat16)
        near_copy(r, True).start()
        near_copy(r, False).start()

    def row_step(r, carry):
        for copy in relays(r):
            copy.wait_recv()

        def span(which, own_ref):
            return jnp.concatenate(
                [l2_ref[which, r], l1_ref[which, r], own_ref[r], r1_ref[which, r],
                 r2_ref[which, r]],
                axis=0,
            )

        dq, dk, dv = block_grads(q_ref[r], g_ref[r], span(0, k_ref), span(1, v_ref), bias_ref[r])
        qg_ref[r] = dq
        for which, full in ((0, dk), (1, dv)):
            s_fl[which, r] = full[:w2].astype(jnp.bfloat16)
            near_l[which, r] = full[w2:w2 + w1]
            own_s[which, r] = full[w2 + w1:w2 + w1 + cc]
            near_r[which, r] = full[w2 + w1 + cc:w2 + 2 * w1 + cc]
            s_fr[which, r] = full[w2 + 2 * w1 + cc:].astype(jnp.bfloat16)
        far_copy(r, True).start()
        far_copy(r, False).start()

        @pl.when(r > 2)
        def _():
            send_near(r - 3)

        return carry

    lax.fori_loop(0, rows, row_step, 0)
    send_near(rows - 3)
    send_near(rows - 2)
    send_near(rows - 1)
    for copy in relays(0, whole=True):
        copy.wait_send()
    for src, dst, slot in ((s_fl, x_fr, 0), (s_fr, x_fl, 1)):
        pltpu.make_async_remote_copy(
            src_ref=src, dst_ref=dst, send_sem=far_send.at[slot], recv_sem=far_recv_r.at[0],
            device_id=dev(1 - 2 * (1 - slot)), device_id_type=mesh_ids).wait_send()
    for to_left in (True, False):
        near_copy(0, to_left, whole=True).wait()
    f32 = jnp.float32
    for which, out_ref in ((0, kg_ref), (1, vg_ref)):
        out_ref[...] = own_s[which] + x_nr[which].astype(f32) + x_nl[which].astype(f32)


def fused_row(queries, out_grad, key_grid, value_grid, l1, r1, bias, w2):
    rows, cc, width = queries.shape
    w1 = l1.shape[2]
    vmem = pl.BlockSpec(memory_space=pltpu.VMEM)
    grads = jax.ShapeDtypeStruct((rows, cc, width), jnp.float32)
    bf = jnp.bfloat16
    f32 = jnp.float32
    return pl.pallas_call(
        functools.partial(fused_row_kernel, w2),
        in_specs=[vmem] * 7,
        out_specs=[vmem] * 3,
        out_shape=(grads, grads, grads),
        scratch_shapes=[
            pltpu.VMEM((2, rows, w2, width), bf),
            pltpu.VMEM((2, rows, w2, width), bf),
            pltpu.VMEM((2, rows, cc, width), f32),
            pltpu.VMEM((2, rows, w1, width), f32),
            pltpu.VMEM((2, rows, w1, width), f32),
            pltpu.VMEM((2, rows, w2, width), bf),
            pltpu.VMEM((2, rows, w2, width), bf),
            pltpu.VMEM((2, rows, w1, width), bf),
            pltpu.VMEM((2, rows, w1, width), bf),
            pltpu.VMEM((2, rows, w2, width), bf),
            pltpu.VMEM((2, rows, w2, width), bf),
            pltpu.VMEM((2, rows, cc, width), bf),
            pltpu.VMEM((2, rows, cc, width), bf),
            pltpu.SemaphoreType.DMA((2,)),
            pltpu.SemaphoreType.DMA((rows,)),
            pltpu.SemaphoreType.DMA((rows,)),
            pltpu.SemaphoreType.DMA((2,)),
            pltpu.SemaphoreType.DMA((rows,)),
            pltpu.SemaphoreType.DMA((rows,)),
            pltpu.SemaphoreType.DMA((2,)),
            pltpu.SemaphoreType.DMA((2,)),
        ],
        compiler_params=pltpu.CompilerParams(
            collective_id=0, has_side_effects=True, vmem_limit_bytes=60 * 1024 * 1024
        ),
    )(queries, out_grad, key_grid, value_grid, l1, r1, bias)


def column_kernel(x_ref, o_ref):
    groups, arrays, strip, rows, width = x_ref.shape
    per = max(1, LANES // (groups * rows))

    def joined(which):
        return jnp.concatenate(
            [x_ref[s, which, c] for c in range(per) for s in range(groups)], axis=0
        )

    whole_rows = groups * rows
    i = lax.broadcasted_iota(jnp.int32, (per * whole_rows, per * whole_rows), 0) // whole_rows
    j = lax.broadcasted_iota(jnp.int32, (per * whole_rows, per * whole_rows), 1) // whole_rows
    bias = jnp.where(i == j, 0.0, -jnp.inf).astype(jnp.float32)
    for step in range(strip // per):
        def pick(which):
            return jnp.concatenate(
                [x_ref[s, which, step * per + c] for c in range(per) for s in range(groups)],
                axis=0,
            )

        grads = block_grads(pick(0), pick(3), pick(1), pick(2), bias)
        for which, full in enumerate(grads):
            low = full.astype(jnp.bfloat16)
            for c in range(per):
                for s in range(groups):
                    start = c * whole_rows + s * rows
                    o_ref[s, which, step * per + c] = low[start:start + rows]


def column_attention(whole):
    groups, arrays, strip, rows, width = whole.shape
    vmem = pl.BlockSpec(memory_space=pltpu.VMEM)
    return pl.pallas_call(
        column_kernel,
        in_specs=[vmem],
        out_specs=vmem,
        out_shape=jax.ShapeDtypeStruct((groups, 3, strip, rows, width), jnp.bfloat16),
    )(whole)


def band_bias(mask_rows, offsets, first_col, grid_cols, block_cols):
    band_reach = HALF + OFFMAX
    query_cols = first_col + jnp.arange(block_cols, dtype=jnp.int32)
    key_cols = first_col - band_reach + jnp.arange(block_cols + 2 * band_reach, dtype=jnp.int32)
    inside = (key_cols >= 0) & (key_cols < grid_cols)
    key_block = jnp.clip(key_cols, 0, grid_cols - 1) // BLK
    block_ids = jnp.arange(mask_rows.shape[1], dtype=jnp.int32)
    key_open = jnp.sum(
        mask_rows[:, None, :]
        * (key_block[None, :, None] == block_ids[None, None, :]).astype(jnp.int32),
        axis=-1,
    )
    relative = key_cols[None, None, :] - query_cols[None, :, None] - offsets[:, None, None]
    same_block = key_cols[None, :] // BLK == query_cols[:, None] // BLK
    allowed = (
        (relative >= -HALF)
        & (relative < HALF)
        & inside[None, None, :]
        & ((key_open[:, None, :] > 0) | same_block[None])
    )
    return jnp.where(allowed, 0.0, -jnp.inf).astype(jnp.float32)


def body(queries, key_grid, value_grid, out_grad, tissue_mask, band_offset):
    row_count, col_count, feature_width = queries.shape
    group_count = lax.axis_size("rrow")
    band_reach = HALF + OFFMAX
    near = col_count
    far = band_reach - col_count

    strip = col_count // group_count
    stacked = (
        jnp.stack([queries, key_grid, value_grid, out_grad])
        .reshape(4, row_count, group_count, strip, feature_width)
        .transpose(2, 0, 3, 1, 4)
    )
    whole = lax.all_to_all(stacked, "rrow", split_axis=0, concat_axis=0, tiled=True)

    pair = jnp.stack([key_grid, value_grid])
    l1 = shifted(pair[:, :, col_count - near:], "rcol", 1)
    r1 = shifted(pair[:, :, :near], "rcol", -1)
    grid_cols = col_count * lax.axis_size("rcol")
    first_col = lax.axis_index("rcol") * col_count
    bias = band_bias(tissue_mask, band_offset, first_col, grid_cols, col_count)

    col_out = column_attention(whole)
    back = lax.all_to_all(col_out, "rrow", split_axis=0, concat_axis=0, tiled=True)
    row_grads = fused_row(queries, out_grad, key_grid, value_grid, l1, r1, bias, far)
    back = back.transpose(1, 3, 0, 2, 4).reshape(3, row_count, col_count, feature_width)
    back = back.astype(jnp.float32)
    return tuple((row + col).astype(jnp.bfloat16) for row, col in zip(row_grads, back))


def solution(mesh):
    in_specs = (
        P(("slide", "rrow"), "rcol", None),
        P(("slide", "rrow"), "rcol", None),
        P(("slide", "rrow"), "rcol", None),
        P(("slide", "rrow"), "rcol", None),
        P(("slide", "rrow"), None),
        P(("slide", "rrow")),
    )
    out_specs = (
        P(("slide", "rrow"), "rcol", None),
        P(("slide", "rrow"), "rcol", None),
        P(("slide", "rrow"), "rcol", None),
    )
    return jax.shard_map(body, mesh=mesh, in_specs=in_specs, out_specs=out_specs, check_vma=False)
```

```python
import functools
import math

import jax
import jax.numpy as jnp
from jax import lax
from jax.experimental import pallas as pl
from jax.experimental.pallas import tpu as pltpu
from jax.sharding import PartitionSpec as P

HD = 64
BLK = 16
HALF = 32
OFFMAX = 16
SCALE = 1.0 / math.sqrt(HD)
LANES = 128


def shifted(block, axis, distance):
    devices = range(lax.axis_size(axis))
    route = [(i - distance, i) for i in devices if i - distance in devices]
    return lax.ppermute(block, axis, route)


def dot_nt(a, b):
    return lax.dot_general(a, b, (((1,), (1,)), ((), ())), preferred_element_type=jnp.float32)


def dot_tn(a, b):
    return lax.dot_general(a, b, (((0,), (0,)), ((), ())), preferred_element_type=jnp.float32)


def head_stack(x, heads):
    rows, width = x.shape
    lane_head = lax.broadcasted_iota(jnp.int32, (heads, 1, width), 2) // HD
    which = lax.broadcasted_iota(jnp.int32, (heads, 1, width), 0)
    kept = jnp.where(lane_head == which, x[None], jnp.zeros_like(x)[None])
    return kept.reshape(heads * rows, width)


def block_grads(q, g, k, v, bias):
    nq, width = q.shape
    heads = width // HD
    group = min(width, 2 * LANES)
    per_group = group // HD
    lanes = [slice(t * group, (t + 1) * group) for t in range(width // group)]
    qm = [head_stack(q[:, part], per_group) for part in lanes]
    gm = [head_stack(g[:, part], per_group) for part in lanes]
    full_bias = jnp.broadcast_to(bias[None], (heads,) + bias.shape).reshape(heads * nq, -1)
    s = jnp.concatenate([dot_nt(a, k[:, part]) for a, part in zip(qm, lanes)], axis=0)
    s = s * SCALE + full_bias
    mx = jnp.max(s, axis=1, keepdims=True)
    e = jnp.exp(s - mx)
    p = e / jnp.sum(e, axis=1, keepdims=True)
    pb = p.astype(jnp.bfloat16)
    gw = jnp.concatenate([dot_nt(a, v[:, part]) for a, part in zip(gm, lanes)], axis=0)
    delta = jnp.sum(pb.astype(jnp.float32) * gw, axis=1, keepdims=True)
    ds = (p * (gw - delta)).astype(jnp.bfloat16)
    rows = per_group * nq
    dk = jnp.concatenate(
        [dot_tn(ds[t * rows:(t + 1) * rows], a) for t, a in enumerate(qm)], axis=1
    ) * SCALE
    dv = jnp.concatenate(
        [dot_tn(pb[t * rows:(t + 1) * rows], a) for t, a in enumerate(gm)], axis=1
    )
    lane = lax.broadcasted_iota(jnp.int32, (1, LANES), 1)
    low = lane < HD
    tiles = []
    for pair in range(width // LANES):
        both = jnp.dot(
            ds[2 * pair * nq:(2 * pair + 2) * nq],
            k[:, pair * LANES:(pair + 1) * LANES],
            preferred_element_type=jnp.float32,
        )
        tiles.append(jnp.where(low, both[:nq], both[nq:]) * SCALE)
    dq = jnp.concatenate(tiles, axis=1)
    return dq, dk, dv


def fused_row_kernel(w2, q_ref, g_ref, k_ref, v_ref, l1_ref, r1_ref, bias_ref,
                     qg_ref, kg_ref, vg_ref,
                     l2_ref, r2_ref, own_s, near_l, near_r, s_fl, s_fr, s_nl, s_nr, x_fr, x_fl,
                     x_nr, x_nl, halo_send, halo_recv_l, halo_recv_r, far_send, far_recv_r, far_recv_l,
                     near_send, near_recv):
    rows, cc, width = q_ref.shape
    w1 = l1_ref.shape[2]
    n = lax.axis_size("rcol")
    me = lax.axis_index("rcol")
    here = (lax.axis_index("slide"), lax.axis_index("rrow"))
    mesh_ids = pl.DeviceIdType.MESH

    def dev(distance):
        return here + (lax.rem(me + distance + n, n),)

    barrier = pltpu.get_barrier_semaphore()
    for distance in (-1, 1):
        pl.semaphore_signal(barrier, 1, device_id=dev(distance), device_id_type=mesh_ids)
    pl.semaphore_wait(barrier, 2)

    def relays(r, whole=False):
        rs = slice(None) if whole else pl.ds(r, 1)
        return (
            pltpu.make_async_remote_copy(
                src_ref=l1_ref.at[:, rs, pl.ds(w1 - w2, w2)], dst_ref=l2_ref.at[:, rs],
                send_sem=halo_send.at[0], recv_sem=halo_recv_l.at[r],
                device_id=dev(1), device_id_type=mesh_ids),
            pltpu.make_async_remote_copy(
                src_ref=r1_ref.at[:, rs, pl.ds(0, w2)], dst_ref=r2_ref.at[:, rs],
                send_sem=halo_send.at[1], recv_sem=halo_recv_r.at[r],
                device_id=dev(-1), device_id_type=mesh_ids),
        )

    for r in range(rows):
        for copy in relays(r):
            copy.start()

    def far_copy(r, to_left):
        if to_left:
            return pltpu.make_async_remote_copy(
                src_ref=s_fl.at[:, pl.ds(r, 1)], dst_ref=x_fr.at[:, pl.ds(r, 1)],
                send_sem=far_send.at[0], recv_sem=far_recv_r.at[r],
                device_id=dev(-1), device_id_type=mesh_ids)
        return pltpu.make_async_remote_copy(
            src_ref=s_fr.at[:, pl.ds(r, 1)], dst_ref=x_fl.at[:, pl.ds(r, 1)],
            send_sem=far_send.at[1], recv_sem=far_recv_l.at[r],
            device_id=dev(1), device_id_type=mesh_ids)

    def near_copy(r, to_left, whole=False):
        rs = slice(None) if whole else pl.ds(r, 1)
        if to_left:
            return pltpu.make_async_remote_copy(
                src_ref=s_nl.at[:, rs], dst_ref=x_nr.at[:, rs],
                send_sem=near_send.at[0], recv_sem=near_recv.at[0],
                device_id=dev(-1), device_id_type=mesh_ids)
        return pltpu.make_async_remote_copy(
            src_ref=s_nr.at[:, rs], dst_ref=x_nl.at[:, rs],
            send_sem=near_send.at[1], recv_sem=near_recv.at[1],
            device_id=dev(1), device_id_type=mesh_ids)

    def send_near(r):
        far_copy(r, True).wait_recv()
        far_copy(r, False).wait_recv()
        f32 = jnp.float32
        s_nl[:, r, :w1 - w2] = near_l[:, r, :w1 - w2].astype(jnp.bfloat16)
        s_nl[:, r, w1 - w2:] = (near_l[:, r, w1 - w2:] + x_fr[:, r].astype(f32)).astype(jnp.bfloat16)
        s_nr[:, r, :w2] = (near_r[:, r, :w2] + x_fl[:, r].astype(f32)).astype(jnp.bfloat16)
        s_nr[:, r, w2:] = near_r[:, r, w2:].astype(jnp.bfloat16)
        near_copy(r, True).start()
        near_copy(r, False).start()

    def row_step(r, carry):
        for copy in relays(r):
            copy.wait_recv()

        def span(which, own_ref):
            return jnp.concatenate(
                [l2_ref[which, r], l1_ref[which, r], own_ref[r], r1_ref[which, r],
                 r2_ref[which, r]],
                axis=0,
            )

        dq, dk, dv = block_grads(q_ref[r], g_ref[r], span(0, k_ref), span(1, v_ref), bias_ref[r])
        qg_ref[r] = dq
        for which, full in ((0, dk), (1, dv)):
            s_fl[which, r] = full[:w2].astype(jnp.bfloat16)
            near_l[which, r] = full[w2:w2 + w1]
            own_s[which, r] = full[w2 + w1:w2 + w1 + cc]
            near_r[which, r] = full[w2 + w1 + cc:w2 + 2 * w1 + cc]
            s_fr[which, r] = full[w2 + 2 * w1 + cc:].astype(jnp.bfloat16)
        far_copy(r, True).start()
        far_copy(r, False).start()

        @pl.when(r > 1)
        def _():
            send_near(r - 2)

        return carry

    lax.fori_loop(0, rows, row_step, 0)
    send_near(rows - 2)
    send_near(rows - 1)
    for copy in relays(0, whole=True):
        copy.wait_send()
    for src, dst, slot in ((s_fl, x_fr, 0), (s_fr, x_fl, 1)):
        pltpu.make_async_remote_copy(
            src_ref=src, dst_ref=dst, send_sem=far_send.at[slot], recv_sem=far_recv_r.at[0],
            device_id=dev(1 - 2 * (1 - slot)), device_id_type=mesh_ids).wait_send()
    for to_left in (True, False):
        near_copy(0, to_left, whole=True).wait()
    f32 = jnp.float32
    for which, out_ref in ((0, kg_ref), (1, vg_ref)):
        out_ref[...] = own_s[which] + x_nr[which].astype(f32) + x_nl[which].astype(f32)


def fused_row(queries, out_grad, key_grid, value_grid, l1, r1, bias, w2):
    rows, cc, width = queries.shape
    w1 = l1.shape[2]
    vmem = pl.BlockSpec(memory_space=pltpu.VMEM)
    grads = jax.ShapeDtypeStruct((rows, cc, width), jnp.float32)
    bf = jnp.bfloat16
    f32 = jnp.float32
    return pl.pallas_call(
        functools.partial(fused_row_kernel, w2),
        in_specs=[vmem] * 7,
        out_specs=[vmem] * 3,
        out_shape=(grads, grads, grads),
        scratch_shapes=[
            pltpu.VMEM((2, rows, w2, width), bf),
            pltpu.VMEM((2, rows, w2, width), bf),
            pltpu.VMEM((2, rows, cc, width), f32),
            pltpu.VMEM((2, rows, w1, width), f32),
            pltpu.VMEM((2, rows, w1, width), f32),
            pltpu.VMEM((2, rows, w2, width), bf),
            pltpu.VMEM((2, rows, w2, width), bf),
            pltpu.VMEM((2, rows, w1, width), bf),
            pltpu.VMEM((2, rows, w1, width), bf),
            pltpu.VMEM((2, rows, w2, width), bf),
            pltpu.VMEM((2, rows, w2, width), bf),
            pltpu.VMEM((2, rows, cc, width), bf),
            pltpu.VMEM((2, rows, cc, width), bf),
            pltpu.SemaphoreType.DMA((2,)),
            pltpu.SemaphoreType.DMA((rows,)),
            pltpu.SemaphoreType.DMA((rows,)),
            pltpu.SemaphoreType.DMA((2,)),
            pltpu.SemaphoreType.DMA((rows,)),
            pltpu.SemaphoreType.DMA((rows,)),
            pltpu.SemaphoreType.DMA((2,)),
            pltpu.SemaphoreType.DMA((2,)),
        ],
        compiler_params=pltpu.CompilerParams(
            collective_id=0, has_side_effects=True, vmem_limit_bytes=60 * 1024 * 1024
        ),
    )(queries, out_grad, key_grid, value_grid, l1, r1, bias)


def column_kernel(x_ref, order_ref, o_ref):
    groups, arrays, strip, rows, width = x_ref.shape
    per = max(1, LANES // (groups * rows))

    def joined(which):
        return jnp.concatenate(
            [x_ref[s, which, c] for c in range(per) for s in range(groups)], axis=0
        )

    whole_rows = groups * rows
    i = lax.broadcasted_iota(jnp.int32, (per * whole_rows, per * whole_rows), 0) // whole_rows
    j = lax.broadcasted_iota(jnp.int32, (per * whole_rows, per * whole_rows), 1) // whole_rows
    bias = jnp.where(i == j, 0.0, -jnp.inf).astype(jnp.float32)
    for step in range(strip // per):
        def pick(which):
            return jnp.concatenate(
                [x_ref[s, which, step * per + c] for c in range(per) for s in range(groups)],
                axis=0,
            )

        grads = block_grads(pick(0), pick(3), pick(1), pick(2), bias)
        for which, full in enumerate(grads):
            low = full.astype(jnp.bfloat16)
            for c in range(per):
                for s in range(groups):
                    start = c * whole_rows + s * rows
                    o_ref[s, which, step * per + c] = low[start:start + rows]


def column_attention(whole, order):
    groups, arrays, strip, rows, width = whole.shape
    vmem = pl.BlockSpec(memory_space=pltpu.VMEM)
    return pl.pallas_call(
        column_kernel,
        in_specs=[vmem, vmem],
        out_specs=vmem,
        out_shape=jax.ShapeDtypeStruct((groups, 3, strip, rows, width), jnp.bfloat16),
    )(whole, order)


def band_bias(mask_rows, offsets, first_col, grid_cols, block_cols):
    band_reach = HALF + OFFMAX
    query_cols = first_col + jnp.arange(block_cols, dtype=jnp.int32)
    key_cols = first_col - band_reach + jnp.arange(block_cols + 2 * band_reach, dtype=jnp.int32)
    inside = (key_cols >= 0) & (key_cols < grid_cols)
    key_block = jnp.clip(key_cols, 0, grid_cols - 1) // BLK
    block_ids = jnp.arange(mask_rows.shape[1], dtype=jnp.int32)
    key_open = jnp.sum(
        mask_rows[:, None, :]
        * (key_block[None, :, None] == block_ids[None, None, :]).astype(jnp.int32),
        axis=-1,
    )
    relative = key_cols[None, None, :] - query_cols[None, :, None] - offsets[:, None, None]
    same_block = key_cols[None, :] // BLK == query_cols[:, None] // BLK
    allowed = (
        (relative >= -HALF)
        & (relative < HALF)
        & inside[None, None, :]
        & ((key_open[:, None, :] > 0) | same_block[None])
    )
    return jnp.where(allowed, 0.0, -jnp.inf).astype(jnp.float32)


def body(queries, key_grid, value_grid, out_grad, tissue_mask, band_offset):
    row_count, col_count, feature_width = queries.shape
    group_count = lax.axis_size("rrow")
    band_reach = HALF + OFFMAX
    near = col_count
    far = band_reach - col_count

    strip = col_count // group_count
    stacked = (
        jnp.stack([queries, key_grid, value_grid, out_grad])
        .reshape(4, row_count, group_count, strip, feature_width)
        .transpose(2, 0, 3, 1, 4)
    )
    whole = lax.all_to_all(stacked, "rrow", split_axis=0, concat_axis=0, tiled=True)

    pair = jnp.stack([key_grid, value_grid])
    l1 = shifted(pair[:, :, col_count - near:], "rcol", 1)
    r1 = shifted(pair[:, :, :near], "rcol", -1)
    grid_cols = col_count * lax.axis_size("rcol")
    first_col = lax.axis_index("rcol") * col_count
    bias = band_bias(tissue_mask, band_offset, first_col, grid_cols, col_count)

    col_out = column_attention(whole, bias[:, :8, :])
    back = lax.all_to_all(col_out, "rrow", split_axis=0, concat_axis=0, tiled=True)
    row_grads = fused_row(queries, out_grad, key_grid, value_grid, l1, r1, bias, far)
    back = back.transpose(1, 3, 0, 2, 4).reshape(3, row_count, col_count, feature_width)
    back = back.astype(jnp.float32)
    return tuple((row + col).astype(jnp.bfloat16) for row, col in zip(row_grads, back))


def solution(mesh):
    in_specs = (
        P(("slide", "rrow"), "rcol", None),
        P(("slide", "rrow"), "rcol", None),
        P(("slide", "rrow"), "rcol", None),
        P(("slide", "rrow"), "rcol", None),
        P(("slide", "rrow"), None),
        P(("slide", "rrow")),
    )
    out_specs = (
        P(("slide", "rrow"), "rcol", None),
        P(("slide", "rrow"), "rcol", None),
        P(("slide", "rrow"), "rcol", None),
    )
    return jax.shard_map(body, mesh=mesh, in_specs=in_specs, out_specs=out_specs, check_vma=False)
```
